32 devices in a mesh: dp: 4 (over x, core), fsdp: 8 (over z, y).
Axes of the slice: x: 2, y: 2, z: 4, core: 2. Of those that a mesh axis runs over, the one named last changes fastest.
Arguments:
- tokens: bfloat16 [32, 256, 768], P(('dp', 'fsdp')), may hold values from -6 to 6
- lengths: int32 [32], P(('dp', 'fsdp')), may hold values from 129 to 256
- query_weight: bfloat16 [2, 768, 768], P(None, ('dp', 'fsdp')), may hold values from -0.21875 to 0.21875
- key_weight: bfloat16 [2, 768, 768], P(None, ('dp', 'fsdp')), may hold values from -0.21875 to 0.21875
- value_weight: bfloat16 [2, 768, 768], P(None, ('dp', 'fsdp')), may hold values from -0.21875 to 0.21875
- attn_out_weight: bfloat16 [2, 768, 768], P(None, ('dp', 'fsdp')), may hold values from -1.75 to 1.75
- up_weight: bfloat16 [2, 768, 3072], P(None, ('dp', 'fsdp')), may hold values from -0.21875 to 0.21875
- down_weight: bfloat16 [2, 3072, 768], P(None, None, ('dp', 'fsdp')), may hold values from -0.109375 to 0.109375
- norm_gains: bfloat16 [2, 2, 768], P(None, None, ('dp', 'fsdp')), may hold values from 0.5 to 1.5
- cotangent: bfloat16 [32, 256, 768], P(('dp', 'fsdp')), may hold values from -6 to 6
Outputs:
- activations: bfloat16 [32, 256, 768], P(('dp', 'fsdp'))
- input_grad: float32 [32, 256, 768], P(('dp', 'fsdp'))
- grad_query: float32 [2, 768, 768], P(None, ('dp', 'fsdp'))
- grad_key: float32 [2, 768, 768], P(None, ('dp', 'fsdp'))
- grad_value: float32 [2, 768, 768], P(None, ('dp', 'fsdp'))
- grad_attn_out: float32 [2, 768, 768], P(None, ('dp', 'fsdp'))
- grad_up: float32 [2, 768, 3072], P(None, ('dp', 'fsdp'))
- grad_down: float32 [2, 3072, 768], P(None, None, ('dp', 'fsdp'))
- grad_gains: float32 [2, 2, 768], P(None, None, ('dp', 'fsdp'))
The draws below stay inside these ranges and needn't reach their ends.
All inputs are finite; a program needn't handle non-finite values.
Results may differ from the reference program's by a relative error of at most 0.025.
Values may be sent and summed in bfloat16 or wider, within the bound.
No kernel may reach another device: no remote copies, remote signals or barrier semaphores. Data moves between devices by JAX's collectives and lax.ppermute only.
A program may use at most 256 MiB of HBM per device.

```python
import math
import jax
import jax.numpy as jnp
from jax import lax

D = 768
HEADS = 12
HEAD_DIM = 64
FF = 3072
SEQ = 256
LAYERS = 2
BLK = 128
SEQS = 32


def draw_lengths(key, part):
    first, second = jax.random.split(jax.random.fold_in(key, 11))
    values = jax.random.randint(first, (SEQS,), BLK + 1, SEQ + 1, dtype=jnp.int32)
    order = jax.random.permutation(second, SEQS)
    values = values.at[order[0]].set(SEQ)
    values = values.at[order[1]].set(BLK + 1)
    return values


def with_spikes(entries, key, source, target, parts, factor):
    def block_of(axis_at):
        return (jnp.arange(entries.shape[axis_at]) // (entries.shape[axis_at] // parts)).reshape((-1,) + (1,) * (entries.ndim - 1 - axis_at))

    near = jax.random.permutation(key, parts)[block_of(target)]
    far = (block_of(target) + parts // 2) % parts
    return jnp.where((block_of(source) == near) | (block_of(source) == far), factor * entries, entries)


def block_levels(own_key, shape, pieces, low, high):
    def one(dim, shards_of):
        heights = jax.random.uniform(jax.random.fold_in(jax.random.fold_in(own_key, 6), dim), (shards_of,), jnp.float32, low / len(pieces), high / len(pieces))
        return jnp.repeat(jnp.exp(heights), shape[dim] // shards_of).reshape((-1,) + (1,) * (len(shape) - dim - 1))

    loudness = one(*pieces[0])
    for cut in pieces[1:]:
        loudness = loudness * one(*cut)
    return loudness


def bell_draw(stream_key, extent, scale, most, cuts=(), held_as=jnp.bfloat16):
    entries = scale * jax.random.normal(stream_key, extent, jnp.float32)
    if cuts:
        entries = entries * block_levels(stream_key, extent, cuts, -0.22, 0.18)
    return jnp.clip(entries, -most, most).astype(held_as)


def heavy_noise(own_key, shape, scale, limit, cuts, heavy, kind=jnp.bfloat16):
    values = scale * jax.random.normal(own_key, shape, jnp.float32)
    if cuts:
        values = values * block_levels(own_key, shape, cuts, -0.22, 0.18)
    return jnp.clip(with_spikes(values, jax.random.fold_in(own_key, 3), *heavy), -limit, limit).astype(kind)


def setup_inputs(seed: int = 0) -> dict:
    arg_keys = jax.random.split(jax.random.key(seed), 11)
    tokens = bell_draw(arg_keys[0], (SEQS, SEQ, D), 1.0, 6.0, ((0, 32),))
    lengths = draw_lengths(jax.random.fold_in(arg_keys[10], 71), 0)
    query_weight = bell_draw(arg_keys[2], (LAYERS, D, D), D ** -0.5, 0.21875, ((1, 32),))
    key_weight = bell_draw(arg_keys[3], (LAYERS, D, D), D ** -0.5, 0.21875, ((1, 32),))
    value_weight = bell_draw(arg_keys[4], (LAYERS, D, D), D ** -0.5, 0.21875, ((1, 32),))
    attn_out_weight = bell_draw(arg_keys[5], (LAYERS, D, D), (D // 64) ** -0.5, 1.75, ((1, 32),))
    up_weight = bell_draw(arg_keys[6], (LAYERS, D, FF), D ** -0.5, 0.21875, ((1, 32),))
    down_weight = bell_draw(arg_keys[7], (LAYERS, FF, D), FF ** -0.5, 0.109375, ((2, 32),))
    norm_gains = jnp.clip(1.0 + 0.1 * jax.random.normal(arg_keys[8], (LAYERS, 2, D), jnp.float32), 0.5, 1.5).astype(jnp.bfloat16)
    cotangent = heavy_noise(arg_keys[9], (SEQS, SEQ, D), 1.0, 6.0, ((0, 32),), (0, 2, 32, 2.75))
    return dict(tokens=tokens, lengths=lengths, query_weight=query_weight, key_weight=key_weight, value_weight=value_weight, attn_out_weight=attn_out_weight, up_weight=up_weight, down_weight=down_weight, norm_gains=norm_gains, cotangent=cotangent)


@jax.custom_vjp
def low(v):
    return lax.optimization_barrier(v.astype(jnp.bfloat16)).astype(jnp.float32)

@jax.custom_vjp
def low_back(v):
    return v

def low_keep(v):
    return (low(v), None)

def low_pass(kept, grad):
    return (grad,)

def back_keep(v):
    return (v, None)

def back_low(kept, grad):
    return (low(grad),)
low.defvjp(low_keep, low_pass)
low_back.defvjp(back_keep, back_low)

def low_both(value):
    return low_back(low(value))

def product(left, right):
    return jnp.einsum('gsd,df->gsf', left, right, precision=lax.Precision.HIGHEST)

def norm(value, gain):
    centred = value - lax.optimization_barrier(jnp.mean(value, axis=-1, keepdims=True))
    spread = lax.optimization_barrier(jnp.mean(centred * centred, axis=-1, keepdims=True))
    return centred * lax.rsqrt(spread + 1e-05) * gain

def layer(hidden_in, lengths_group, weights, swap):
    query_w, key_w, value_w, out_w, up_w, down_w, gains = weights
    count = hidden_in.shape[0]
    inputs_low = low(hidden_in)
    query = low_both(product(inputs_low, query_w)).reshape(count, 2, BLK, HEADS, HEAD_DIM)
    keys = low_both(product(inputs_low, key_w)).reshape(count, 2, BLK, HEADS, HEAD_DIM)
    values = low_both(product(inputs_low, value_w)).reshape(count, 2, BLK, HEADS, HEAD_DIM)
    positions = jnp.arange(SEQ, dtype=jnp.int32).reshape(2, BLK)
    if swap:
        keys = keys[:, ::-1]
        values = values[:, ::-1]
        positions = positions[::-1]
    visible = positions[None] < lengths_group[:, None, None]
    scores = jnp.einsum('gbqhd,gbkhd->gbhqk', query, keys, precision=lax.Precision.HIGHEST) * 0.125
    scores = low_back(scores)
    scores = jnp.where(visible[:, :, None, None, :], scores, -1e+30)
    shares = low(jax.nn.softmax(scores, axis=-1))
    mixed = jnp.einsum('gbhqk,gbkhd->gbqhd', shares, values, precision=lax.Precision.HIGHEST)
    mixed = low_both(mixed.reshape(count, SEQ, D))
    attended = low_back(product(mixed, out_w))
    normed = norm(hidden_in + attended, gains[0])
    expanded = low_back(product(low(normed), up_w))
    activated = low(jax.nn.gelu(expanded, approximate=True))
    shrunk = low_back(product(activated, down_w))
    return norm(normed + shrunk, gains[1])

def forward(hidden, params, lengths_group):
    for index in range(LAYERS):
        hidden = layer(hidden, lengths_group, tuple((w[index] for w in params)), index % 2 == 1)
    return hidden

def reference(tokens, lengths, query_weight, key_weight, value_weight, attn_out_weight, up_weight, down_weight, norm_gains, cotangent):
    params = tuple((w.astype(jnp.float32) for w in (query_weight, key_weight, value_weight, attn_out_weight, up_weight, down_weight, norm_gains)))
    group = math.gcd(SEQS, max(1, 4096 // SEQ))
    groups = SEQS // group
    inputs = tokens.astype(jnp.float32).reshape(groups, group, SEQ, D)
    lengths_all = lengths.reshape(groups, group)
    seeds = cotangent.astype(jnp.float32).reshape(groups, group, SEQ, D)

    def advance(total, item):
        hidden, lengths_group, seed_grad = item
        result, pull = jax.vjp(lambda h, p: forward(h, p, lengths_group), hidden, params)
        grad_hidden, grad_params = pull(seed_grad)
        return (jax.tree.map(lambda a, b: a + b, total, grad_params), (result, grad_hidden))
    start = jax.tree.map(jnp.zeros_like, params)
    total, (results, grad_inputs) = lax.scan(advance, start, (inputs, lengths_all, seeds))
    return (results.reshape(SEQS, SEQ, D).astype(jnp.bfloat16), grad_inputs.reshape(SEQS, SEQ, D), total[0], total[1], total[2], total[3], total[4], total[5], total[6])
```

```python
import jax
import jax.numpy as jnp
from jax import lax
from jax.sharding import PartitionSpec as P

D = 768
HEADS = 12
HEAD_DIM = 64
FF = 3072
LAYERS = 2
PAD = 128


def norm(value, gain):
    centred = value - jnp.mean(value, axis=-1, keepdims=True)
    spread = jnp.mean(centred * centred, axis=-1, keepdims=True)
    return centred * lax.rsqrt(spread + 1e-05) * gain


def gelu_tanh(value):
    return jax.nn.gelu(value, approximate=True)


def product(left, right):
    return jnp.dot(left, right, preferred_element_type=jnp.float32)


def product_left_t(left, right):
    return lax.dot_general(
        left, right, (((0,), (0,)), ((), ())), preferred_element_type=jnp.float32
    )


def product_right_t(left, right):
    return lax.dot_general(
        left, right, (((1,), (1,)), ((), ())), preferred_element_type=jnp.float32
    )


def pack(shards, layer):
    query_w, key_w, value_w, out_w, up_w, down_w, gains = (member[layer] for member in shards)
    rows = query_w.shape[0]
    gain_columns = jnp.pad(gains.T, ((0, 0), (0, PAD - 2)))
    return jnp.concatenate([query_w, key_w, value_w, out_w, up_w, down_w.T, gain_columns], axis=1)


def collect(shards, layer):
    return lax.all_gather(pack(shards, layer), ("dp", "fsdp"), axis=0, tiled=True)


def unpack(gathered):
    qkv_w = gathered[:, : 3 * D]
    out_w = gathered[:, 3 * D : 4 * D]
    up_w = gathered[:, 4 * D : 4 * D + FF]
    down_t = gathered[:, 4 * D + FF : 4 * D + 2 * FF]
    gains = gathered[:, 4 * D + 2 * FF : 4 * D + 2 * FF + 2].T.astype(jnp.float32)
    return (qkv_w, out_w, up_w, down_t, gains)


def visible_keys(length, token_count, swap):
    half = token_count // 2
    positions = lax.broadcasted_iota(jnp.int32, (2, half), 0) * half + lax.broadcasted_iota(
        jnp.int32, (2, half), 1
    )
    if swap:
        positions = positions[::-1]
    return positions < length


def split_heads(value):
    return value.reshape(2, value.shape[0] // 2, HEADS, HEAD_DIM)


def paired_heads(query, keys, values, swap):
    query_heads = split_heads(query)
    key_heads = split_heads(keys)
    value_heads = split_heads(values)
    if swap:
        key_heads = key_heads[::-1]
        value_heads = value_heads[::-1]
    return (query_heads, key_heads, value_heads)


def masked_scores(query_heads, key_heads, visible):
    scores = (
        jnp.einsum("bqhd,bkhd->bhqk", query_heads, key_heads, preferred_element_type=jnp.float32)
        * 0.125
    )
    return jnp.where(visible[:, None, None, :], scores, -1e30)


def attend_forward(query, keys, values, visible, swap):
    token_count = query.shape[0]
    query_heads, key_heads, value_heads = paired_heads(query, keys, values, swap)
    scores = masked_scores(query_heads, key_heads, visible)
    highest = jnp.max(scores, axis=-1, keepdims=True)
    raised = jnp.exp(scores - highest)
    total = jnp.sum(raised, axis=-1, keepdims=True)
    shares = (raised / total).astype(jnp.bfloat16)
    mixed = jnp.einsum("bhqk,bkhd->bqhd", shares, value_heads, preferred_element_type=jnp.float32)
    return (mixed.reshape(token_count, -1), highest + jnp.log(total))


def attend_backward(query, keys, values, visible, swap, log_total, grad_mixed):
    token_count = query.shape[0]
    query_heads, key_heads, value_heads = paired_heads(query, keys, values, swap)
    scores = masked_scores(query_heads, key_heads, visible)
    shares = jnp.exp(scores - log_total)
    shares_low = shares.astype(jnp.bfloat16)
    grad_heads = split_heads(grad_mixed)
    grad_values = jnp.einsum(
        "bhqk,bqhd->bkhd", shares_low, grad_heads, preferred_element_type=jnp.float32
    )
    grad_shares = jnp.einsum(
        "bqhd,bkhd->bhqk", grad_heads, value_heads, preferred_element_type=jnp.float32
    )
    inner = jnp.sum(shares * grad_shares, axis=-1, keepdims=True)
    grad_scores = (shares * (grad_shares - inner)).astype(jnp.bfloat16)
    grad_query = (
        jnp.einsum("bhqk,bkhd->bqhd", grad_scores, key_heads, preferred_element_type=jnp.float32)
        * 0.125
    )
    grad_keys = (
        jnp.einsum("bhqk,bqhd->bkhd", grad_scores, query_heads, preferred_element_type=jnp.float32)
        * 0.125
    )
    if swap:
        grad_keys = grad_keys[::-1]
        grad_values = grad_values[::-1]
    return tuple(
        (
            member.reshape(token_count, -1).astype(jnp.bfloat16)
            for member in (grad_query, grad_keys, grad_values)
        )
    )


def layer_forward(hidden, length, weights, swap):
    qkv_w, out_w, up_w, down_t, gains = weights
    inputs_low = hidden.astype(jnp.bfloat16)
    qkv = product(inputs_low, qkv_w).astype(jnp.bfloat16)
    query, keys, values = qkv[:, :D], qkv[:, D : 2 * D], qkv[:, 2 * D :]
    visible = visible_keys(length, hidden.shape[0], swap)
    mixed, log_total = attend_forward(query, keys, values, visible, swap)
    mixed_low = mixed.astype(jnp.bfloat16)
    first_sum = hidden + product(mixed_low, out_w)
    normed = norm(first_sum, gains[0])
    normed_low = normed.astype(jnp.bfloat16)
    expanded = product(normed_low, up_w)
    activated = gelu_tanh(expanded).astype(jnp.bfloat16)
    second_sum = normed + product_right_t(activated, down_t)
    output = norm(second_sum, gains[1])
    kept = (
        inputs_low,
        query,
        keys,
        values,
        log_total,
        mixed_low,
        first_sum,
        normed_low,
        expanded,
        activated,
        second_sum,
    )
    return (output, kept)


def layer_backward(grad_output, kept, weights, swap, length):
    qkv_w, out_w, up_w, down_t, gains = weights
    (
        inputs_low,
        query,
        keys,
        values,
        log_total,
        mixed_low,
        first_sum,
        normed_low,
        expanded,
        activated,
        second_sum,
    ) = kept
    grad_second, grad_gain_second = jax.vjp(norm, second_sum, gains[1])[1](grad_output)
    down_low = grad_second.astype(jnp.bfloat16)
    grad_active = product(down_low, down_t)
    up_low = jax.vjp(gelu_tanh, expanded)[1](grad_active)[0].astype(jnp.bfloat16)
    grad_normed = grad_second + product_right_t(up_low, up_w)
    grad_first, grad_gain_first = jax.vjp(norm, first_sum, gains[0])[1](grad_normed)
    attn_low = grad_first.astype(jnp.bfloat16)
    grad_mixed = product_right_t(attn_low, out_w).astype(jnp.bfloat16)
    visible = visible_keys(length, query.shape[0], swap)
    grad_qkv = jnp.concatenate(
        attend_backward(query, keys, values, visible, swap, log_total, grad_mixed), axis=1
    )
    grad_inputs = grad_first + product_right_t(grad_qkv, qkv_w)
    gain_columns = jnp.pad(
        jnp.stack([grad_gain_first, grad_gain_second], axis=1), ((0, 0), (0, PAD - 2))
    )
    low = jnp.bfloat16
    terms = jnp.concatenate(
        [
            product_left_t(inputs_low, grad_qkv).astype(low),
            product_left_t(mixed_low, attn_low).astype(low),
            product_left_t(normed_low, up_low).astype(low),
            product_left_t(down_low, activated).astype(low),
            gain_columns.astype(low),
        ],
        axis=1,
    )
    return (grad_inputs, terms)


def arrange(summed):
    summed = summed.astype(jnp.float32)
    bounds = [0, D, 2 * D, 3 * D, 4 * D, 4 * D + FF, 4 * D + 2 * FF, 4 * D + 2 * FF + 2]
    member = [summed[:, bounds[j] : bounds[j + 1]] for j in range(7)]
    return (*member[:5], member[5].T, member[6].T)


def per_device(
    tokens,
    lengths,
    query_weight,
    key_weight,
    value_weight,
    attn_out_weight,
    up_weight,
    down_weight,
    norm_gains,
    cotangent,
):
    shards = (
        query_weight,
        key_weight,
        value_weight,
        attn_out_weight,
        up_weight,
        down_weight,
        norm_gains,
    )
    hidden = tokens[0].astype(jnp.float32)
    length = lengths[0]
    weights_all = [unpack(collect(shards, layer)) for layer in range(LAYERS)]
    kept_all = []
    for layer in range(LAYERS):
        hidden, kept = layer_forward(hidden, length, weights_all[layer], layer % 2 == 1)
        kept_all.append(kept)
    activations = hidden.astype(jnp.bfloat16)[None]
    grad_hidden = cotangent[0].astype(jnp.float32)
    layer_grads = [None] * LAYERS
    for layer in reversed(range(LAYERS)):
        grad_hidden, terms = layer_backward(
            grad_hidden, kept_all[layer], weights_all[layer], layer % 2 == 1, length
        )
        summed = lax.psum_scatter(terms, ("dp", "fsdp"), scatter_dimension=0, tiled=True)
        layer_grads[layer] = arrange(summed)
    stacked = tuple((jnp.stack([entry[member] for entry in layer_grads]) for member in range(7)))
    return (activations, grad_hidden[None], *stacked)


def solution(mesh):
    placed = (
        P(("dp", "fsdp"), None, None),
        P(("dp", "fsdp")),
        P(None, ("dp", "fsdp"), None),
        P(None, ("dp", "fsdp"), None),
        P(None, ("dp", "fsdp"), None),
        P(None, ("dp", "fsdp"), None),
        P(None, ("dp", "fsdp"), None),
        P(None, None, ("dp", "fsdp")),
        P(None, None, ("dp", "fsdp")),
        P(("dp", "fsdp"), None, None),
    )
    return jax.shard_map(
        per_device,
        mesh=mesh,
        in_specs=placed,
        out_specs=(
            P(("dp", "fsdp"), None, None),
            P(("dp", "fsdp"), None, None),
            P(None, ("dp", "fsdp"), None),
            P(None, ("dp", "fsdp"), None),
            P(None, ("dp", "fsdp"), None),
            P(None, ("dp", "fsdp"), None),
            P(None, ("dp", "fsdp"), None),
            P(None, None, ("dp", "fsdp")),
            P(None, None, ("dp", "fsdp")),
        ),
        check_vma=False,
    )
```

```python
import functools

import jax
import jax.numpy as jnp
from jax import lax
from jax.experimental import pallas as pl
from jax.experimental.pallas import tpu as pltpu
import numpy as np
from jax.sharding import PartitionSpec as P

D = 768
HEADS = 12
HEAD_DIM = 64
FF = 3072
LAYERS = 2
PAD = 128


def norm(value, gain):
    centred = value - jnp.mean(value, axis=-1, keepdims=True)
    spread = jnp.mean(centred * centred, axis=-1, keepdims=True)
    return centred * lax.rsqrt(spread + 1e-05) * gain


def gelu_tanh(value):
    return jax.nn.gelu(value, approximate=True)


def product(left, right):
    return jnp.dot(left, right, preferred_element_type=jnp.float32)


def product_left_t(left, right):
    return lax.dot_general(
        left, right, (((0,), (0,)), ((), ())), preferred_element_type=jnp.float32
    )


def product_right_t(left, right):
    return lax.dot_general(
        left, right, (((1,), (1,)), ((), ())), preferred_element_type=jnp.float32
    )


def pack(shards, layer):
    query_w, key_w, value_w, out_w, up_w, down_w, gains = (member[layer] for member in shards)
    rows = query_w.shape[0]
    gain_columns = jnp.pad(gains.T, ((0, 0), (0, PAD - 2)))
    return jnp.concatenate([query_w, key_w, value_w, out_w, up_w, down_w.T, gain_columns], axis=1)


def collect(shards, layer):
    return lax.all_gather(pack(shards, layer), ("dp", "fsdp"), axis=0, tiled=True)


def unpack(gathered):
    qkv_w = gathered[:, : 3 * D]
    out_w = gathered[:, 3 * D : 4 * D]
    up_w = gathered[:, 4 * D : 4 * D + FF]
    down_t = gathered[:, 4 * D + FF : 4 * D + 2 * FF]
    gains = gathered[:, 4 * D + 2 * FF : 4 * D + 2 * FF + 2].T.astype(jnp.float32)
    return (qkv_w, out_w, up_w, down_t, gains)


def visible_keys(length, token_count, swap):
    half = token_count // 2
    positions = lax.broadcasted_iota(jnp.int32, (2, half), 0) * half + lax.broadcasted_iota(
        jnp.int32, (2, half), 1
    )
    if swap:
        positions = positions[::-1]
    return positions < length


def split_heads(value):
    return value.reshape(2, value.shape[0] // 2, HEADS, HEAD_DIM)


def paired_heads(query, keys, values, swap):
    query_heads = split_heads(query)
    key_heads = split_heads(keys)
    value_heads = split_heads(values)
    if swap:
        key_heads = key_heads[::-1]
        value_heads = value_heads[::-1]
    return (query_heads, key_heads, value_heads)


def masked_scores(query_heads, key_heads, visible):
    scores = (
        jnp.einsum("bqhd,bkhd->bhqk", query_heads, key_heads, preferred_element_type=jnp.float32)
        * 0.125
    )
    return jnp.where(visible[:, None, None, :], scores, -1e30)


def attend_forward(query, keys, values, visible, swap):
    token_count = query.shape[0]
    query_heads, key_heads, value_heads = paired_heads(query, keys, values, swap)
    scores = masked_scores(query_heads, key_heads, visible)
    highest = jnp.max(scores, axis=-1, keepdims=True)
    raised = jnp.exp(scores - highest)
    total = jnp.sum(raised, axis=-1, keepdims=True)
    shares = (raised / total).astype(jnp.bfloat16)
    mixed = jnp.einsum("bhqk,bkhd->bqhd", shares, value_heads, preferred_element_type=jnp.float32)
    return (mixed.reshape(token_count, -1), highest + jnp.log(total))


def attend_backward(query, keys, values, visible, swap, log_total, grad_mixed):
    token_count = query.shape[0]
    query_heads, key_heads, value_heads = paired_heads(query, keys, values, swap)
    scores = masked_scores(query_heads, key_heads, visible)
    shares = jnp.exp(scores - log_total)
    shares_low = shares.astype(jnp.bfloat16)
    grad_heads = split_heads(grad_mixed)
    grad_values = jnp.einsum(
        "bhqk,bqhd->bkhd", shares_low, grad_heads, preferred_element_type=jnp.float32
    )
    grad_shares = jnp.einsum(
        "bqhd,bkhd->bhqk", grad_heads, value_heads, preferred_element_type=jnp.float32
    )
    inner = jnp.sum(shares * grad_shares, axis=-1, keepdims=True)
    grad_scores = (shares * (grad_shares - inner)).astype(jnp.bfloat16)
    grad_query = (
        jnp.einsum("bhqk,bkhd->bqhd", grad_scores, key_heads, preferred_element_type=jnp.float32)
        * 0.125
    )
    grad_keys = (
        jnp.einsum("bhqk,bqhd->bkhd", grad_scores, query_heads, preferred_element_type=jnp.float32)
        * 0.125
    )
    if swap:
        grad_keys = grad_keys[::-1]
        grad_values = grad_values[::-1]
    return tuple(
        (
            member.reshape(token_count, -1).astype(jnp.bfloat16)
            for member in (grad_query, grad_keys, grad_values)
        )
    )


def layer_forward(hidden, length, weights, swap):
    qkv_w, out_w, up_w, down_t, gains = weights
    inputs_low = hidden.astype(jnp.bfloat16)
    qkv = product(inputs_low, qkv_w).astype(jnp.bfloat16)
    query, keys, values = qkv[:, :D], qkv[:, D : 2 * D], qkv[:, 2 * D :]
    visible = visible_keys(length, hidden.shape[0], swap)
    mixed, log_total = attend_forward(query, keys, values, visible, swap)
    mixed_low = mixed.astype(jnp.bfloat16)
    first_sum = hidden + product(mixed_low, out_w)
    normed = norm(first_sum, gains[0])
    normed_low = normed.astype(jnp.bfloat16)
    expanded = product(normed_low, up_w)
    activated = gelu_tanh(expanded).astype(jnp.bfloat16)
    second_sum = normed + product_right_t(activated, down_t)
    output = norm(second_sum, gains[1])
    kept = (
        inputs_low,
        query,
        keys,
        values,
        log_total,
        mixed_low,
        first_sum,
        normed_low,
        expanded,
        activated,
        second_sum,
    )
    return (output, kept)


def layer_backward(grad_output, kept, weights, swap, length):
    qkv_w, out_w, up_w, down_t, gains = weights
    (
        inputs_low,
        query,
        keys,
        values,
        log_total,
        mixed_low,
        first_sum,
        normed_low,
        expanded,
        activated,
        second_sum,
    ) = kept
    grad_second, grad_gain_second = jax.vjp(norm, second_sum, gains[1])[1](grad_output)
    down_low = grad_second.astype(jnp.bfloat16)
    grad_active = product(down_low, down_t)
    up_low = jax.vjp(gelu_tanh, expanded)[1](grad_active)[0].astype(jnp.bfloat16)
    grad_normed = grad_second + product_right_t(up_low, up_w)
    grad_first, grad_gain_first = jax.vjp(norm, first_sum, gains[0])[1](grad_normed)
    attn_low = grad_first.astype(jnp.bfloat16)
    grad_mixed = product_right_t(attn_low, out_w).astype(jnp.bfloat16)
    visible = visible_keys(length, query.shape[0], swap)
    grad_qkv = jnp.concatenate(
        attend_backward(query, keys, values, visible, swap, log_total, grad_mixed), axis=1
    )
    grad_inputs = grad_first + product_right_t(grad_qkv, qkv_w)
    operands = (
        inputs_low,
        grad_qkv,
        mixed_low,
        attn_low,
        normed_low,
        up_low,
        down_low,
        activated,
        jnp.stack([grad_gain_first, grad_gain_second]),
    )
    return (grad_inputs, operands)


def plain_terms(operands):
    (inputs_low, grad_qkv, mixed_low, attn_low, normed_low, up_low, down_low, activated, gains) = (
        operands
    )
    low = jnp.bfloat16
    return jnp.concatenate(
        [
            product_left_t(inputs_low, grad_qkv).astype(low),
            product_left_t(mixed_low, attn_low).astype(low),
            product_left_t(normed_low, up_low).astype(low),
            product_left_t(down_low, activated).astype(low),
            jnp.pad(gains.T, ((0, 0), (0, PAD - 2))).astype(low),
        ],
        axis=1,
    )


def plain_reduce(operands):
    summed = lax.psum_scatter(
        plain_terms(operands), ("dp", "fsdp"), scatter_dimension=0, tiled=True
    ).astype(jnp.float32)
    bounds = [0, D, 2 * D, 3 * D, 4 * D, 4 * D + FF, 4 * D + 2 * FF, 4 * D + 2 * FF + 2]
    member = [summed[:, bounds[j] : bounds[j + 1]] for j in range(7)]
    return (*member[:5], member[5].T, member[6].T)


class Grid:
    def __init__(self):
        places = [
            (x, core, z, y) for x in range(2) for core in range(2) for z in range(4) for y in range(2)
        ]
        number = {place: index for index, place in enumerate(places)}

        def route(move, senders=range(4)):
            return [
                (number[place], number[move(*place)]) for place in places if place[2] in senders
            ]

        self.core = route(lambda x, core, z, y: (x, 1 - core, z, y))
        self.along_x = route(lambda x, core, z, y: (1 - x, core, z, y))
        self.along_y = route(lambda x, core, z, y: (x, core, z, 1 - y))
        self.pair = route(lambda x, core, z, y: (x, core, z ^ 1, y))
        self.middle = route(lambda x, core, z, y: (x, core, 3 - z, y), (1, 2))
        self.outward = route(lambda x, core, z, y: (x, core, z ^ 1, y), (1, 2))
        self.inward = route(lambda x, core, z, y: (x, core, z ^ 1, y), (0, 3))


def swap(value, route):
    return lax.ppermute(value, ("dp", "fsdp"), route)


SLOTS = np.array([(dx, dy, s) for dx, dy in ((1, 1), (1, 0), (0, 1), (0, 0)) for s in range(4)])


def row_orders(unit):
    dp, fsdp = lax.axis_index("dp"), lax.axis_index("fsdp")
    x, core, z, y = dp // 2, dp % 2, fsdp // 2, fsdp % 2
    dx, dy, s = (jnp.asarray(np.repeat(SLOTS[:, j], unit), jnp.int32) for j in range(3))
    offset = jnp.asarray(np.tile(np.arange(unit), 16), jnp.int32)
    place = jnp.where(s < 2, z ^ s, jnp.where(z < 2, s, 3 - s))
    natural = lax.broadcasted_iota(jnp.int32, (32 * unit, 16 * unit), 0)

    def order(owner):
        row = ((((x ^ dx) * 2 + owner) * 4 + place) * 2 + (y ^ dy)) * unit + offset
        return (natural == row[None]).astype(jnp.bfloat16)

    return order(core), order(1 - core)


def share_left(value, orders, grid):
    mine, other = (
        lax.dot_general(
            order, value, (((0,), (1,)), ((), ())), preferred_element_type=jnp.float32
        ).astype(jnp.bfloat16)
        for order in orders
    )
    return (mine, swap(other, grid.core))


def both(value, grid):
    return (value, swap(value, grid.core))


ROWS = ((0, 2), (2, 4), (4, 8), (8, 12), (12, 16))


def dot(left, right):
    return jnp.dot(left, right, preferred_element_type=jnp.float32)


def ffn_terms(normed_t, up_low, down_t, activated, unit):
    tile = D
    steps = FF // tile

    def body(na, nb, ua, ub, da, db, aa, ab, *outs):
        def put(value):
            value = value.astype(jnp.bfloat16)
            for (low, high), out in zip(ROWS, outs):
                out[...] = value[low * unit : high * unit]

        step = pl.program_id(0)

        @pl.when(step < steps)
        def _():
            put(dot(na[...], ua[...]) + dot(nb[...], ub[...]))

        @pl.when(step >= steps)
        def _():
            put(dot(da[...], aa[...]) + dot(db[...], ab[...]))

    def whole(value):
        return pl.BlockSpec(value.shape, lambda j: (0, 0))

    first = pl.BlockSpec((up_low[0].shape[0], tile), lambda j: (0, jnp.minimum(j, steps - 1)))
    second = pl.BlockSpec((up_low[0].shape[0], tile), lambda j: (0, jnp.maximum(j - steps, 0)))
    return pl.pallas_call(
        body,
        grid=(2 * steps,),
        in_specs=[whole(v) for v in normed_t]
        + [first, first]
        + [whole(v) for v in down_t]
        + [second, second],
        out_specs=[pl.BlockSpec(((b - a) * unit, tile), lambda j: (0, j)) for a, b in ROWS],
        out_shape=[
            jax.ShapeDtypeStruct(((b - a) * unit, 2 * FF), jnp.bfloat16) for a, b in ROWS
        ],
        cost_estimate=pl.CostEstimate(
            flops=2 * 512 * 16 * unit * 2 * FF, bytes_accessed=12 << 20, transcendentals=0
        ),
        compiler_params=pltpu.CompilerParams(vmem_limit_bytes=32 << 20),
    )(*normed_t, *up_low, *down_t, *activated)


def attention_terms(inputs_t, grad_qkv, mixed_t, attn_low, unit):
    tokens = attn_low[0].shape[0]

    def body(ia, ib, qa, qb, ma, mb, oa, ob, *outs):
        def put(value, column):
            value = value.astype(jnp.bfloat16)
            for (low, high), out in zip(ROWS, outs):
                out[:, column : column + value.shape[1]] = value[low * unit : high * unit]

        for j in range(3):
            part = slice(j * D, (j + 1) * D)
            put(dot(ia[...], qa[:, part]) + dot(ib[...], qb[:, part]), j * D)
        put(dot(ma[:, :tokens], oa[...]) + dot(mb[:, :tokens], ob[...]), 3 * D)
        put(ma[:, tokens:].astype(jnp.float32) + mb[:, tokens:].astype(jnp.float32), 4 * D)

    return pl.pallas_call(
        body,
        in_specs=[pl.BlockSpec(memory_space=pltpu.VMEM)] * 8,
        out_specs=[pl.BlockSpec(memory_space=pltpu.VMEM)] * 5,
        out_shape=[
            jax.ShapeDtypeStruct(((b - a) * unit, 4 * D + PAD), jnp.bfloat16) for a, b in ROWS
        ],
        cost_estimate=pl.CostEstimate(
            flops=2 * 512 * 16 * unit * 4 * D, bytes_accessed=6 << 20, transcendentals=0
        ),
        compiler_params=pltpu.CompilerParams(vmem_limit_bytes=32 << 20),
    )(*inputs_t, *grad_qkv, *mixed_t, *attn_low)


def add(*values):
    return sum(value.astype(jnp.float32) for value in values)


def reduce_chunk(pieces, grid, unit):
    low = jnp.bfloat16
    two = 2 * unit
    diagonal_a, diagonal_b, to_x, to_y, own = pieces
    from_x = swap(diagonal_a, grid.along_x)
    from_y = swap(diagonal_b, grid.along_y)
    to_x = jnp.concatenate([to_x[:two], add(to_x[two:], from_y).astype(low)], axis=0)
    to_y = jnp.concatenate([add(to_y[:two], from_x).astype(low), to_y[two:]], axis=0)
    from_x = swap(to_x, grid.along_x)
    from_y = swap(to_y, grid.along_y)
    far = add(own[two:], from_x[two:], from_y[two:]).astype(low)
    received = swap(far, grid.inward)
    far = add(far, received).astype(low)
    received = swap(far, grid.middle)
    near = add(own[:two], from_x[:two], from_y[:two], received)
    received = swap(near[unit:].astype(low), grid.pair)
    return add(near[:unit], received)


def grid_reduce(operands, orders, grid, unit):
    (inputs_low, grad_qkv, mixed_low, attn_low, normed_low, up_low, down_low, activated, gains) = (
        operands
    )
    ffn = ffn_terms(
        share_left(normed_low, orders, grid),
        both(up_low, grid),
        share_left(down_low, orders, grid),
        both(activated, grid),
        unit,
    )
    gain_rows = jnp.pad(gains.astype(jnp.bfloat16), ((0, PAD - 2), (0, 0)))
    attention = attention_terms(
        share_left(inputs_low, orders, grid),
        both(grad_qkv, grid),
        share_left(jnp.concatenate([mixed_low, gain_rows], axis=0), orders, grid),
        both(attn_low, grid),
        unit,
    )
    ffn = reduce_chunk(ffn, grid, unit)
    attention = reduce_chunk(attention, grid, unit)
    return (
        attention[:, :D],
        attention[:, D : 2 * D],
        attention[:, 2 * D : 3 * D],
        attention[:, 3 * D : 4 * D],
        ffn[:, :FF],
        ffn[:, FF:].T,
        attention[:, 4 * D : 4 * D + 2].T,
    )


def per_device(
    sizes,
    tokens,
    lengths,
    query_weight,
    key_weight,
    value_weight,
    attn_out_weight,
    up_weight,
    down_weight,
    norm_gains,
    cotangent,
):
    shards = (
        query_weight,
        key_weight,
        value_weight,
        attn_out_weight,
        up_weight,
        down_weight,
        norm_gains,
    )
    hidden = tokens[0].astype(jnp.float32)
    length = lengths[0]
    weights_all = [unpack(collect(shards, layer)) for layer in range(LAYERS)]
    kept_all = []
    for layer in range(LAYERS):
        hidden, kept = layer_forward(hidden, length, weights_all[layer], layer % 2 == 1)
        kept_all.append(kept)
    activations = hidden.astype(jnp.bfloat16)[None]
    grad_hidden = cotangent[0].astype(jnp.float32)
    layer_grads = [None] * LAYERS
    tuned = sizes == (4, 8)
    if tuned:
        unit = query_weight.shape[1]
        grid, orders = Grid(), row_orders(unit)
    for layer in reversed(range(LAYERS)):
        grad_hidden, operands = layer_backward(
            grad_hidden, kept_all[layer], weights_all[layer], layer % 2 == 1, length
        )
        if tuned:
            layer_grads[layer] = grid_reduce(operands, orders, grid, unit)
        else:
            layer_grads[layer] = plain_reduce(operands)
    stacked = tuple((jnp.stack([entry[member] for entry in layer_grads]) for member in range(7)))
    return (activations, grad_hidden[None], *stacked)


def solution(mesh):
    placed = (
        P(("dp", "fsdp"), None, None),
        P(("dp", "fsdp")),
        P(None, ("dp", "fsdp"), None),
        P(None, ("dp", "fsdp"), None),
        P(None, ("dp", "fsdp"), None),
        P(None, ("dp", "fsdp"), None),
        P(None, ("dp", "fsdp"), None),
        P(None, None, ("dp", "fsdp")),
        P(None, None, ("dp", "fsdp")),
        P(("dp", "fsdp"), None, None),
    )
    return jax.shard_map(
        functools.partial(per_device, (mesh.shape["dp"], mesh.shape["fsdp"])),
        mesh=mesh,
        in_specs=placed,
        out_specs=(
            P(("dp", "fsdp"), None, None),
            P(("dp", "fsdp"), None, None),
            P(None, ("dp", "fsdp"), None),
            P(None, ("dp", "fsdp"), None),
            P(None, ("dp", "fsdp"), None),
            P(None, ("dp", "fsdp"), None),
            P(None, ("dp", "fsdp"), None),
            P(None, None, ("dp", "fsdp")),
            P(None, None, ("dp", "fsdp")),
        ),
        check_vma=False,
    )
```

```python
import functools

import jax
import jax.numpy as jnp
from jax import lax
from jax.experimental import pallas as pl
from jax.experimental.pallas import tpu as pltpu
import numpy as np
from jax.sharding import PartitionSpec as P

D = 768
HEADS = 12
HEAD_DIM = 64
FF = 3072
LAYERS = 2
PAD = 128


def norm(value, gain):
    centred = value - jnp.mean(value, axis=-1, keepdims=True)
    spread = jnp.mean(centred * centred, axis=-1, keepdims=True)
    return centred * lax.rsqrt(spread + 1e-05) * gain


def gelu_tanh(value):
    return jax.nn.gelu(value, approximate=True)


def product(left, right):
    return jnp.dot(left, right, preferred_element_type=jnp.float32)


def product_left_t(left, right):
    return lax.dot_general(
        left, right, (((0,), (0,)), ((), ())), preferred_element_type=jnp.float32
    )


def product_right_t(left, right):
    return lax.dot_general(
        left, right, (((1,), (1,)), ((), ())), preferred_element_type=jnp.float32
    )


def pack_attention(shards, layer):
    query_w, key_w, value_w, out_w, _, _, gains = (member[layer] for member in shards)
    gain_columns = jnp.pad(gains.T, ((0, 0), (0, PAD - 2)))
    return jnp.concatenate([query_w, key_w, value_w, out_w, gain_columns], axis=1)


def pack_ffn(shards, layer):
    return jnp.concatenate([shards[4][layer], shards[5][layer].T], axis=1)


def plain_gather(block):
    return lax.all_gather(block, ("dp", "fsdp"), axis=0, tiled=True)


def unpack(attention, ffn):
    return (
        attention[:, : 3 * D],
        attention[:, 3 * D : 4 * D],
        ffn[:, :FF],
        ffn[:, FF:],
        attention[:, 4 * D : 4 * D + 2].T.astype(jnp.float32),
    )


def visible_keys(length, token_count, swap):
    half = token_count // 2
    positions = lax.broadcasted_iota(jnp.int32, (2, half), 0) * half + lax.broadcasted_iota(
        jnp.int32, (2, half), 1
    )
    if swap:
        positions = positions[::-1]
    return positions < length


def split_heads(value):
    return value.reshape(2, value.shape[0] // 2, HEADS, HEAD_DIM)


def paired_heads(query, keys, values, swap):
    query_heads = split_heads(query)
    key_heads = split_heads(keys)
    value_heads = split_heads(values)
    if swap:
        key_heads = key_heads[::-1]
        value_heads = value_heads[::-1]
    return (query_heads, key_heads, value_heads)


def masked_scores(query_heads, key_heads, visible):
    scores = (
        jnp.einsum("bqhd,bkhd->bhqk", query_heads, key_heads, preferred_element_type=jnp.float32)
        * 0.125
    )
    return jnp.where(visible[:, None, None, :], scores, -1e30)


def attend_forward(query, keys, values, visible, swap):
    token_count = query.shape[0]
    query_heads, key_heads, value_heads = paired_heads(query, keys, values, swap)
    scores = masked_scores(query_heads, key_heads, visible)
    highest = jnp.max(scores, axis=-1, keepdims=True)
    raised = jnp.exp(scores - highest)
    total = jnp.sum(raised, axis=-1, keepdims=True)
    shares = (raised / total).astype(jnp.bfloat16)
    mixed = jnp.einsum("bhqk,bkhd->bqhd", shares, value_heads, preferred_element_type=jnp.float32)
    return (mixed.reshape(token_count, -1), highest + jnp.log(total))


def attend_backward(query, keys, values, visible, swap, log_total, grad_mixed):
    token_count = query.shape[0]
    query_heads, key_heads, value_heads = paired_heads(query, keys, values, swap)
    scores = masked_scores(query_heads, key_heads, visible)
    shares = jnp.exp(scores - log_total)
    shares_low = shares.astype(jnp.bfloat16)
    grad_heads = split_heads(grad_mixed)
    grad_values = jnp.einsum(
        "bhqk,bqhd->bkhd", shares_low, grad_heads, preferred_element_type=jnp.float32
    )
    grad_shares = jnp.einsum(
        "bqhd,bkhd->bhqk", grad_heads, value_heads, preferred_element_type=jnp.float32
    )
    inner = jnp.sum(shares * grad_shares, axis=-1, keepdims=True)
    grad_scores = (shares * (grad_shares - inner)).astype(jnp.bfloat16)
    grad_query = (
        jnp.einsum("bhqk,bkhd->bqhd", grad_scores, key_heads, preferred_element_type=jnp.float32)
        * 0.125
    )
    grad_keys = (
        jnp.einsum("bhqk,bqhd->bkhd", grad_scores, query_heads, preferred_element_type=jnp.float32)
        * 0.125
    )
    if swap:
        grad_keys = grad_keys[::-1]
        grad_values = grad_values[::-1]
    return tuple(
        (
            member.reshape(token_count, -1).astype(jnp.bfloat16)
            for member in (grad_query, grad_keys, grad_values)
        )
    )


def layer_forward(hidden, length, weights, swap):
    qkv_w, out_w, up_w, down_t, gains = weights
    inputs_low = hidden.astype(jnp.bfloat16)
    qkv = product(inputs_low, qkv_w).astype(jnp.bfloat16)
    query, keys, values = qkv[:, :D], qkv[:, D : 2 * D], qkv[:, 2 * D :]
    visible = visible_keys(length, hidden.shape[0], swap)
    mixed, log_total = attend_forward(query, keys, values, visible, swap)
    mixed_low = mixed.astype(jnp.bfloat16)
    first_sum = hidden + product(mixed_low, out_w)
    normed = norm(first_sum, gains[0])
    normed_low = normed.astype(jnp.bfloat16)
    expanded = product(normed_low, up_w)
    activated = gelu_tanh(expanded).astype(jnp.bfloat16)
    second_sum = normed + product_right_t(activated, down_t)
    output = norm(second_sum, gains[1])
    kept = (
        inputs_low,
        query,
        keys,
        values,
        log_total,
        mixed_low,
        first_sum,
        normed_low,
        expanded,
        activated,
        second_sum,
    )
    return (output, kept)


def down_backward(grad_output, kept, weights):
    grad_second, grad_gain = jax.vjp(norm, kept[10], weights[4][1])[1](grad_output)
    return (grad_second, grad_second.astype(jnp.bfloat16), grad_gain)


def up_backward(grad_second, down_low, kept, weights):
    grad_active = product(down_low, weights[3])
    up_low = jax.vjp(gelu_tanh, kept[8])[1](grad_active)[0].astype(jnp.bfloat16)
    return (grad_second + product_right_t(up_low, weights[2]), up_low)


def mixed_backward(grad_normed, kept, weights):
    grad_first, grad_gain = jax.vjp(norm, kept[6], weights[4][0])[1](grad_normed)
    attn_low = grad_first.astype(jnp.bfloat16)
    grad_mixed = product_right_t(attn_low, weights[1]).astype(jnp.bfloat16)
    return (grad_first, attn_low, grad_mixed, grad_gain)


def scores_backward(grad_mixed, kept, swapped, length):
    query, keys, values, log_total = kept[1:5]
    visible = visible_keys(length, query.shape[0], swapped)
    return jnp.concatenate(
        attend_backward(query, keys, values, visible, swapped, log_total, grad_mixed), axis=1
    )


def inputs_backward(grad_first, grad_qkv, weights):
    return grad_first + product_right_t(grad_qkv, weights[0])


def plain_scatter(terms):
    return lax.psum_scatter(
        terms.astype(jnp.bfloat16), ("dp", "fsdp"), scatter_dimension=0, tiled=True
    ).astype(jnp.float32)


def plain_ffn_terms(operands):
    normed_low, up_low, down_low, activated = operands
    return jnp.concatenate(
        [
            product_left_t(normed_low, up_low).astype(jnp.bfloat16),
            product_left_t(down_low, activated).astype(jnp.bfloat16),
        ],
        axis=1,
    )


def plain_attention_terms(operands, gains):
    inputs_low, grad_qkv, mixed_low, attn_low = operands
    return jnp.concatenate(
        [
            product_left_t(inputs_low, grad_qkv).astype(jnp.bfloat16),
            product_left_t(mixed_low, attn_low).astype(jnp.bfloat16),
            jnp.pad(gains.T, ((0, 0), (0, PAD - 2))).astype(jnp.bfloat16),
        ],
        axis=1,
    )


def attention_outputs(summed):
    return (
        *(summed[:, j * D : (j + 1) * D] for j in range(4)),
        summed[:, 4 * D : 4 * D + 2].T,
    )


def ffn_outputs(summed):
    return (summed[:, :FF], summed[:, FF:].T)


class Grid:
    def __init__(self):
        places = [
            (x, core, z, y) for x in range(2) for core in range(2) for z in range(4) for y in range(2)
        ]
        number = {place: index for index, place in enumerate(places)}

        def route(move, senders=range(4)):
            return [
                (number[place], number[move(*place)]) for place in places if place[2] in senders
            ]

        self.core = route(lambda x, core, z, y: (x, 1 - core, z, y))
        self.along_x = route(lambda x, core, z, y: (1 - x, core, z, y))
        self.along_y = route(lambda x, core, z, y: (x, core, z, 1 - y))
        self.pair = route(lambda x, core, z, y: (x, core, z ^ 1, y))
        self.middle = route(lambda x, core, z, y: (x, core, 3 - z, y), (1, 2))
        self.outward = route(lambda x, core, z, y: (x, core, z ^ 1, y), (1, 2))
        self.inward = route(lambda x, core, z, y: (x, core, z ^ 1, y), (0, 3))


def swap(value, route):
    return lax.ppermute(value, ("dp", "fsdp"), route)


SLOTS = np.array([(dx, dy, s) for dx, dy in ((1, 1), (1, 0), (0, 1), (0, 0)) for s in range(4)])


def row_order(unit):
    dp, fsdp = lax.axis_index("dp"), lax.axis_index("fsdp")
    x, core, z, y = dp // 2, dp % 2, fsdp // 2, fsdp % 2
    dx, dy, s = (jnp.asarray(np.repeat(SLOTS[:, j], unit), jnp.int32) for j in range(3))
    offset = jnp.asarray(np.tile(np.arange(unit), 16), jnp.int32)
    place = jnp.where(s < 2, z ^ s, jnp.where(z < 2, s, 3 - s))
    rows = jnp.concatenate(
        [
            ((((x ^ dx) * 2 + owner) * 4 + place) * 2 + (y ^ dy)) * unit + offset
            for owner in (core, 1 - core)
        ]
    )
    natural = lax.broadcasted_iota(jnp.int32, (32 * unit, 32 * unit), 0)
    return (natural == rows[None]).astype(jnp.bfloat16)


def share_left(values, order, grid):
    lengths = [max(value.shape[0], PAD) for value in values]
    half = D // 2

    def body(order_ref, *refs):
        for j, value_ref in enumerate(refs[: len(values)]):
            ordered = dot(value_ref[...].astype(jnp.bfloat16), order_ref[...])
            short = lengths[j] - ordered.shape[0]
            if short:
                ordered = jnp.concatenate([ordered, jnp.zeros((short, D), jnp.float32)], axis=0)
            turned = ordered.T.astype(jnp.bfloat16)
            refs[len(values) + 2 * j][...] = turned[:half]
            refs[len(values) + 2 * j + 1][...] = turned[half:]

    turned = pl.pallas_call(
        body,
        in_specs=[VMEM_SPEC] * (1 + len(values)),
        out_specs=[VMEM_SPEC] * (2 * len(values)),
        out_shape=shapes(*(((half, n), jnp.bfloat16) for n in lengths for _ in range(2))),
        cost_estimate=pl.CostEstimate(
            flops=2 * D * D * sum(lengths), bytes_accessed=2 << 20, transcendentals=0
        ),
        compiler_params=params(24),
    )(order, *values)
    return [(turned[2 * j], swap(turned[2 * j + 1], grid.core)) for j in range(len(values))]


def both(value, grid):
    return (value, swap(value, grid.core))


ROWS = ((0, 2), (2, 4), (4, 8), (8, 12), (12, 16))


def dot(left, right):
    return jnp.dot(left, right, preferred_element_type=jnp.float32)


def dot_nt(left, right):
    return lax.dot_general(
        left, right, (((1,), (1,)), ((), ())), preferred_element_type=jnp.float32
    )


def dot_tn(left, right):
    return lax.dot_general(
        left, right, (((0,), (0,)), ((), ())), preferred_element_type=jnp.float32
    )


def lane_masks():
    lane = lax.broadcasted_iota(jnp.int32, (1, 2 * HEAD_DIM), 1)
    first = (lane < HEAD_DIM).astype(jnp.float32)
    return first.astype(jnp.bfloat16), (1.0 - first).astype(jnp.bfloat16), lane < HEAD_DIM


def two_heads(value, masks):
    return jnp.concatenate([value * masks[0], value * masks[1]], axis=0)


def pair_softmax(query_pair, keys, key_block, length):
    half = keys.shape[0]
    scores = dot_nt(query_pair, keys) * 0.125
    position = lax.broadcasted_iota(jnp.int32, scores.shape, 1) + key_block * half
    scores = jnp.where(position < length, scores, -1e30)
    raised = jnp.exp(scores - jnp.max(scores, axis=-1, keepdims=True))
    return raised / jnp.sum(raised, axis=-1, keepdims=True)


def normalised(value):
    centred = value - jnp.mean(value, axis=-1, keepdims=True)
    rate = lax.rsqrt(jnp.mean(centred * centred, axis=-1, keepdims=True) + 1e-05)
    return centred * rate, rate


def norm_backward(value, gain, grad):
    ratio, rate = normalised(value)
    scaled = grad * gain
    slope = jnp.mean(scaled * ratio, axis=-1, keepdims=True)
    result = rate * (scaled - jnp.mean(scaled, axis=-1, keepdims=True) - ratio * slope)
    return result, jnp.sum(grad * ratio, axis=0, keepdims=True)


def head_parts(half, swapped):
    for block in range(2):
        key_block = 1 - block if swapped else block
        rows = slice(block * half, (block + 1) * half)
        key_rows = slice(key_block * half, (key_block + 1) * half)
        for pair in range(HEADS // 2):
            yield key_block, rows, key_rows, pair * 2 * HEAD_DIM


VMEM_SPEC = pl.BlockSpec(memory_space=pltpu.VMEM)
SMEM_SPEC = pl.BlockSpec(memory_space=pltpu.SMEM)
ANY_SPEC = pl.BlockSpec(memory_space=pl.ANY)


def params(mebibytes):
    return pltpu.CompilerParams(vmem_limit_bytes=mebibytes << 20)


def shapes(*pairs):
    return [jax.ShapeDtypeStruct(shape, dtype) for shape, dtype in pairs]


def attention_columns(weights, start, target, sems):
    copies = []
    for part in range(5):
        width = D if part < 4 else PAD
        copies.append(
            pltpu.make_async_copy(
                weights.at[:, pl.ds(start + part * D, width)],
                target.at[:, pl.ds(part * D, width)],
                sems.at[part],
            )
        )
    for copy in copies:
        copy.start()
    return copies


def attention_forward(hidden, lengths, weights, start, swapped):
    tokens = hidden.shape[0]
    half = tokens // 2
    low = jnp.bfloat16

    def body(length_ref, hidden_ref, w_any, low_out, qkv, mixed, first_sum, gains, w, sems):
        copies = attention_columns(w_any, start, w, sems)
        value = hidden_ref[...].astype(low)
        low_out[...] = value
        masks = lane_masks()
        for part in range(3):
            copies[part].wait()
            columns = slice(part * D, (part + 1) * D)
            qkv[:, columns] = dot(value, w[:, columns]).astype(low)
        for key_block, rows, key_rows, lane in head_parts(half, swapped):
            query = two_heads(qkv[rows, lane : lane + 128], masks)
            keys = qkv[key_rows, D + lane : D + lane + 128]
            values = qkv[key_rows, 2 * D + lane : 2 * D + lane + 128]
            shares = pair_softmax(query, keys, key_block, length_ref[0]).astype(low)
            out = dot(shares, values)
            mixed[rows, lane : lane + 128] = jnp.where(masks[2], out[:half], out[half:]).astype(low)
        copies[3].wait()
        first_sum[...] = hidden_ref[...] + dot(mixed[...], w[:, 3 * D : 4 * D])
        copies[4].wait()
        gains[...] = w[:, 4 * D :].astype(jnp.float32).T[:8]

    return pl.pallas_call(
        body,
        in_specs=[SMEM_SPEC, VMEM_SPEC, ANY_SPEC],
        out_specs=[VMEM_SPEC] * 5,
        out_shape=shapes(
            ((tokens, D), low),
            ((tokens, 3 * D), low),
            ((tokens, D), low),
            ((tokens, D), jnp.float32),
            ((8, D), jnp.float32),
        ),
        scratch_shapes=[pltpu.VMEM((D, 4 * D + PAD), low), pltpu.SemaphoreType.DMA((5,))],
        cost_estimate=pl.CostEstimate(
            flops=2 * tokens * D * 4 * D, bytes_accessed=9 << 20, transcendentals=0
        ),
        compiler_params=params(40),
    )(lengths, hidden, weights)


FF_TILE = D


def ffn_forward(first_sum, gains, weights, start):
    tokens = first_sum.shape[0]
    low = jnp.bfloat16
    steps = FF // FF_TILE
    first = start // FF_TILE

    def body(sum_ref, gain_ref, up, down, normed_low, activated, slope, second_sum, out, total):
        step = pl.program_id(0)

        @pl.when(step == 0)
        def _():
            normed = normalised(sum_ref[...])[0] * gain_ref[0:1]
            normed_low[...] = normed.astype(low)
            total[...] = normed

        u = dot(normed_low[...], up[...])
        inner = 0.7978845608028654 * (u + 0.044715 * (u * u * u))
        wave = jnp.tanh(inner)
        active = (0.5 * u * (1.0 + wave)).astype(low)
        slope[...] = (
            0.5 * (1.0 + wave)
            + 0.5 * u * (1.0 - wave * wave) * (0.7978845608028654 * (1.0 + 0.134145 * (u * u)))
        ).astype(low)
        activated[...] = active
        total[...] += dot_nt(active, down[...])

        @pl.when(step == steps - 1)
        def _():
            second_sum[...] = total[...]
            out[...] = normalised(total[...])[0] * gain_ref[1:2]

    def fixed(shape):
        return pl.BlockSpec(shape, lambda j: (0, 0))

    wide = pl.BlockSpec((tokens, FF_TILE), lambda j: (0, j))
    return pl.pallas_call(
        body,
        grid=(steps,),
        in_specs=[
            fixed((tokens, D)),
            fixed((8, D)),
            pl.BlockSpec((D, FF_TILE), lambda j: (0, first + j)),
            pl.BlockSpec((D, FF_TILE), lambda j: (0, first + steps + j)),
        ],
        out_specs=[fixed((tokens, D)), wide, wide, fixed((tokens, D)), fixed((tokens, D))],
        out_shape=shapes(
            ((tokens, D), low),
            ((tokens, FF), low),
            ((tokens, FF), low),
            ((tokens, D), jnp.float32),
            ((tokens, D), jnp.float32),
        ),
        scratch_shapes=[pltpu.VMEM((tokens, D), jnp.float32)],
        cost_estimate=pl.CostEstimate(
            flops=4 * tokens * D * FF, bytes_accessed=15 << 20, transcendentals=tokens * FF
        ),
        compiler_params=params(40),
    )(first_sum, gains, weights, weights)


def second_norm_backward(grad, second_sum, gains):
    tokens = grad.shape[0]

    def body(grad_ref, sum_ref, gain_ref, out, low_out, gain_out):
        result, gain_grad = norm_backward(sum_ref[...], gain_ref[1:2], grad_ref[...].astype(jnp.float32))
        out[...] = result
        low_out[...] = result.astype(jnp.bfloat16)
        gain_out[...] = gain_grad

    return pl.pallas_call(
        body,
        in_specs=[VMEM_SPEC] * 3,
        out_specs=[VMEM_SPEC] * 3,
        out_shape=shapes(
            ((tokens, D), jnp.float32), ((tokens, D), jnp.bfloat16), ((1, D), jnp.float32)
        ),
        cost_estimate=pl.CostEstimate(flops=0, bytes_accessed=3 << 20, transcendentals=0),
        compiler_params=params(16),
    )(grad, second_sum, gains)


def up_backward_kernel(grad_second, down_low, slope, weights, start):
    tokens = grad_second.shape[0]
    low = jnp.bfloat16
    steps = FF // FF_TILE
    first = start // FF_TILE

    def body(grad_ref, low_ref, slope_ref, up, down, up_low, out):
        step = pl.program_id(0)

        @pl.when(step == 0)
        def _():
            out[...] = grad_ref[...]

        piece = (dot(low_ref[...], down[...]) * slope_ref[...].astype(jnp.float32)).astype(low)
        up_low[...] = piece
        out[...] += dot_nt(piece, up[...])

    def fixed(shape):
        return pl.BlockSpec(shape, lambda j: (0, 0))

    wide = pl.BlockSpec((tokens, FF_TILE), lambda j: (0, j))
    return pl.pallas_call(
        body,
        grid=(steps,),
        in_specs=[
            fixed((tokens, D)),
            fixed((tokens, D)),
            wide,
            pl.BlockSpec((D, FF_TILE), lambda j: (0, first + j)),
            pl.BlockSpec((D, FF_TILE), lambda j: (0, first + steps + j)),
        ],
        out_specs=[wide, fixed((tokens, D))],
        out_shape=shapes(((tokens, FF), low), ((tokens, D), jnp.float32)),
        cost_estimate=pl.CostEstimate(
            flops=4 * tokens * D * FF, bytes_accessed=14 << 20, transcendentals=0
        ),
        compiler_params=params(40),
    )(grad_second, down_low, slope, weights, weights)


def attention_backward_kernel(grad, first_sum, gains, qkv, lengths, weights, start, swapped):
    tokens = grad.shape[0]
    half = tokens // 2
    low = jnp.bfloat16

    def body(length_ref, grad_ref, sum_ref, gain_ref, qkv_ref, w_any, *rest):
        attn_low, grad_qkv, grad_in, gain_out, grad_mixed, w, sems = rest
        copies = attention_columns(w_any, start, w, sems)
        masks = lane_masks()
        result, gain_grad = norm_backward(sum_ref[...], gain_ref[0:1], grad_ref[...])
        grad_in[...] = result
        attn_low[...] = result.astype(low)
        gain_out[...] = gain_grad
        copies[3].wait()
        grad_mixed[...] = dot_nt(attn_low[...], w[:, 3 * D : 4 * D]).astype(low)
        for key_block, rows, key_rows, lane in head_parts(half, swapped):
            query = two_heads(qkv_ref[rows, lane : lane + 128], masks)
            keys = qkv_ref[key_rows, D + lane : D + lane + 128]
            values = qkv_ref[key_rows, 2 * D + lane : 2 * D + lane + 128]
            arriving = two_heads(grad_mixed[rows, lane : lane + 128], masks)
            shares = pair_softmax(query, keys, key_block, length_ref[0])
            grad_values = dot_tn(shares.astype(low), arriving)
            grad_shares = dot_nt(arriving, values)
            inner = jnp.sum(shares * grad_shares, axis=-1, keepdims=True)
            grad_scores = (shares * (grad_shares - inner)).astype(low)
            grad_query = dot(grad_scores, keys) * 0.125
            grad_keys = dot_tn(grad_scores, query) * 0.125
            grad_qkv[rows, lane : lane + 128] = jnp.where(
                masks[2], grad_query[:half], grad_query[half:]
            ).astype(low)
            grad_qkv[key_rows, D + lane : D + lane + 128] = grad_keys.astype(low)
            grad_qkv[key_rows, 2 * D + lane : 2 * D + lane + 128] = grad_values.astype(low)
        for part in (0, 1, 2):
            copies[part].wait()
            columns = slice(part * D, (part + 1) * D)
            grad_in[...] += dot_nt(grad_qkv[:, columns], w[:, columns])
        copies[4].wait()

    return pl.pallas_call(
        body,
        in_specs=[SMEM_SPEC] + [VMEM_SPEC] * 4 + [ANY_SPEC],
        out_specs=[VMEM_SPEC] * 4,
        out_shape=shapes(
            ((tokens, D), low),
            ((tokens, 3 * D), low),
            ((tokens, D), jnp.float32),
            ((1, D), jnp.float32),
        ),
        scratch_shapes=[
            pltpu.VMEM((tokens, D), low),
            pltpu.VMEM((D, 4 * D + PAD), low),
            pltpu.SemaphoreType.DMA((5,)),
        ],
        cost_estimate=pl.CostEstimate(
            flops=2 * tokens * D * 4 * D, bytes_accessed=10 << 20, transcendentals=0
        ),
        compiler_params=params(40),
    )(lengths, grad, first_sum, gains, qkv, weights)


def matrix_terms(left_t, right, unit):
    tile = D

    def body(la, lb, ra, rb, *outs):
        value = (dot(la[...], ra[...]) + dot(lb[...], rb[...])).astype(jnp.bfloat16)
        for (low, high), out in zip(ROWS, outs):
            out[...] = value[low * unit : high * unit]

    def whole(value):
        return pl.BlockSpec(value.shape, lambda j: (0, 0))

    tokens, width = right[0].shape
    column = pl.BlockSpec((tokens, tile), lambda j: (0, j))
    return pl.pallas_call(
        body,
        grid=(width // tile,),
        in_specs=[whole(v) for v in left_t] + [column, column],
        out_specs=[pl.BlockSpec(((b - a) * unit, tile), lambda j: (0, j)) for a, b in ROWS],
        out_shape=[jax.ShapeDtypeStruct(((b - a) * unit, width), jnp.bfloat16) for a, b in ROWS],
        cost_estimate=pl.CostEstimate(
            flops=4 * tokens * 16 * unit * width, bytes_accessed=6 << 20, transcendentals=0
        ),
        compiler_params=pltpu.CompilerParams(vmem_limit_bytes=32 << 20),
    )(*left_t, *right)


def attention_terms(inputs_t, grad_qkv, mixed_t, attn_low, gains_t, unit, extra=()):
    wide = extra[1][0].shape[1] if extra else 0
    width = 4 * D + PAD + wide

    def body(ia, ib, qa, qb, ma, mb, oa, ob, ga, gb, *refs):
        outs = refs[4 if extra else 0 :]

        def put(value, column):
            value = value.astype(jnp.bfloat16)
            for (low, high), out in zip(ROWS, outs):
                out[:, column : column + value.shape[1]] = value[low * unit : high * unit]

        for j in range(3):
            part = slice(j * D, (j + 1) * D)
            put(dot(ia[...], qa[:, part]) + dot(ib[...], qb[:, part]), j * D)
        put(dot(ma[...], oa[...]) + dot(mb[...], ob[...]), 3 * D)
        put(ga[...].astype(jnp.float32) + gb[...].astype(jnp.float32), 4 * D)
        for j in range(wide // D):
            la, lb, ra, rb = refs[:4]
            part = slice(j * D, (j + 1) * D)
            put(dot(la[...], ra[:, part]) + dot(lb[...], rb[:, part]), 4 * D + PAD + j * D)

    operands = [*inputs_t, *grad_qkv, *mixed_t, *attn_low, *gains_t]
    for pair in extra:
        operands += pair
    return pl.pallas_call(
        body,
        in_specs=[VMEM_SPEC] * len(operands),
        out_specs=[VMEM_SPEC] * 5,
        out_shape=shapes(*((((b - a) * unit, width), jnp.bfloat16) for a, b in ROWS)),
        cost_estimate=pl.CostEstimate(
            flops=2 * 512 * 16 * unit * width, bytes_accessed=12 << 20, transcendentals=0
        ),
        compiler_params=params(40),
    )(*operands)


def add(*values):
    return sum(value.astype(jnp.float32) for value in values)


class Reduction:
    def __init__(self, pieces, grid, unit):
        self.grid, self.unit, self.round, self.due = grid, unit, 0, False
        self.out, self.kept = list(pieces[:2]), list(pieces[2:])

    def state(self):
        return (self.out, self.kept)

    def restore(self, state):
        self.out, self.kept = state

    def send(self):
        grid = self.grid
        routes = (
            (grid.along_x, grid.along_y),
            (grid.along_x, grid.along_y),
            (grid.inward,),
            (grid.middle,),
            (grid.pair,),
        )[self.round]
        self.out = [swap(value, route) for value, route in zip(self.out, routes)]
        self.round += 1

    def prepare(self):
        low, unit, two = jnp.bfloat16, self.unit, 2 * self.unit
        if self.round == 1:
            (from_x, from_y), (to_x, to_y, own) = self.out, self.kept
            to_x = jnp.concatenate([to_x[:two], add(to_x[two:], from_y).astype(low)], axis=0)
            to_y = jnp.concatenate([add(to_y[:two], from_x).astype(low), to_y[two:]], axis=0)
            self.out, self.kept = [to_x, to_y], [own]
        elif self.round == 2:
            (from_x, from_y), (own,) = self.out, self.kept
            self.out = [add(own[two:], from_x[two:], from_y[two:]).astype(low)]
            self.kept = [add(own[:two], from_x[:two], from_y[:two]).astype(low), self.out[0]]
        elif self.round == 3:
            near, far = self.kept
            self.out, self.kept = [add(far, self.out[0]).astype(low)], [near]
        else:
            near = add(self.kept[0], self.out[0])
            self.out, self.kept = [near[unit:].astype(low)], [near[:unit]]

    def result(self):
        return add(self.kept[0], self.out[0])


def gate(values, *earlier):
    return lax.optimization_barrier((values, earlier))[0]


class Segments:
    def __init__(self):
        self.active = []

    def run(self, sends, late, compute, values):
        for reduction in sends:
            if reduction not in self.active:
                self.active.append(reduction)
        waiting = [r for r in self.active if r not in sends and r not in late and r.due]
        for reduction in sends:
            reduction.send()
            reduction.due = True
        for reduction in late:
            if reduction.due:
                reduction.prepare()
            reduction.send()
            reduction.due = True
        for reduction in waiting:
            if reduction.round < 2:
                reduction.prepare()
                reduction.due = False
        values = compute(values)
        states = [reduction.state() for reduction in self.active]
        states, values = lax.optimization_barrier((states, values))
        for reduction, state in zip(self.active, states):
            reduction.restore(state)
        self.active = [r for r in self.active if r.round < 5]
        return values


class Gathering:
    def __init__(self, block, grid):
        self.pieces, self.grid, self.unit = [block], grid, block.shape[0]
        self.steps = [self.pair, self.middle, self.outward, self.square, self.diagonal]

    def advance(self):
        self.pieces = list(self.steps.pop(0)(self.pieces, self.grid, 2 * self.unit))

    @staticmethod
    def pair(pieces, grid, two):
        (block,) = pieces
        return (jnp.concatenate([block, swap(block, grid.pair)], axis=0),)

    @staticmethod
    def middle(pieces, grid, two):
        (near,) = pieces
        return (near, swap(near, grid.middle))

    @staticmethod
    def outward(pieces, grid, two):
        near, far = pieces
        z = lax.axis_index("fsdp") // 2
        far = jnp.where((z == 1) | (z == 2), far, swap(far, grid.outward))
        return (jnp.concatenate([near, far], axis=0),)

    @staticmethod
    def square(pieces, grid, two):
        (line,) = pieces
        return (line, swap(line, grid.along_x), swap(line, grid.along_y))

    @staticmethod
    def diagonal(pieces, grid, two):
        line, from_x, from_y = pieces
        return (
            swap(from_y[:two], grid.along_x),
            swap(from_x[two:], grid.along_y),
            from_x,
            from_y,
            line,
        )

    def result(self):
        pieces = self.pieces
        return place_blocks(pieces + [swap(piece, self.grid.core) for piece in pieces], self.unit)


def place_blocks(pieces, unit):
    width = pieces[0].shape[1]
    dp, fsdp = lax.axis_index("dp"), lax.axis_index("fsdp")
    x, core, z, y = dp // 2, dp % 2, fsdp // 2, fsdp % 2
    dx, dy, s = (jnp.asarray(SLOTS[:, j], jnp.int32) for j in range(3))
    place = jnp.where(s < 2, z ^ s, jnp.where(z < 2, s, 3 - s))
    rows = jnp.concatenate(
        [(((x ^ dx) * 2 + owner) * 4 + place) * 2 + (y ^ dy) for owner in (core, 1 - core)]
    )

    tiles = unit // 8

    def body(rows_ref, *refs):
        sources, target = refs[:10], refs[10]
        for half in range(2):
            for (low, high), source in zip(ROWS, sources[half * 5 : half * 5 + 5]):
                for slot in range(low, high):
                    row = rows_ref[half * 16 + slot] * tiles
                    first = (slot - low) * tiles
                    target[pl.ds(row, tiles)] = source[first : first + tiles]

    placed = pl.pallas_call(
        body,
        in_specs=[pl.BlockSpec(memory_space=pltpu.SMEM)]
        + [pl.BlockSpec(memory_space=pltpu.VMEM)] * 10,
        out_specs=pl.BlockSpec(memory_space=pltpu.VMEM),
        out_shape=jax.ShapeDtypeStruct((32 * tiles, 8, width), jnp.bfloat16),
        cost_estimate=pl.CostEstimate(
            flops=0, bytes_accessed=4 * 32 * unit * width, transcendentals=0
        ),
        compiler_params=pltpu.CompilerParams(vmem_limit_bytes=40 << 20),
    )(rows, *(piece.reshape(-1, 8, width) for piece in pieces))
    return placed.reshape(32 * unit, width)


def per_device(
    sizes,
    tokens,
    lengths,
    query_weight,
    key_weight,
    value_weight,
    attn_out_weight,
    up_weight,
    down_weight,
    norm_gains,
    cotangent,
):
    shards = (
        query_weight,
        key_weight,
        value_weight,
        attn_out_weight,
        up_weight,
        down_weight,
        norm_gains,
    )
    if sizes == (4, 8):
        return grid_step(tokens, lengths, shards, cotangent)
    hidden = tokens[0].astype(jnp.float32)
    length = lengths[0]
    weights_all = [
        unpack(plain_gather(pack_attention(shards, j)), plain_gather(pack_ffn(shards, j)))
        for j in range(LAYERS)
    ]
    kept_all = []
    for layer in range(LAYERS):
        hidden, kept = layer_forward(hidden, length, weights_all[layer], layer % 2 == 1)
        kept_all.append(kept)
    grad = cotangent[0].astype(jnp.float32)
    outputs = [None] * LAYERS
    for layer in reversed(range(LAYERS)):
        kept, weights = kept_all[layer], weights_all[layer]
        grad_second, down_low, gain_second = down_backward(grad, kept, weights)
        grad_normed, up_low = up_backward(grad_second, down_low, kept, weights)
        ffn = plain_scatter(plain_ffn_terms((kept[7], up_low, down_low, kept[9])))
        grad_first, attn_low, grad_mixed, gain_first = mixed_backward(grad_normed, kept, weights)
        grad_qkv = scores_backward(grad_mixed, kept, layer % 2 == 1, length)
        grad = inputs_backward(grad_first, grad_qkv, weights)
        gains = jnp.stack([gain_first, gain_second])
        attention = plain_scatter(
            plain_attention_terms((kept[0], grad_qkv, kept[5], attn_low), gains)
        )
        outputs[layer] = (attention_outputs(attention), ffn_outputs(ffn))
    return finish(hidden, grad, outputs)


def finish(hidden, grad, outputs):
    layers = [(*attention[:4], *ffn, attention[4]) for attention, ffn in outputs]
    stacked = tuple((jnp.stack([entry[member] for entry in layers]) for member in range(7)))
    return (hidden.astype(jnp.bfloat16)[None], grad[None], *stacked)


def gather_first_layer(blocks, grid):
    attention, ffn = (Gathering(block, grid) for block in blocks)
    for moves in (
        (attention,),
        (attention, ffn),
        (attention, ffn),
        (attention, ffn),
        (attention,),
    ):
        for gathering in moves:
            gathering.advance()
        attention.pieces, ffn.pieces = lax.optimization_barrier((attention.pieces, ffn.pieces))
    first = attention.result()
    ffn.advance()
    ffn.advance()
    return first, ffn.result()


def grid_step(tokens, lengths, shards, cotangent):
    grid, unit = Grid(), shards[0].shape[1]
    order = row_order(unit)

    second = plain_gather(
        jnp.concatenate([pack_ffn(shards, 1), pack_attention(shards, 1)], axis=1)
    )
    first = gather_first_layer((pack_attention(shards, 0), pack_ffn(shards, 0)), grid)
    attention_at = ((first[0], 0, False), (second, 2 * FF, True))
    ffn_at = ((first[1], 0), (second, 0))

    hidden = tokens[0].astype(jnp.float32)
    kept, left, right = [], [], []
    for layer in range(LAYERS):
        inputs_low, qkv, mixed, first_sum, gains = attention_forward(
            hidden, lengths, *attention_at[layer]
        )
        normed_low, activated, slope, second_sum, hidden = ffn_forward(
            first_sum, gains, *ffn_at[layer]
        )
        kept.append((qkv, first_sum, gains, slope, second_sum))
        left.append(share_left((inputs_low, mixed, normed_low), order, grid))
        right.append(both(activated, grid))

    segments = Segments()

    def norm_part(layer, grad):
        qkv, first_sum, gains, slope, second_sum = kept[layer]
        grad_second, down_low, gain_grad = second_norm_backward(grad, second_sum, gains)
        return grad_second, down_low, gain_grad, *share_left((down_low,), order, grid)

    def up_part(layer, grad_second, down_low):
        up_low, grad = up_backward_kernel(grad_second, down_low, kept[layer][3], *ffn_at[layer])
        return grad, up_low

    def attention_part(layer, grad):
        qkv, first_sum, gains, slope, second_sum = kept[layer]
        return attention_backward_kernel(
            grad, first_sum, gains, qkv, lengths, *attention_at[layer]
        )

    def attention_pieces(layer, attn_low, grad_qkv, gain_first, gain_second, extra=()):
        gains = jnp.concatenate([gain_first, gain_second, jnp.zeros((6, D), jnp.float32)], axis=0)
        inputs_t, mixed_t, _ = left[layer]
        (gains_t,) = share_left((gains,), order, grid)
        return attention_terms(
            inputs_t, both(grad_qkv, grid), mixed_t, both(attn_low, grid), gains_t, unit, extra
        )

    grad_second, down_low, gain_second_1, down_t = norm_part(1, cotangent[0])
    pieces = matrix_terms(down_t, right[1], unit)
    grad_second, down_low, pieces = lax.optimization_barrier((grad_second, down_low, pieces))
    down_1 = Reduction(pieces, grid, unit)

    def work(values):
        grad, up_low = up_part(1, *values)
        return (grad, matrix_terms(left[1][2], both(up_low, grid), unit))

    grad, pieces = segments.run([down_1], [], work, (grad_second, down_low))
    up_1 = Reduction(pieces, grid, unit)

    def work(values):
        return attention_part(1, values)

    attn_low, grad_qkv, grad, gain_first = segments.run([up_1], [], work, grad)

    def work(values):
        return norm_part(0, values)

    grad_second, down_low, gain_second_0, down_t = segments.run([down_1], [], work, grad)

    def work(values):
        return attention_pieces(
            1, attn_low, grad_qkv, gain_first, gain_second_1, (down_t, right[0])
        )

    pieces = segments.run([up_1], [down_1], work, ())
    joined = Reduction(pieces, grid, unit)

    def work(values):
        grad, up_low = up_part(0, *values)
        return (grad, matrix_terms(left[0][2], both(up_low, grid), unit))

    grad, pieces = segments.run([joined], [down_1, up_1], work, (grad_second, down_low))
    up_0 = Reduction(pieces, grid, unit)

    def work(values):
        attn_low, grad_qkv, grad, gain_first = attention_part(0, values)
        return grad, attention_pieces(0, attn_low, grad_qkv, gain_first, gain_second_0)

    grad, pieces = segments.run([], [joined, down_1, up_1], work, grad)
    attention_0 = Reduction(pieces, grid, unit)

    def nothing(values):
        return values

    segments.run([up_0], [up_1], nothing, ())
    segments.run([attention_0], [], nothing, ())
    segments.run([up_0], [joined], nothing, ())
    segments.run([attention_0], [joined, up_0], nothing, ())
    segments.run([], [attention_0, up_0], nothing, ())
    segments.run([], [attention_0, joined, up_0], nothing, ())
    segments.run([], [attention_0], nothing, ())

    width = 4 * D + PAD
    middle, down_0 = joined.result()[:, :width], joined.result()[:, width:]
    outputs = [
        (attention_outputs(attention_0.result()), (up_0.result(), down_0.T)),
        (attention_outputs(middle), (up_1.result(), down_1.result().T)),
    ]
    return finish(hidden, grad, outputs)


def solution(mesh):
    placed = (
        P(("dp", "fsdp"), None, None),
        P(("dp", "fsdp")),
        P(None, ("dp", "fsdp"), None),
        P(None, ("dp", "fsdp"), None),
        P(None, ("dp", "fsdp"), None),
        P(None, ("dp", "fsdp"), None),
        P(None, ("dp", "fsdp"), None),
        P(None, None, ("dp", "fsdp")),
        P(None, None, ("dp", "fsdp")),
        P(("dp", "fsdp"), None, None),
    )
    return jax.shard_map(
        functools.partial(per_device, (mesh.shape["dp"], mesh.shape["fsdp"])),
        mesh=mesh,
        in_specs=placed,
        out_specs=(
            P(("dp", "fsdp"), None, None),
            P(("dp", "fsdp"), None, None),
            P(None, ("dp", "fsdp"), None),
            P(None, ("dp", "fsdp"), None),
            P(None, ("dp", "fsdp"), None),
            P(None, ("dp", "fsdp"), None),
            P(None, ("dp", "fsdp"), None),
            P(None, None, ("dp", "fsdp")),
            P(None, None, ("dp", "fsdp")),
        ),
        check_vma=False,
    )
```

```python
import functools

import jax
import jax.numpy as jnp
from jax import lax
from jax.experimental import pallas as pl
from jax.experimental.pallas import tpu as pltpu
import numpy as np
from jax.sharding import PartitionSpec as P

D = 768
HEADS = 12
HEAD_DIM = 64
FF = 3072
LAYERS = 2
PAD = 128
LIGHT = pl.CostEstimate(flops=1 << 20, bytes_accessed=1 << 16, transcendentals=0)


def norm(value, gain):
    centred = value - jnp.mean(value, axis=-1, keepdims=True)
    spread = jnp.mean(centred * centred, axis=-1, keepdims=True)
    return centred * lax.rsqrt(spread + 1e-05) * gain


def gelu_tanh(value):
    return jax.nn.gelu(value, approximate=True)


def product(left, right):
    return jnp.dot(left, right, preferred_element_type=jnp.float32)


def product_left_t(left, right):
    return lax.dot_general(
        left, right, (((0,), (0,)), ((), ())), preferred_element_type=jnp.float32
    )


def product_right_t(left, right):
    return lax.dot_general(
        left, right, (((1,), (1,)), ((), ())), preferred_element_type=jnp.float32
    )


def pack_attention(shards, layer):
    query_w, key_w, value_w, out_w, _, _, gains = (member[layer] for member in shards)
    gain_columns = jnp.pad(gains.T, ((0, 0), (0, PAD - 2)))
    return jnp.concatenate([query_w, key_w, value_w, out_w, gain_columns], axis=1)


def pack_ffn(shards, layer):
    return jnp.concatenate([shards[4][layer], shards[5][layer].T], axis=1)


def plain_gather(block):
    return lax.all_gather(block, ("dp", "fsdp"), axis=0, tiled=True)


def unpack(attention, ffn):
    return (
        attention[:, : 3 * D],
        attention[:, 3 * D : 4 * D],
        ffn[:, :FF],
        ffn[:, FF:],
        attention[:, 4 * D : 4 * D + 2].T.astype(jnp.float32),
    )


def visible_keys(length, token_count, swap):
    half = token_count // 2
    positions = lax.broadcasted_iota(jnp.int32, (2, half), 0) * half + lax.broadcasted_iota(
        jnp.int32, (2, half), 1
    )
    if swap:
        positions = positions[::-1]
    return positions < length


def split_heads(value):
    return value.reshape(2, value.shape[0] // 2, HEADS, HEAD_DIM)


def paired_heads(query, keys, values, swap):
    query_heads = split_heads(query)
    key_heads = split_heads(keys)
    value_heads = split_heads(values)
    if swap:
        key_heads = key_heads[::-1]
        value_heads = value_heads[::-1]
    return (query_heads, key_heads, value_heads)


def masked_scores(query_heads, key_heads, visible):
    scores = (
        jnp.einsum("bqhd,bkhd->bhqk", query_heads, key_heads, preferred_element_type=jnp.float32)
        * 0.125
    )
    return jnp.where(visible[:, None, None, :], scores, -1e30)


def attend_forward(query, keys, values, visible, swap):
    token_count = query.shape[0]
    query_heads, key_heads, value_heads = paired_heads(query, keys, values, swap)
    scores = masked_scores(query_heads, key_heads, visible)
    highest = jnp.max(scores, axis=-1, keepdims=True)
    raised = jnp.exp(scores - highest)
    total = jnp.sum(raised, axis=-1, keepdims=True)
    shares = (raised / total).astype(jnp.bfloat16)
    mixed = jnp.einsum("bhqk,bkhd->bqhd", shares, value_heads, preferred_element_type=jnp.float32)
    return (mixed.reshape(token_count, -1), highest + jnp.log(total))


def attend_backward(query, keys, values, visible, swap, log_total, grad_mixed):
    token_count = query.shape[0]
    query_heads, key_heads, value_heads = paired_heads(query, keys, values, swap)
    scores = masked_scores(query_heads, key_heads, visible)
    shares = jnp.exp(scores - log_total)
    shares_low = shares.astype(jnp.bfloat16)
    grad_heads = split_heads(grad_mixed)
    grad_values = jnp.einsum(
        "bhqk,bqhd->bkhd", shares_low, grad_heads, preferred_element_type=jnp.float32
    )
    grad_shares = jnp.einsum(
        "bqhd,bkhd->bhqk", grad_heads, value_heads, preferred_element_type=jnp.float32
    )
    inner = jnp.sum(shares * grad_shares, axis=-1, keepdims=True)
    grad_scores = (shares * (grad_shares - inner)).astype(jnp.bfloat16)
    grad_query = (
        jnp.einsum("bhqk,bkhd->bqhd", grad_scores, key_heads, preferred_element_type=jnp.float32)
        * 0.125
    )
    grad_keys = (
        jnp.einsum("bhqk,bqhd->bkhd", grad_scores, query_heads, preferred_element_type=jnp.float32)
        * 0.125
    )
    if swap:
        grad_keys = grad_keys[::-1]
        grad_values = grad_values[::-1]
    return tuple(
        (
            member.reshape(token_count, -1).astype(jnp.bfloat16)
            for member in (grad_query, grad_keys, grad_values)
        )
    )


def layer_forward(hidden, length, weights, swap):
    qkv_w, out_w, up_w, down_t, gains = weights
    inputs_low = hidden.astype(jnp.bfloat16)
    qkv = product(inputs_low, qkv_w).astype(jnp.bfloat16)
    query, keys, values = qkv[:, :D], qkv[:, D : 2 * D], qkv[:, 2 * D :]
    visible = visible_keys(length, hidden.shape[0], swap)
    mixed, log_total = attend_forward(query, keys, values, visible, swap)
    mixed_low = mixed.astype(jnp.bfloat16)
    first_sum = hidden + product(mixed_low, out_w)
    normed = norm(first_sum, gains[0])
    normed_low = normed.astype(jnp.bfloat16)
    expanded = product(normed_low, up_w)
    activated = gelu_tanh(expanded).astype(jnp.bfloat16)
    second_sum = normed + product_right_t(activated, down_t)
    output = norm(second_sum, gains[1])
    kept = (
        inputs_low,
        query,
        keys,
        values,
        log_total,
        mixed_low,
        first_sum,
        normed_low,
        expanded,
        activated,
        second_sum,
    )
    return (output, kept)


def down_backward(grad_output, kept, weights):
    grad_second, grad_gain = jax.vjp(norm, kept[10], weights[4][1])[1](grad_output)
    return (grad_second, grad_second.astype(jnp.bfloat16), grad_gain)


def up_backward(grad_second, down_low, kept, weights):
    grad_active = product(down_low, weights[3])
    up_low = jax.vjp(gelu_tanh, kept[8])[1](grad_active)[0].astype(jnp.bfloat16)
    return (grad_second + product_right_t(up_low, weights[2]), up_low)


def mixed_backward(grad_normed, kept, weights):
    grad_first, grad_gain = jax.vjp(norm, kept[6], weights[4][0])[1](grad_normed)
    attn_low = grad_first.astype(jnp.bfloat16)
    grad_mixed = product_right_t(attn_low, weights[1]).astype(jnp.bfloat16)
    return (grad_first, attn_low, grad_mixed, grad_gain)


def scores_backward(grad_mixed, kept, swapped, length):
    query, keys, values, log_total = kept[1:5]
    visible = visible_keys(length, query.shape[0], swapped)
    return jnp.concatenate(
        attend_backward(query, keys, values, visible, swapped, log_total, grad_mixed), axis=1
    )


def inputs_backward(grad_first, grad_qkv, weights):
    return grad_first + product_right_t(grad_qkv, weights[0])


def plain_scatter(terms):
    return lax.psum_scatter(
        terms.astype(jnp.bfloat16), ("dp", "fsdp"), scatter_dimension=0, tiled=True
    ).astype(jnp.float32)


def plain_ffn_terms(operands):
    normed_low, up_low, down_low, activated = operands
    return jnp.concatenate(
        [
            product_left_t(normed_low, up_low).astype(jnp.bfloat16),
            product_left_t(down_low, activated).astype(jnp.bfloat16),
        ],
        axis=1,
    )


def plain_attention_terms(operands, gains):
    inputs_low, grad_qkv, mixed_low, attn_low = operands
    return jnp.concatenate(
        [
            product_left_t(inputs_low, grad_qkv).astype(jnp.bfloat16),
            product_left_t(mixed_low, attn_low).astype(jnp.bfloat16),
            jnp.pad(gains.T, ((0, 0), (0, PAD - 2))).astype(jnp.bfloat16),
        ],
        axis=1,
    )


def attention_outputs(summed):
    return (
        *(summed[:, j * D : (j + 1) * D] for j in range(4)),
        summed[:, 4 * D : 4 * D + 2].T,
    )


def ffn_outputs(summed):
    return (summed[:, :FF], summed[:, FF:].T)


class Grid:
    def __init__(self):
        places = [
            (x, core, z, y) for x in range(2) for core in range(2) for z in range(4) for y in range(2)
        ]
        number = {place: index for index, place in enumerate(places)}

        def route(move, senders=range(4)):
            return [
                (number[place], number[move(*place)]) for place in places if place[2] in senders
            ]

        self.core = route(lambda x, core, z, y: (x, 1 - core, z, y))
        self.along_x = route(lambda x, core, z, y: (1 - x, core, z, y))
        self.along_y = route(lambda x, core, z, y: (x, core, z, 1 - y))
        self.pair = route(lambda x, core, z, y: (x, core, z ^ 1, y))
        self.middle = route(lambda x, core, z, y: (x, core, 3 - z, y), (1, 2))
        self.outward = route(lambda x, core, z, y: (x, core, z ^ 1, y), (1, 2))
        self.inward = route(lambda x, core, z, y: (x, core, z ^ 1, y), (0, 3))


def swap(value, route):
    return lax.ppermute(value, ("dp", "fsdp"), route)


SLOTS = np.array([(dx, dy, s) for dx, dy in ((1, 1), (1, 0), (0, 1), (0, 0)) for s in range(4)])


def row_order(unit):
    dp, fsdp = lax.axis_index("dp"), lax.axis_index("fsdp")
    x, core, z, y = dp // 2, dp % 2, fsdp // 2, fsdp % 2
    dx, dy, s = (jnp.asarray(np.repeat(SLOTS[:, j], unit), jnp.int32) for j in range(3))
    offset = jnp.asarray(np.tile(np.arange(unit), 16), jnp.int32)
    place = jnp.where(s < 2, z ^ s, jnp.where(z < 2, s, 3 - s))
    rows = jnp.concatenate(
        [
            ((((x ^ dx) * 2 + owner) * 4 + place) * 2 + (y ^ dy)) * unit + offset
            for owner in (core, 1 - core)
        ]
    )
    natural = lax.broadcasted_iota(jnp.int32, (32 * unit, 32 * unit), 0)
    return (natural == rows[None]).astype(jnp.bfloat16)


def share_left(values, order):
    lengths = [max(value.shape[0], PAD) for value in values]
    half = D // 2

    def body(order_ref, *refs):
        for j, value_ref in enumerate(refs[: len(values)]):
            ordered = dot(value_ref[...].astype(jnp.bfloat16), order_ref[...])
            short = lengths[j] - ordered.shape[0]
            if short:
                ordered = jnp.concatenate([ordered, jnp.zeros((short, D), jnp.float32)], axis=0)
            turned = ordered.T.astype(jnp.bfloat16)
            refs[len(values) + 2 * j][...] = turned[:half]
            refs[len(values) + 2 * j + 1][...] = turned[half:]

    turned = pl.pallas_call(
        body,
        in_specs=[VMEM_SPEC] * (1 + len(values)),
        out_specs=[VMEM_SPEC] * (2 * len(values)),
        out_shape=shapes(*(((half, n), jnp.bfloat16) for n in lengths for _ in range(2))),
        cost_estimate=LIGHT,
        compiler_params=params(8),
    )(order, *values)
    return [(turned[2 * j], turned[2 * j + 1]) for j in range(len(values))]


def both(value, grid):
    return (value, swap(value, grid.core))


def traded(pair, grid):
    return (pair[0], swap(pair[1], grid.core))


ROWS = ((0, 2), (2, 4), (4, 8), (8, 12), (12, 16))


def dot(left, right):
    return jnp.dot(left, right, preferred_element_type=jnp.float32)


def dot_nt(left, right):
    return lax.dot_general(
        left, right, (((1,), (1,)), ((), ())), preferred_element_type=jnp.float32
    )


def dot_tn(left, right):
    return lax.dot_general(
        left, right, (((0,), (0,)), ((), ())), preferred_element_type=jnp.float32
    )


def lane_masks():
    lane = lax.broadcasted_iota(jnp.int32, (1, 2 * HEAD_DIM), 1)
    first = (lane < HEAD_DIM).astype(jnp.float32)
    return first.astype(jnp.bfloat16), (1.0 - first).astype(jnp.bfloat16), lane < HEAD_DIM


def two_heads(value, masks):
    return jnp.concatenate([value * masks[0], value * masks[1]], axis=0)


def pair_softmax(query_pair, keys, key_block, length):
    half = keys.shape[0]
    scores = dot_nt(query_pair, keys) * 0.125
    position = lax.broadcasted_iota(jnp.int32, scores.shape, 1) + key_block * half
    scores = jnp.where(position < length, scores, -1e30)
    raised = jnp.exp(scores - jnp.max(scores, axis=-1, keepdims=True))
    return raised / jnp.sum(raised, axis=-1, keepdims=True)


def normalised(value):
    centred = value - jnp.mean(value, axis=-1, keepdims=True)
    rate = lax.rsqrt(jnp.mean(centred * centred, axis=-1, keepdims=True) + 1e-05)
    return centred * rate, rate


def norm_backward(value, gain, grad):
    ratio, rate = normalised(value)
    scaled = grad * gain
    slope = jnp.mean(scaled * ratio, axis=-1, keepdims=True)
    result = rate * (scaled - jnp.mean(scaled, axis=-1, keepdims=True) - ratio * slope)
    return result, jnp.sum(grad * ratio, axis=0, keepdims=True)


def head_parts(half, swapped):
    for block in range(2):
        key_block = 1 - block if swapped else block
        rows = slice(block * half, (block + 1) * half)
        key_rows = slice(key_block * half, (key_block + 1) * half)
        for pair in range(HEADS // 2):
            yield key_block, rows, key_rows, pair * 2 * HEAD_DIM


VMEM_SPEC = pl.BlockSpec(memory_space=pltpu.VMEM)
SMEM_SPEC = pl.BlockSpec(memory_space=pltpu.SMEM)
ANY_SPEC = pl.BlockSpec(memory_space=pl.ANY)


def params(mebibytes):
    return pltpu.CompilerParams(vmem_limit_bytes=mebibytes << 20)


def shapes(*pairs):
    return [jax.ShapeDtypeStruct(shape, dtype) for shape, dtype in pairs]


def attention_columns(weights, start, target, sems):
    copies = []
    for part in range(5):
        width = D if part < 4 else PAD
        copies.append(
            pltpu.make_async_copy(
                weights.at[:, pl.ds(start + part * D, width)],
                target.at[:, pl.ds(part * D, width)],
                sems.at[part],
            )
        )
    for copy in copies:
        copy.start()
    return copies


def attention_forward(hidden, lengths, weights, start, swapped):
    tokens = hidden.shape[0]
    half = tokens // 2
    low = jnp.bfloat16

    def body(length_ref, hidden_ref, w_any, low_out, qkv, mixed, first_sum, gains, w, sems):
        copies = attention_columns(w_any, start, w, sems)
        value = hidden_ref[...].astype(low)
        low_out[...] = value
        masks = lane_masks()
        for part in range(3):
            copies[part].wait()
            columns = slice(part * D, (part + 1) * D)
            qkv[:, columns] = dot(value, w[:, columns]).astype(low)
        for key_block, rows, key_rows, lane in head_parts(half, swapped):
            query = two_heads(qkv[rows, lane : lane + 128], masks)
            keys = qkv[key_rows, D + lane : D + lane + 128]
            values = qkv[key_rows, 2 * D + lane : 2 * D + lane + 128]
            shares = pair_softmax(query, keys, key_block, length_ref[0]).astype(low)
            out = dot(shares, values)
            mixed[rows, lane : lane + 128] = jnp.where(masks[2], out[:half], out[half:]).astype(low)
        copies[3].wait()
        first_sum[...] = hidden_ref[...] + dot(mixed[...], w[:, 3 * D : 4 * D])
        copies[4].wait()
        gains[...] = w[:, 4 * D :].astype(jnp.float32).T[:8]

    return pl.pallas_call(
        body,
        in_specs=[SMEM_SPEC, VMEM_SPEC, ANY_SPEC],
        out_specs=[VMEM_SPEC] * 5,
        out_shape=shapes(
            ((tokens, D), low),
            ((tokens, 3 * D), low),
            ((tokens, D), low),
            ((tokens, D), jnp.float32),
            ((8, D), jnp.float32),
        ),
        scratch_shapes=[pltpu.VMEM((D, 4 * D + PAD), low), pltpu.SemaphoreType.DMA((5,))],
        cost_estimate=LIGHT,
        compiler_params=params(14),
    )(lengths, hidden, weights)


FF_TILE = D


def ffn_forward(first_sum, gains, weights, start):
    tokens = first_sum.shape[0]
    low = jnp.bfloat16
    steps = FF // FF_TILE
    first = start // FF_TILE

    def body(sum_ref, gain_ref, up, down, normed_low, activated, slope, second_sum, out, total):
        step = pl.program_id(0)

        @pl.when(step == 0)
        def _():
            normed = normalised(sum_ref[...])[0] * gain_ref[0:1]
            normed_low[...] = normed.astype(low)
            total[...] = normed

        u = dot(normed_low[...], up[...])
        inner = 0.7978845608028654 * (u + 0.044715 * (u * u * u))
        wave = jnp.tanh(inner)
        active = (0.5 * u * (1.0 + wave)).astype(low)
        slope[...] = (
            0.5 * (1.0 + wave)
            + 0.5 * u * (1.0 - wave * wave) * (0.7978845608028654 * (1.0 + 0.134145 * (u * u)))
        ).astype(low)
        activated[...] = active
        total[...] += dot_nt(active, down[...])

        @pl.when(step == steps - 1)
        def _():
            second_sum[...] = total[...]
            out[...] = normalised(total[...])[0] * gain_ref[1:2]

    def fixed(shape):
        return pl.BlockSpec(shape, lambda j: (0, 0))

    wide = pl.BlockSpec((tokens, FF_TILE), lambda j: (0, j))
    return pl.pallas_call(
        body,
        grid=(steps,),
        in_specs=[
            fixed((tokens, D)),
            fixed((8, D)),
            pl.BlockSpec((D, FF_TILE), lambda j: (0, first + j)),
            pl.BlockSpec((D, FF_TILE), lambda j: (0, first + steps + j)),
        ],
        out_specs=[fixed((tokens, D)), wide, wide, fixed((tokens, D)), fixed((tokens, D))],
        out_shape=shapes(
            ((tokens, D), low),
            ((tokens, FF), low),
            ((tokens, FF), low),
            ((tokens, D), jnp.float32),
            ((tokens, D), jnp.float32),
        ),
        scratch_shapes=[pltpu.VMEM((tokens, D), jnp.float32)],
        cost_estimate=LIGHT,
        compiler_params=params(16),
    )(first_sum, gains, weights, weights)


def second_norm_backward(grad, second_sum, gains):
    tokens = grad.shape[0]

    def body(grad_ref, sum_ref, gain_ref, out, low_out, gain_out):
        result, gain_grad = norm_backward(sum_ref[...], gain_ref[1:2], grad_ref[...].astype(jnp.float32))
        out[...] = result
        low_out[...] = result.astype(jnp.bfloat16)
        gain_out[...] = gain_grad

    return pl.pallas_call(
        body,
        in_specs=[VMEM_SPEC] * 3,
        out_specs=[VMEM_SPEC] * 3,
        out_shape=shapes(
            ((tokens, D), jnp.float32), ((tokens, D), jnp.bfloat16), ((1, D), jnp.float32)
        ),
        cost_estimate=LIGHT,
        compiler_params=params(6),
    )(grad, second_sum, gains)


def up_backward_kernel(grad_second, down_low, slope, weights, start):
    tokens = grad_second.shape[0]
    low = jnp.bfloat16
    steps = FF // FF_TILE
    first = start // FF_TILE

    def body(grad_ref, low_ref, slope_ref, up, down, up_low, out):
        step = pl.program_id(0)

        @pl.when(step == 0)
        def _():
            out[...] = grad_ref[...]

        piece = (dot(low_ref[...], down[...]) * slope_ref[...].astype(jnp.float32)).astype(low)
        up_low[...] = piece
        out[...] += dot_nt(piece, up[...])

    def fixed(shape):
        return pl.BlockSpec(shape, lambda j: (0, 0))

    wide = pl.BlockSpec((tokens, FF_TILE), lambda j: (0, j))
    return pl.pallas_call(
        body,
        grid=(steps,),
        in_specs=[
            fixed((tokens, D)),
            fixed((tokens, D)),
            wide,
            pl.BlockSpec((D, FF_TILE), lambda j: (0, first + j)),
            pl.BlockSpec((D, FF_TILE), lambda j: (0, first + steps + j)),
        ],
        out_specs=[wide, fixed((tokens, D))],
        out_shape=shapes(((tokens, FF), low), ((tokens, D), jnp.float32)),
        cost_estimate=LIGHT,
        compiler_params=params(12),
    )(grad_second, down_low, slope, weights, weights)


def attention_backward_kernel(grad, first_sum, gains, qkv, lengths, weights, start, swapped):
    tokens = grad.shape[0]
    half = tokens // 2
    low = jnp.bfloat16

    def body(length_ref, grad_ref, sum_ref, gain_ref, qkv_ref, w_any, *rest):
        attn_low, grad_qkv, grad_in, gain_out, grad_mixed, w, sems = rest
        copies = attention_columns(w_any, start, w, sems)
        masks = lane_masks()
        result, gain_grad = norm_backward(sum_ref[...], gain_ref[0:1], grad_ref[...])
        grad_in[...] = result
        attn_low[...] = result.astype(low)
        gain_out[...] = gain_grad
        copies[3].wait()
        grad_mixed[...] = dot_nt(attn_low[...], w[:, 3 * D : 4 * D]).astype(low)
        for key_block, rows, key_rows, lane in head_parts(half, swapped):
            query = two_heads(qkv_ref[rows, lane : lane + 128], masks)
            keys = qkv_ref[key_rows, D + lane : D + lane + 128]
            values = qkv_ref[key_rows, 2 * D + lane : 2 * D + lane + 128]
            arriving = two_heads(grad_mixed[rows, lane : lane + 128], masks)
            shares = pair_softmax(query, keys, key_block, length_ref[0])
            grad_values = dot_tn(shares.astype(low), arriving)
            grad_shares = dot_nt(arriving, values)
            inner = jnp.sum(shares * grad_shares, axis=-1, keepdims=True)
            grad_scores = (shares * (grad_shares - inner)).astype(low)
            grad_query = dot(grad_scores, keys) * 0.125
            grad_keys = dot_tn(grad_scores, query) * 0.125
            grad_qkv[rows, lane : lane + 128] = jnp.where(
                masks[2], grad_query[:half], grad_query[half:]
            ).astype(low)
            grad_qkv[key_rows, D + lane : D + lane + 128] = grad_keys.astype(low)
            grad_qkv[key_rows, 2 * D + lane : 2 * D + lane + 128] = grad_values.astype(low)
        for part in (0, 1, 2):
            copies[part].wait()
            columns = slice(part * D, (part + 1) * D)
            grad_in[...] += dot_nt(grad_qkv[:, columns], w[:, columns])
        copies[4].wait()

    return pl.pallas_call(
        body,
        in_specs=[SMEM_SPEC] + [VMEM_SPEC] * 4 + [ANY_SPEC],
        out_specs=[VMEM_SPEC] * 4,
        out_shape=shapes(
            ((tokens, D), low),
            ((tokens, 3 * D), low),
            ((tokens, D), jnp.float32),
            ((1, D), jnp.float32),
        ),
        scratch_shapes=[
            pltpu.VMEM((tokens, D), low),
            pltpu.VMEM((D, 4 * D + PAD), low),
            pltpu.SemaphoreType.DMA((5,)),
        ],
        cost_estimate=LIGHT,
        compiler_params=params(16),
    )(lengths, grad, first_sum, gains, qkv, weights)


def matrix_terms(products, unit):
    tile = D
    tokens, width = products[0][1][0].shape
    steps = width // tile

    def body(*refs):
        outs = refs[4 * len(products) :]
        for j in range(len(products)):
            la, lb, ra, rb = refs[4 * j : 4 * j + 4]

            @pl.when(pl.program_id(0) // steps == j)
            def _(la=la, lb=lb, ra=ra, rb=rb):
                value = (dot(la[...], ra[...]) + dot(lb[...], rb[...])).astype(jnp.bfloat16)
                for (low, high), out in zip(ROWS, outs):
                    out[...] = value[low * unit : high * unit]

    in_specs, operands = [], []
    for j, (left, right) in enumerate(products):
        whole = pl.BlockSpec(left[0].shape, lambda i: (0, 0))
        column = pl.BlockSpec(
            (tokens, tile), lambda i, j=j: (0, jnp.clip(i - j * steps, 0, steps - 1))
        )
        in_specs += [whole, whole, column, column]
        operands += [*left, *right]
    wide = width * len(products)
    return pl.pallas_call(
        body,
        grid=(wide // tile,),
        in_specs=in_specs,
        out_specs=[pl.BlockSpec(((b - a) * unit, tile), lambda i: (0, i)) for a, b in ROWS],
        out_shape=shapes(*((((b - a) * unit, wide), jnp.bfloat16) for a, b in ROWS)),
        cost_estimate=LIGHT,
        compiler_params=params(10),
    )(*operands)


def attention_terms(inputs_t, grad_qkv, mixed_t, attn_low, gains_t, unit):
    def body(ia, ib, qa, qb, ma, mb, oa, ob, ga, gb, *outs):
        def put(value, column):
            value = value.astype(jnp.bfloat16)
            for (low, high), out in zip(ROWS, outs):
                out[:, column : column + value.shape[1]] = value[low * unit : high * unit]

        for j in range(3):
            part = slice(j * D, (j + 1) * D)
            put(dot(ia[...], qa[:, part]) + dot(ib[...], qb[:, part]), j * D)
        put(dot(ma[...], oa[...]) + dot(mb[...], ob[...]), 3 * D)
        put(ga[...].astype(jnp.float32) + gb[...].astype(jnp.float32), 4 * D)

    operands = [*inputs_t, *grad_qkv, *mixed_t, *attn_low, *gains_t]
    return pl.pallas_call(
        body,
        in_specs=[VMEM_SPEC] * len(operands),
        out_specs=[VMEM_SPEC] * 5,
        out_shape=shapes(*((((b - a) * unit, 4 * D + PAD), jnp.bfloat16) for a, b in ROWS)),
        cost_estimate=LIGHT,
        compiler_params=params(12),
    )(*operands)


def add(*values):
    return sum(value.astype(jnp.float32) for value in values)


class Reduction:
    def __init__(self, pieces, grid, unit):
        self.grid, self.unit, self.round = grid, unit, 0
        self.out, self.kept = list(pieces[:2]), list(pieces[2:])

    def state(self):
        return (self.out, self.kept)

    def restore(self, state):
        self.out, self.kept = state

    def send(self):
        grid = self.grid
        routes = (
            (grid.along_x, grid.along_y),
            (grid.along_x, grid.along_y),
            (grid.inward,),
            (grid.middle,),
            (grid.pair,),
        )[self.round]
        self.out = [swap(value, route) for value, route in zip(self.out, routes)]
        self.round += 1

    def prepare(self):
        low, unit, two = jnp.bfloat16, self.unit, 2 * self.unit
        if self.round == 1:
            (from_x, from_y), (to_x, to_y, own) = self.out, self.kept
            to_x = jnp.concatenate([to_x[:two], add(to_x[two:], from_y).astype(low)], axis=0)
            to_y = jnp.concatenate([add(to_y[:two], from_x).astype(low), to_y[two:]], axis=0)
            self.out, self.kept = [to_x, to_y], [own]
        elif self.round == 2:
            (from_x, from_y), (own,) = self.out, self.kept
            self.out = [add(own[two:], from_x[two:], from_y[two:]).astype(low)]
            self.kept = [add(own[:two], from_x[:two], from_y[:two]).astype(low), self.out[0]]
        elif self.round == 3:
            near, far = self.kept
            self.out, self.kept = [add(far, self.out[0]).astype(low)], [near]
        else:
            near = add(self.kept[0], self.out[0])
            self.out, self.kept = [near[unit:].astype(low)], [near[:unit]]

    def result(self):
        return add(self.kept[0], self.out[0])


def gate(values, *earlier):
    return lax.optimization_barrier((values, earlier))[0]


class Segments:
    def __init__(self):
        self.active = []

    def run(self, sends, compute=None, values=()):
        for reduction in sends:
            if reduction not in self.active:
                self.active.append(reduction)
            if reduction.round:
                reduction.prepare()
            reduction.send()
        if compute:
            values = compute(*values)
        states = [reduction.state() for reduction in self.active]
        states, values = lax.optimization_barrier((states, values))
        for reduction, state in zip(self.active, states):
            reduction.restore(state)
        self.active = [r for r in self.active if r.round < 5]
        return values


class Gathering:
    def __init__(self, block, grid):
        self.pieces, self.grid, self.unit = [block], grid, block.shape[0]
        self.steps = [self.pair, self.middle, self.outward, self.square, self.diagonal]

    def advance(self):
        self.pieces = list(self.steps.pop(0)(self.pieces, self.grid, 2 * self.unit))

    @staticmethod
    def pair(pieces, grid, two):
        (block,) = pieces
        return (jnp.concatenate([block, swap(block, grid.pair)], axis=0),)

    @staticmethod
    def middle(pieces, grid, two):
        (near,) = pieces
        return (near, swap(near, grid.middle))

    @staticmethod
    def outward(pieces, grid, two):
        near, far = pieces
        z = lax.axis_index("fsdp") // 2
        far = jnp.where((z == 1) | (z == 2), far, swap(far, grid.outward))
        return (jnp.concatenate([near, far], axis=0),)

    @staticmethod
    def square(pieces, grid, two):
        (line,) = pieces
        return (line, swap(line, grid.along_x), swap(line, grid.along_y))

    @staticmethod
    def diagonal(pieces, grid, two):
        line, from_x, from_y = pieces
        return (
            swap(from_y[:two], grid.along_x),
            swap(from_x[two:], grid.along_y),
            from_x,
            from_y,
            line,
        )

    def result(self):
        pieces = self.pieces
        return place_blocks(pieces + [swap(piece, self.grid.core) for piece in pieces], self.unit)


def place_blocks(pieces, unit):
    width = pieces[0].shape[1]
    dp, fsdp = lax.axis_index("dp"), lax.axis_index("fsdp")
    x, core, z, y = dp // 2, dp % 2, fsdp // 2, fsdp % 2
    dx, dy, s = (jnp.asarray(SLOTS[:, j], jnp.int32) for j in range(3))
    place = jnp.where(s < 2, z ^ s, jnp.where(z < 2, s, 3 - s))
    rows = jnp.concatenate(
        [(((x ^ dx) * 2 + owner) * 4 + place) * 2 + (y ^ dy) for owner in (core, 1 - core)]
    )

    tiles = unit // 8

    def body(rows_ref, *refs):
        sources, target = refs[:10], refs[10]
        for half in range(2):
            for (low, high), source in zip(ROWS, sources[half * 5 : half * 5 + 5]):
                for slot in range(low, high):
                    row = rows_ref[half * 16 + slot] * tiles
                    first = (slot - low) * tiles
                    target[pl.ds(row, tiles)] = source[first : first + tiles]

    placed = pl.pallas_call(
        body,
        in_specs=[pl.BlockSpec(memory_space=pltpu.SMEM)]
        + [pl.BlockSpec(memory_space=pltpu.VMEM)] * 10,
        out_specs=pl.BlockSpec(memory_space=pltpu.VMEM),
        out_shape=jax.ShapeDtypeStruct((32 * tiles, 8, width), jnp.bfloat16),
        cost_estimate=LIGHT,
        compiler_params=params(22),
    )(rows, *(piece.reshape(-1, 8, width) for piece in pieces))
    return placed.reshape(32 * unit, width)


def per_device(
    sizes,
    tokens,
    lengths,
    query_weight,
    key_weight,
    value_weight,
    attn_out_weight,
    up_weight,
    down_weight,
    norm_gains,
    cotangent,
):
    shards = (
        query_weight,
        key_weight,
        value_weight,
        attn_out_weight,
        up_weight,
        down_weight,
        norm_gains,
    )
    if sizes == (4, 8):
        return grid_step(tokens, lengths, shards, cotangent)
    hidden = tokens[0].astype(jnp.float32)
    length = lengths[0]
    weights_all = [
        unpack(plain_gather(pack_attention(shards, j)), plain_gather(pack_ffn(shards, j)))
        for j in range(LAYERS)
    ]
    kept_all = []
    for layer in range(LAYERS):
        hidden, kept = layer_forward(hidden, length, weights_all[layer], layer % 2 == 1)
        kept_all.append(kept)
    grad = cotangent[0].astype(jnp.float32)
    outputs = [None] * LAYERS
    for layer in reversed(range(LAYERS)):
        kept, weights = kept_all[layer], weights_all[layer]
        grad_second, down_low, gain_second = down_backward(grad, kept, weights)
        grad_normed, up_low = up_backward(grad_second, down_low, kept, weights)
        ffn = plain_scatter(plain_ffn_terms((kept[7], up_low, down_low, kept[9])))
        grad_first, attn_low, grad_mixed, gain_first = mixed_backward(grad_normed, kept, weights)
        grad_qkv = scores_backward(grad_mixed, kept, layer % 2 == 1, length)
        grad = inputs_backward(grad_first, grad_qkv, weights)
        gains = jnp.stack([gain_first, gain_second])
        attention = plain_scatter(
            plain_attention_terms((kept[0], grad_qkv, kept[5], attn_low), gains)
        )
        outputs[layer] = (attention_outputs(attention), ffn_outputs(ffn))
    return finish(hidden, grad, outputs)


def finish(hidden, grad, outputs):
    layers = [(*attention[:4], *ffn, attention[4]) for attention, ffn in outputs]
    stacked = tuple((jnp.stack([entry[member] for entry in layers]) for member in range(7)))
    return (hidden.astype(jnp.bfloat16)[None], grad[None], *stacked)


def gather_first_layer(blocks, grid, attend):
    attention, ffn = (Gathering(block, grid) for block in blocks)
    for moves in (
        (attention,),
        (attention, ffn),
        (attention,),
        (attention, ffn),
        (attention, ffn),
    ):
        for gathering in moves:
            gathering.advance()
        attention.pieces, ffn.pieces = lax.optimization_barrier((attention.pieces, ffn.pieces))
    ffn.advance()
    weights = attention.result()
    attended = attend(weights)
    ffn.pieces, attended = lax.optimization_barrier((ffn.pieces, attended))
    ffn.advance()
    return weights, ffn.result(), attended


def grid_step(tokens, lengths, shards, cotangent):
    grid, unit = Grid(), shards[0].shape[1]
    order = row_order(unit)
    hidden = tokens[0].astype(jnp.float32)

    second = plain_gather(
        jnp.concatenate([pack_ffn(shards, 1), pack_attention(shards, 1)], axis=1)
    )

    def attend(weights):
        return attention_forward(hidden, lengths, weights, 0, False)

    attention, ffn, attended = gather_first_layer(
        (pack_attention(shards, 0), pack_ffn(shards, 0)), grid, attend
    )
    attention_at = ((attention, 0, False), (second, 2 * FF, True))
    ffn_at = ((ffn, 0), (second, 0))

    kept, left, right = [], [], []
    for layer in range(LAYERS):
        if layer:
            attended = attention_forward(hidden, lengths, *attention_at[layer])
        inputs_low, qkv, mixed, first_sum, gains = attended
        normed_low, activated, slope, second_sum, hidden = ffn_forward(
            first_sum, gains, *ffn_at[layer]
        )
        kept.append((qkv, first_sum, gains, slope, second_sum))
        left.append(share_left((inputs_low, mixed, normed_low), order))
        right.append(both(activated, grid))

    def norm_part(layer, grad):
        grad_second, down_low, gain_grad = second_norm_backward(
            grad, kept[layer][4], kept[layer][2]
        )
        return grad_second, down_low, gain_grad, share_left((down_low,), order)[0]

    def up_part(layer, grad_second, down_low):
        up_low, grad = up_backward_kernel(grad_second, down_low, kept[layer][3], *ffn_at[layer])
        return grad, up_low

    def attention_part(layer, grad):
        qkv, first_sum, gains = kept[layer][:3]
        attn_low, grad_qkv, grad, gain_first = attention_backward_kernel(
            grad, first_sum, gains, qkv, lengths, *attention_at[layer]
        )
        return grad, grad_qkv, attn_low, gain_first

    def attention_pieces(layer, grad_qkv, attn_low, gain_first, gain_second):
        gains = jnp.concatenate([gain_first, gain_second, jnp.zeros((6, D), jnp.float32)], axis=0)
        inputs_t, mixed_t, gains_t = (
            traded(pair, grid) for pair in (*left[layer][:2], share_left((gains,), order)[0])
        )
        return attention_terms(
            inputs_t, both(grad_qkv, grid), mixed_t, both(attn_low, grid), gains_t, unit
        )

    def up_product(layer, up_low):
        return traded(left[layer][2], grid), both(up_low, grid)

    segments = Segments()
    grad_second, down_low, gain_second, down_t = norm_part(1, cotangent[0])
    pieces = matrix_terms([(traded(down_t, grid), right[1])], unit)
    grad_second, down_low, pieces = lax.optimization_barrier((grad_second, down_low, pieces))
    down_1 = Reduction(pieces, grid, unit)

    def work(grad_second, down_low):
        return up_part(1, grad_second, down_low)

    grad, up_low = segments.run([down_1], work, (grad_second, down_low))

    def work(grad, up_low):
        return attention_part(1, grad), matrix_terms([up_product(1, up_low)], unit)

    (grad, *rest), pieces = segments.run([down_1], work, (grad, up_low))
    up_1 = Reduction(pieces, grid, unit)

    def work(grad, *rest):
        return norm_part(0, grad), attention_pieces(1, *rest, gain_second)

    (grad_second, down_low, gain_second_0, down_t), pieces = segments.run(
        [up_1, down_1], work, (grad, *rest)
    )
    attention_1 = Reduction(pieces, grid, unit)

    def work(grad_second, down_low):
        return up_part(0, grad_second, down_low)

    grad, up_low = segments.run([up_1, down_1], work, (grad_second, down_low))

    def work(up_low, down_t):
        return matrix_terms([(traded(down_t, grid), right[0]), up_product(0, up_low)], unit)

    pieces = segments.run([attention_1, down_1, up_1], work, (up_low, down_t))
    ffn_0 = Reduction(pieces, grid, unit)

    def work(grad):
        return attention_part(0, grad)

    grad, *rest = segments.run([attention_1, up_1], work, (grad,))

    def work(*rest):
        return attention_pieces(0, *rest, gain_second_0)

    pieces = segments.run([ffn_0, up_1, attention_1], work, rest)
    attention_0 = Reduction(pieces, grid, unit)
    segments.run([ffn_0, attention_1])
    segments.run([attention_0, attention_1])
    segments.run([attention_0, ffn_0])
    segments.run([attention_0, ffn_0])
    segments.run([attention_0, ffn_0])
    segments.run([attention_0])

    summed = ffn_0.result()
    outputs = [
        (attention_outputs(attention_0.result()), (summed[:, FF:], summed[:, :FF].T)),
        (attention_outputs(attention_1.result()), (up_1.result(), down_1.result().T)),
    ]
    return finish(hidden, grad, outputs)


def solution(mesh):
    placed = (
        P(("dp", "fsdp"), None, None),
        P(("dp", "fsdp")),
        P(None, ("dp", "fsdp"), None),
        P(None, ("dp", "fsdp"), None),
        P(None, ("dp", "fsdp"), None),
        P(None, ("dp", "fsdp"), None),
        P(None, ("dp", "fsdp"), None),
        P(None, None, ("dp", "fsdp")),
        P(None, None, ("dp", "fsdp")),
        P(("dp", "fsdp"), None, None),
    )
    return jax.shard_map(
        functools.partial(per_device, (mesh.shape["dp"], mesh.shape["fsdp"])),
        mesh=mesh,
        in_specs=placed,
        out_specs=(
            P(("dp", "fsdp"), None, None),
            P(("dp", "fsdp"), None, None),
            P(None, ("dp", "fsdp"), None),
            P(None, ("dp", "fsdp"), None),
            P(None, ("dp", "fsdp"), None),
            P(None, ("dp", "fsdp"), None),
            P(None, ("dp", "fsdp"), None),
            P(None, None, ("dp", "fsdp")),
            P(None, None, ("dp", "fsdp")),
        ),
        check_vma=False,
    )
```

```python
import functools

import jax
import jax.numpy as jnp
from jax import lax
from jax.experimental import pallas as pl
from jax.experimental.pallas import tpu as pltpu
import numpy as np
from jax.sharding import PartitionSpec as P

D = 768
HEADS = 12
HEAD_DIM = 64
FF = 3072
LAYERS = 2
PAD = 128
LIGHT = pl.CostEstimate(flops=1 << 20, bytes_accessed=1 << 16, transcendentals=0)


def norm(value, gain):
    centred = value - jnp.mean(value, axis=-1, keepdims=True)
    spread = jnp.mean(centred * centred, axis=-1, keepdims=True)
    return centred * lax.rsqrt(spread + 1e-05) * gain


def gelu_tanh(value):
    return jax.nn.gelu(value, approximate=True)


def product(left, right):
    return jnp.dot(left, right, preferred_element_type=jnp.float32)


def product_left_t(left, right):
    return lax.dot_general(
        left, right, (((0,), (0,)), ((), ())), preferred_element_type=jnp.float32
    )


def product_right_t(left, right):
    return lax.dot_general(
        left, right, (((1,), (1,)), ((), ())), preferred_element_type=jnp.float32
    )


def pack_attention(shards, layer):
    query_w, key_w, value_w, out_w, _, _, gains = (member[layer] for member in shards)
    gain_columns = jnp.pad(gains.T, ((0, 0), (0, PAD - 2)))
    return jnp.concatenate([query_w, key_w, value_w, out_w, gain_columns], axis=1)


def pack_ffn(shards, layer):
    return jnp.concatenate([shards[4][layer], shards[5][layer].T], axis=1)


def plain_gather(block):
    return lax.all_gather(block, ("dp", "fsdp"), axis=0, tiled=True)


def unpack(attention, ffn):
    return (
        attention[:, : 3 * D],
        attention[:, 3 * D : 4 * D],
        ffn[:, :FF],
        ffn[:, FF:],
        attention[:, 4 * D : 4 * D + 2].T.astype(jnp.float32),
    )


def visible_keys(length, token_count, swap):
    half = token_count // 2
    positions = lax.broadcasted_iota(jnp.int32, (2, half), 0) * half + lax.broadcasted_iota(
        jnp.int32, (2, half), 1
    )
    if swap:
        positions = positions[::-1]
    return positions < length


def split_heads(value):
    return value.reshape(2, value.shape[0] // 2, HEADS, HEAD_DIM)


def paired_heads(query, keys, values, swap):
    query_heads = split_heads(query)
    key_heads = split_heads(keys)
    value_heads = split_heads(values)
    if swap:
        key_heads = key_heads[::-1]
        value_heads = value_heads[::-1]
    return (query_heads, key_heads, value_heads)


def masked_scores(query_heads, key_heads, visible):
    scores = (
        jnp.einsum("bqhd,bkhd->bhqk", query_heads, key_heads, preferred_element_type=jnp.float32)
        * 0.125
    )
    return jnp.where(visible[:, None, None, :], scores, -1e30)


def attend_forward(query, keys, values, visible, swap):
    token_count = query.shape[0]
    query_heads, key_heads, value_heads = paired_heads(query, keys, values, swap)
    scores = masked_scores(query_heads, key_heads, visible)
    highest = jnp.max(scores, axis=-1, keepdims=True)
    raised = jnp.exp(scores - highest)
    total = jnp.sum(raised, axis=-1, keepdims=True)
    shares = (raised / total).astype(jnp.bfloat16)
    mixed = jnp.einsum("bhqk,bkhd->bqhd", shares, value_heads, preferred_element_type=jnp.float32)
    return (mixed.reshape(token_count, -1), highest + jnp.log(total))


def attend_backward(query, keys, values, visible, swap, log_total, grad_mixed):
    token_count = query.shape[0]
    query_heads, key_heads, value_heads = paired_heads(query, keys, values, swap)
    scores = masked_scores(query_heads, key_heads, visible)
    shares = jnp.exp(scores - log_total)
    shares_low = shares.astype(jnp.bfloat16)
    grad_heads = split_heads(grad_mixed)
    grad_values = jnp.einsum(
        "bhqk,bqhd->bkhd", shares_low, grad_heads, preferred_element_type=jnp.float32
    )
    grad_shares = jnp.einsum(
        "bqhd,bkhd->bhqk", grad_heads, value_heads, preferred_element_type=jnp.float32
    )
    inner = jnp.sum(shares * grad_shares, axis=-1, keepdims=True)
    grad_scores = (shares * (grad_shares - inner)).astype(jnp.bfloat16)
    grad_query = (
        jnp.einsum("bhqk,bkhd->bqhd", grad_scores, key_heads, preferred_element_type=jnp.float32)
        * 0.125
    )
    grad_keys = (
        jnp.einsum("bhqk,bqhd->bkhd", grad_scores, query_heads, preferred_element_type=jnp.float32)
        * 0.125
    )
    if swap:
        grad_keys = grad_keys[::-1]
        grad_values = grad_values[::-1]
    return tuple(
        (
            member.reshape(token_count, -1).astype(jnp.bfloat16)
            for member in (grad_query, grad_keys, grad_values)
        )
    )


def layer_forward(hidden, length, weights, swap):
    qkv_w, out_w, up_w, down_t, gains = weights
    inputs_low = hidden.astype(jnp.bfloat16)
    qkv = product(inputs_low, qkv_w).astype(jnp.bfloat16)
    query, keys, values = qkv[:, :D], qkv[:, D : 2 * D], qkv[:, 2 * D :]
    visible = visible_keys(length, hidden.shape[0], swap)
    mixed, log_total = attend_forward(query, keys, values, visible, swap)
    mixed_low = mixed.astype(jnp.bfloat16)
    first_sum = hidden + product(mixed_low, out_w)
    normed = norm(first_sum, gains[0])
    normed_low = normed.astype(jnp.bfloat16)
    expanded = product(normed_low, up_w)
    activated = gelu_tanh(expanded).astype(jnp.bfloat16)
    second_sum = normed + product_right_t(activated, down_t)
    output = norm(second_sum, gains[1])
    kept = (
        inputs_low,
        query,
        keys,
        values,
        log_total,
        mixed_low,
        first_sum,
        normed_low,
        expanded,
        activated,
        second_sum,
    )
    return (output, kept)


def down_backward(grad_output, kept, weights):
    grad_second, grad_gain = jax.vjp(norm, kept[10], weights[4][1])[1](grad_output)
    return (grad_second, grad_second.astype(jnp.bfloat16), grad_gain)


def up_backward(grad_second, down_low, kept, weights):
    grad_active = product(down_low, weights[3])
    up_low = jax.vjp(gelu_tanh, kept[8])[1](grad_active)[0].astype(jnp.bfloat16)
    return (grad_second + product_right_t(up_low, weights[2]), up_low)


def mixed_backward(grad_normed, kept, weights):
    grad_first, grad_gain = jax.vjp(norm, kept[6], weights[4][0])[1](grad_normed)
    attn_low = grad_first.astype(jnp.bfloat16)
    grad_mixed = product_right_t(attn_low, weights[1]).astype(jnp.bfloat16)
    return (grad_first, attn_low, grad_mixed, grad_gain)


def scores_backward(grad_mixed, kept, swapped, length):
    query, keys, values, log_total = kept[1:5]
    visible = visible_keys(length, query.shape[0], swapped)
    return jnp.concatenate(
        attend_backward(query, keys, values, visible, swapped, log_total, grad_mixed), axis=1
    )


def inputs_backward(grad_first, grad_qkv, weights):
    return grad_first + product_right_t(grad_qkv, weights[0])


def plain_scatter(terms):
    return lax.psum_scatter(
        terms.astype(jnp.bfloat16), ("dp", "fsdp"), scatter_dimension=0, tiled=True
    ).astype(jnp.float32)


def plain_ffn_terms(operands):
    normed_low, up_low, down_low, activated = operands
    return jnp.concatenate(
        [
            product_left_t(normed_low, up_low).astype(jnp.bfloat16),
            product_left_t(down_low, activated).astype(jnp.bfloat16),
        ],
        axis=1,
    )


def plain_attention_terms(operands, gains):
    inputs_low, grad_qkv, mixed_low, attn_low = operands
    return jnp.concatenate(
        [
            product_left_t(inputs_low, grad_qkv).astype(jnp.bfloat16),
            product_left_t(mixed_low, attn_low).astype(jnp.bfloat16),
            jnp.pad(gains.T, ((0, 0), (0, PAD - 2))).astype(jnp.bfloat16),
        ],
        axis=1,
    )


def attention_outputs(summed):
    return (
        *(summed[:, j * D : (j + 1) * D] for j in range(4)),
        summed[:, 4 * D : 4 * D + 2].T,
    )


def ffn_outputs(summed):
    return (summed[:, :FF], summed[:, FF:].T)


class Grid:
    def __init__(self):
        places = [
            (x, core, z, y) for x in range(2) for core in range(2) for z in range(4) for y in range(2)
        ]
        number = {place: index for index, place in enumerate(places)}

        def route(move, senders=range(4)):
            return [
                (number[place], number[move(*place)]) for place in places if place[2] in senders
            ]

        self.core = route(lambda x, core, z, y: (x, 1 - core, z, y))
        self.first = route(
            lambda x, core, z, y: (x, core, z, 1 - y) if core else (1 - x, core, z, y)
        )
        self.second = route(
            lambda x, core, z, y: (1 - x, core, z, y) if core else (x, core, z, 1 - y)
        )
        self.pair = route(lambda x, core, z, y: (x, core, z ^ 1, y))
        self.middle = route(lambda x, core, z, y: (x, core, 3 - z, y), (1, 2))
        self.outward = route(lambda x, core, z, y: (x, core, z ^ 1, y), (1, 2))
        self.line = [route(lambda x, core, z, y, s=s: (x, core, z ^ s, y)) for s in (1, 2, 3)]


def swap(value, route):
    return lax.ppermute(value, ("dp", "fsdp"), route)


SLOTS = np.array([(far, near, s) for far, near in ((1, 1), (1, 0), (0, 1), (0, 0)) for s in range(4)])
ROWS = ((0, 2), (2, 4), (4, 8), (8, 12), (12, 16))
TERM_SLOTS = SLOTS[[0, 1, 4, 5, 2, 3, 10, 11, 6, 7, 8, 9, 12, 13, 14, 15]]
TERM_ROWS = ((0, 4), (4, 8), (8, 10), (10, 12), (12, 16))


def slot_rows(slots, place, x, y, owner):
    first, second = (jnp.asarray(slots[:, j], jnp.int32) for j in range(2))
    along_x = jnp.where(owner == 0, first, second)
    along_y = jnp.where(owner == 0, second, first)
    return (((x ^ along_x) * 2 + owner) * 4 + place) * 2 + (y ^ along_y)


def row_order(unit):
    dp, fsdp = lax.axis_index("dp"), lax.axis_index("fsdp")
    x, core, z, y = dp // 2, dp % 2, fsdp // 2, fsdp % 2
    slots = np.repeat(TERM_SLOTS, unit, axis=0)
    place = z ^ jnp.asarray(slots[:, 2], jnp.int32)
    offset = jnp.asarray(np.tile(np.arange(unit), 16), jnp.int32)
    rows = jnp.concatenate(
        [slot_rows(slots, place, x, y, owner) * unit + offset for owner in (core, 1 - core)]
    )
    natural = lax.broadcasted_iota(jnp.int32, (32 * unit, 32 * unit), 0)
    return (natural == rows[None]).astype(jnp.bfloat16)


def share_left(values, order):
    lengths = [max(value.shape[0], PAD) for value in values]
    half = D // 2

    def body(order_ref, *refs):
        mine, other = refs[len(values) :]
        start = 0
        for length, value_ref in zip(lengths, refs):
            ordered = dot(value_ref[...].astype(jnp.bfloat16), order_ref[...])
            short = length - ordered.shape[0]
            if short:
                ordered = jnp.concatenate([ordered, jnp.zeros((short, D), jnp.float32)], axis=0)
            turned = ordered.T.astype(jnp.bfloat16)
            mine[:, start : start + length] = turned[:half]
            other[:, start : start + length] = turned[half:]
            start += length

    return pl.pallas_call(
        body,
        in_specs=[VMEM_SPEC] * (1 + len(values)),
        out_specs=[VMEM_SPEC] * 2,
        out_shape=shapes(*[((half, sum(lengths)), jnp.bfloat16)] * 2),
        cost_estimate=LIGHT,
        compiler_params=params(8),
    )(order, *values)


def both(value, grid):
    return (value, swap(value, grid.core))


def traded(pair, grid):
    return (pair[0], swap(pair[1], grid.core))


def dot(left, right):
    return jnp.dot(left, right, preferred_element_type=jnp.float32)


def dot_nt(left, right):
    return lax.dot_general(
        left, right, (((1,), (1,)), ((), ())), preferred_element_type=jnp.float32
    )


def dot_tn(left, right):
    return lax.dot_general(
        left, right, (((0,), (0,)), ((), ())), preferred_element_type=jnp.float32
    )


def lane_masks():
    lane = lax.broadcasted_iota(jnp.int32, (1, 2 * HEAD_DIM), 1)
    first = (lane < HEAD_DIM).astype(jnp.float32)
    return first.astype(jnp.bfloat16), (1.0 - first).astype(jnp.bfloat16), lane < HEAD_DIM


def two_heads(value, masks):
    return jnp.concatenate([value * masks[0], value * masks[1]], axis=0)


def pair_softmax(query_pair, keys, key_block, length):
    scores = dot_nt(keys, query_pair) * 0.125
    position = lax.broadcasted_iota(jnp.int32, scores.shape, 0) + key_block * keys.shape[0]
    scores = jnp.where(position < length, scores, -1e30)
    raised = jnp.exp(scores - jnp.max(scores, axis=0, keepdims=True))
    return raised / jnp.sum(raised, axis=0, keepdims=True)


def normalised(value):
    centred = value - jnp.mean(value, axis=-1, keepdims=True)
    rate = lax.rsqrt(jnp.mean(centred * centred, axis=-1, keepdims=True) + 1e-05)
    return centred * rate, rate


def norm_backward(value, gain, grad):
    ratio, rate = normalised(value)
    scaled = grad * gain
    slope = jnp.mean(scaled * ratio, axis=-1, keepdims=True)
    result = rate * (scaled - jnp.mean(scaled, axis=-1, keepdims=True) - ratio * slope)
    return result, jnp.sum(grad * ratio, axis=0, keepdims=True)


def head_parts(half, swapped):
    for block in range(2):
        key_block = 1 - block if swapped else block
        rows = slice(block * half, (block + 1) * half)
        key_rows = slice(key_block * half, (key_block + 1) * half)
        for pair in range(HEADS // 2):
            yield key_block, rows, key_rows, pair * 2 * HEAD_DIM


VMEM_SPEC = pl.BlockSpec(memory_space=pltpu.VMEM)
SMEM_SPEC = pl.BlockSpec(memory_space=pltpu.SMEM)
ANY_SPEC = pl.BlockSpec(memory_space=pl.ANY)


def params(mebibytes):
    return pltpu.CompilerParams(vmem_limit_bytes=mebibytes << 20)


def shapes(*pairs):
    return [jax.ShapeDtypeStruct(shape, dtype) for shape, dtype in pairs]


def attention_columns(weights, start, target, sems):
    copies = []
    for part in range(5):
        width = D if part < 4 else PAD
        copies.append(
            pltpu.make_async_copy(
                weights.at[:, pl.ds(start + part * D, width)],
                target.at[:, pl.ds(part * D, width)],
                sems.at[part],
            )
        )
    for copy in copies:
        copy.start()
    return copies


def attention_forward(hidden, lengths, weights, start, swapped):
    tokens = hidden.shape[0]
    half = tokens // 2
    low = jnp.bfloat16

    def body(length_ref, hidden_ref, w_any, low_out, qkv, mixed, first_sum, gains, w, sems):
        copies = attention_columns(w_any, start, w, sems)
        value = hidden_ref[...].astype(low)
        low_out[...] = value
        masks = lane_masks()
        for part in range(3):
            copies[part].wait()
            columns = slice(part * D, (part + 1) * D)
            qkv[:, columns] = dot(value, w[:, columns]).astype(low)
        for key_block, rows, key_rows, lane in head_parts(half, swapped):
            query = two_heads(qkv[rows, lane : lane + 128], masks)
            keys = qkv[key_rows, D + lane : D + lane + 128]
            values = qkv[key_rows, 2 * D + lane : 2 * D + lane + 128]
            shares = pair_softmax(query, keys, key_block, length_ref[0]).astype(low)
            out = dot_tn(shares, values)
            mixed[rows, lane : lane + 128] = jnp.where(masks[2], out[:half], out[half:]).astype(low)
        copies[3].wait()
        first_sum[...] = hidden_ref[...] + dot(mixed[...], w[:, 3 * D : 4 * D])
        copies[4].wait()
        gains[...] = w[:, 4 * D :].astype(jnp.float32).T[:8]

    return pl.pallas_call(
        body,
        in_specs=[SMEM_SPEC, VMEM_SPEC, ANY_SPEC],
        out_specs=[VMEM_SPEC] * 5,
        out_shape=shapes(
            ((tokens, D), low),
            ((tokens, 3 * D), low),
            ((tokens, D), low),
            ((tokens, D), jnp.float32),
            ((8, D), jnp.float32),
        ),
        scratch_shapes=[pltpu.VMEM((D, 4 * D + PAD), low), pltpu.SemaphoreType.DMA((5,))],
        cost_estimate=LIGHT,
        compiler_params=params(14),
    )(lengths, hidden, weights)


FF_TILE = D


def ffn_forward(first_sum, gains, weights, start):
    tokens = first_sum.shape[0]
    low = jnp.bfloat16
    steps = FF // FF_TILE
    first = start // FF_TILE

    def body(sum_ref, gain_ref, up, down, normed_low, activated, slope, second_sum, out, total):
        step = pl.program_id(0)

        @pl.when(step == 0)
        def _():
            normed = normalised(sum_ref[...])[0] * gain_ref[0:1]
            normed_low[...] = normed.astype(low)
            total[...] = normed

        u = dot(normed_low[...], up[...])
        inner = 0.7978845608028654 * (u + 0.044715 * (u * u * u))
        wave = jnp.tanh(inner)
        active = (0.5 * u * (1.0 + wave)).astype(low)
        slope[...] = (
            0.5 * (1.0 + wave)
            + 0.5 * u * (1.0 - wave * wave) * (0.7978845608028654 * (1.0 + 0.134145 * (u * u)))
        ).astype(low)
        activated[...] = active
        total[...] += dot_nt(active, down[...])

        @pl.when(step == steps - 1)
        def _():
            second_sum[...] = total[...]
            out[...] = normalised(total[...])[0] * gain_ref[1:2]

    def fixed(shape):
        return pl.BlockSpec(shape, lambda j: (0, 0))

    wide = pl.BlockSpec((tokens, FF_TILE), lambda j: (0, j))
    return pl.pallas_call(
        body,
        grid=(steps,),
        in_specs=[
            fixed((tokens, D)),
            fixed((8, D)),
            pl.BlockSpec((D, FF_TILE), lambda j: (0, first + j)),
            pl.BlockSpec((D, FF_TILE), lambda j: (0, first + steps + j)),
        ],
        out_specs=[fixed((tokens, D)), wide, wide, fixed((tokens, D)), fixed((tokens, D))],
        out_shape=shapes(
            ((tokens, D), low),
            ((tokens, FF), low),
            ((tokens, FF), low),
            ((tokens, D), jnp.float32),
            ((tokens, D), jnp.float32),
        ),
        scratch_shapes=[pltpu.VMEM((tokens, D), jnp.float32)],
        cost_estimate=LIGHT,
        compiler_params=params(16),
    )(first_sum, gains, weights, weights)


def second_norm_backward(grad, second_sum, gains):
    tokens = grad.shape[0]

    def body(grad_ref, sum_ref, gain_ref, out, low_out, gain_out):
        result, gain_grad = norm_backward(sum_ref[...], gain_ref[1:2], grad_ref[...].astype(jnp.float32))
        out[...] = result
        low_out[...] = result.astype(jnp.bfloat16)
        gain_out[...] = gain_grad

    return pl.pallas_call(
        body,
        in_specs=[VMEM_SPEC] * 3,
        out_specs=[VMEM_SPEC] * 3,
        out_shape=shapes(
            ((tokens, D), jnp.float32), ((tokens, D), jnp.bfloat16), ((1, D), jnp.float32)
        ),
        cost_estimate=LIGHT,
        compiler_params=params(6),
    )(grad, second_sum, gains)


def up_backward_kernel(grad_second, down_low, slope, weights, start):
    tokens = grad_second.shape[0]
    low = jnp.bfloat16
    steps = FF // FF_TILE
    first = start // FF_TILE

    def body(grad_ref, low_ref, slope_ref, up, down, up_low, out):
        step = pl.program_id(0)

        @pl.when(step == 0)
        def _():
            out[...] = grad_ref[...]

        piece = (dot(low_ref[...], down[...]) * slope_ref[...].astype(jnp.float32)).astype(low)
        up_low[...] = piece
        out[...] += dot_nt(piece, up[...])

    def fixed(shape):
        return pl.BlockSpec(shape, lambda j: (0, 0))

    wide = pl.BlockSpec((tokens, FF_TILE), lambda j: (0, j))
    return pl.pallas_call(
        body,
        grid=(steps,),
        in_specs=[
            fixed((tokens, D)),
            fixed((tokens, D)),
            wide,
            pl.BlockSpec((D, FF_TILE), lambda j: (0, first + j)),
            pl.BlockSpec((D, FF_TILE), lambda j: (0, first + steps + j)),
        ],
        out_specs=[wide, fixed((tokens, D))],
        out_shape=shapes(((tokens, FF), low), ((tokens, D), jnp.float32)),
        cost_estimate=LIGHT,
        compiler_params=params(12),
    )(grad_second, down_low, slope, weights, weights)


def attention_backward_kernel(grad, first_sum, gains, qkv, lengths, weights, start, swapped):
    tokens = grad.shape[0]
    half = tokens // 2
    low = jnp.bfloat16

    def body(length_ref, grad_ref, sum_ref, gain_ref, qkv_ref, w_any, *rest):
        grads, grad_in, gain_out, grad_mixed, w, sems = rest
        copies = attention_columns(w_any, start, w, sems)
        masks = lane_masks()
        result, gain_grad = norm_backward(sum_ref[...], gain_ref[0:1], grad_ref[...])
        grad_in[...] = result
        grads[:, 3 * D :] = result.astype(low)
        gain_out[...] = gain_grad
        copies[3].wait()
        grad_mixed[...] = dot_nt(grads[:, 3 * D :], w[:, 3 * D : 4 * D]).astype(low)
        for key_block, rows, key_rows, lane in head_parts(half, swapped):
            query = two_heads(qkv_ref[rows, lane : lane + 128], masks)
            keys = qkv_ref[key_rows, D + lane : D + lane + 128]
            values = qkv_ref[key_rows, 2 * D + lane : 2 * D + lane + 128]
            arriving = two_heads(grad_mixed[rows, lane : lane + 128], masks)
            shares = pair_softmax(query, keys, key_block, length_ref[0])
            grad_values = dot(shares.astype(low), arriving)
            grad_shares = dot_nt(values, arriving)
            inner = jnp.sum(shares * grad_shares, axis=0, keepdims=True)
            grad_scores = (shares * (grad_shares - inner)).astype(low)
            grad_query = dot_tn(grad_scores, keys) * 0.125
            grad_keys = dot(grad_scores, query) * 0.125
            grads[rows, lane : lane + 128] = jnp.where(
                masks[2], grad_query[:half], grad_query[half:]
            ).astype(low)
            grads[key_rows, D + lane : D + lane + 128] = grad_keys.astype(low)
            grads[key_rows, 2 * D + lane : 2 * D + lane + 128] = grad_values.astype(low)
        for part in (0, 1, 2):
            copies[part].wait()
            columns = slice(part * D, (part + 1) * D)
            grad_in[...] += dot_nt(grads[:, columns], w[:, columns])
        copies[4].wait()

    return pl.pallas_call(
        body,
        in_specs=[SMEM_SPEC] + [VMEM_SPEC] * 4 + [ANY_SPEC],
        out_specs=[VMEM_SPEC] * 3,
        out_shape=shapes(
            ((tokens, 4 * D), low),
            ((tokens, D), jnp.float32),
            ((1, D), jnp.float32),
        ),
        scratch_shapes=[
            pltpu.VMEM((tokens, D), low),
            pltpu.VMEM((D, 4 * D + PAD), low),
            pltpu.SemaphoreType.DMA((5,)),
        ],
        cost_estimate=LIGHT,
        compiler_params=params(16),
    )(lengths, grad, first_sum, gains, qkv, weights)


def matrix_terms(products, unit):
    tile = D
    tokens, width = products[0][2][0].shape
    steps = width // tile

    def body(*refs):
        outs = refs[starts[-1] :]
        for j in range(len(products)):
            la, lb, ra, *received = refs[starts[j] : starts[j + 1]]
            for step in range(steps if len(received) > 1 else 1):
                rb = received[step]
                place = pl.program_id(0) - j * steps
                here = place == step if len(received) > 1 else place // steps == 0

                @pl.when(here)
                def _(la=la, lb=lb, ra=ra, rb=rb):
                    value = (dot(la[...], ra[...]) + dot(lb[...], rb[...])).astype(jnp.bfloat16)
                    for (low, high), out in zip(TERM_ROWS, outs):
                        out[...] = value[low * unit : high * unit]

    in_specs, operands, starts = [], [], [0]
    for j, (left, part, right) in enumerate(products):
        block = pl.BlockSpec((16 * unit, tokens), lambda i, part=part: (0, part))
        column = pl.BlockSpec(
            (tokens, tile), lambda i, j=j: (0, jnp.clip(i - j * steps, 0, steps - 1))
        )
        own, received = right
        if isinstance(received, list):
            whole = pl.BlockSpec((tokens, tile), lambda i: (0, 0))
            in_specs += [block, block, column] + [whole] * steps
            operands += [*left, own, *received]
        else:
            in_specs += [block, block, column, column]
            operands += [*left, own, received]
        starts.append(len(operands))
    wide = width * len(products)
    return pl.pallas_call(
        body,
        grid=(wide // tile,),
        in_specs=in_specs,
        out_specs=[pl.BlockSpec(((b - a) * unit, tile), lambda i: (0, i)) for a, b in TERM_ROWS],
        out_shape=shapes(*((((b - a) * unit, wide), jnp.bfloat16) for a, b in TERM_ROWS)),
        cost_estimate=LIGHT,
        compiler_params=params(10),
    )(*operands)


def attention_terms(left, grads, gains, start, unit):
    tokens = grads[0].shape[0]

    def body(la, lb, ra, rb, ga, gb, *outs):
        def put(value, column):
            value = value.astype(jnp.bfloat16)
            for (low, high), out in zip(TERM_ROWS, outs):
                out[:, column : column + value.shape[1]] = value[low * unit : high * unit]

        for j in range(4):
            part = slice(j * D, (j + 1) * D)
            from_left = slice(0, tokens) if j < 3 else slice(tokens, 2 * tokens)
            put(
                dot(la[:, from_left], ra[:, part]) + dot(lb[:, from_left], rb[:, part]),
                j * D,
            )
        gain = slice(start, start + PAD)
        put(ga[:, gain].astype(jnp.float32) + gb[:, gain].astype(jnp.float32), 4 * D)

    return pl.pallas_call(
        body,
        in_specs=[VMEM_SPEC] * 6,
        out_specs=[VMEM_SPEC] * 5,
        out_shape=shapes(*((((b - a) * unit, 4 * D + PAD), jnp.bfloat16) for a, b in TERM_ROWS)),
        cost_estimate=LIGHT,
        compiler_params=params(12),
    )(*left, *grads, *gains)


def square_sums(came_first, came_second, later_first, later_second):
    rows, width = later_first.shape

    def body(one, other, first, second, first_out, second_out):
        first_out[...] = add(first[...], other[:rows]).astype(jnp.bfloat16)
        second_out[...] = add(second[...], one[:rows]).astype(jnp.bfloat16)

    return pl.pallas_call(
        body,
        in_specs=[VMEM_SPEC] * 4,
        out_specs=[VMEM_SPEC] * 2,
        out_shape=shapes(*[((rows, width), jnp.bfloat16)] * 2),
        cost_estimate=LIGHT,
        compiler_params=params(8),
    )(came_first, came_second, later_first, later_second)


def line_sums(groups, unit):
    two = 2 * unit
    widths = [group[0].shape[1] for group in groups]

    def body(*refs):
        outs = refs[5 * len(groups) :]
        start = 0
        for j, width in enumerate(widths):
            own, one, other, last_first, last_second = refs[5 * j : 5 * j + 5]
            columns = slice(start, start + width)
            near = add(own[:two], one[two:], last_second[...])
            far = add(own[two:], other[two:], last_first[...])
            outs[0][:, columns] = near[:unit]
            outs[1][:, columns] = near[unit:].astype(jnp.bfloat16)
            outs[2][:, columns] = far[:unit].astype(jnp.bfloat16)
            outs[3][:, columns] = far[unit:].astype(jnp.bfloat16)
            start += width

    low = ((unit, sum(widths)), jnp.bfloat16)
    return pl.pallas_call(
        body,
        in_specs=[VMEM_SPEC] * (5 * len(groups)),
        out_specs=[VMEM_SPEC] * 4,
        out_shape=shapes(((unit, sum(widths)), jnp.float32), low, low, low),
        cost_estimate=LIGHT,
        compiler_params=params(14),
    )(*(value for group in groups for value in group))


def add(*values):
    return sum(value.astype(jnp.float32) for value in values)


class Reduction:
    def __init__(self, pieces, grid, unit):
        self.grid, self.unit, self.round, self.joined = grid, unit, 0, False
        self.out, self.kept = list(pieces[:2]), list(pieces[2:])

    def state(self, pending):
        return ([] if pending else self.out, self.kept)

    def restore(self, state):
        out, self.kept = state
        self.out = out or self.out

    def send(self):
        grid = self.grid
        routes = grid.line if self.round == 2 else (grid.first, grid.second)
        self.out = [swap(value, route) for value, route in zip(self.out, routes)]
        self.round += 1

    def prepare(self):
        if self.round == 1:
            later_first, later_second, own = self.kept
            self.kept = [own, *self.out]
            self.out = list(square_sums(*self.out, later_first, later_second))
        elif not self.joined:
            self.join()

    def join(self, *others):
        groups = [(*reduction.kept, *reduction.out) for reduction in (self, *others)]
        own, *self.out = line_sums(groups, self.unit)
        self.kept, self.joined = [own], True

    def result(self):
        return add(self.kept[0], *self.out)


def gate(values, *earlier):
    return lax.optimization_barrier((values, earlier))[0]


class Segments:
    def __init__(self):
        self.active = []

    def join(self, reduction, *others):
        reduction.join(*others)
        self.active = [r for r in self.active if r not in others]

    def run(self, sends, compute=None, values=(), pending=()):
        for reduction in sends:
            if reduction not in self.active:
                self.active.append(reduction)
            if reduction.round:
                reduction.prepare()
            reduction.send()
        if compute:
            values = compute(*values)
        states = [reduction.state(reduction in pending) for reduction in self.active]
        states, values = lax.optimization_barrier((states, values))
        for reduction, state in zip(self.active, states):
            reduction.restore(state)
        self.active = [r for r in self.active if r.round < 3 or r in pending]
        return values


class Gathering:
    def __init__(self, block, grid):
        self.pieces, self.grid, self.unit = [block], grid, block.shape[0]
        self.steps = [self.pair, self.middle, self.outward, self.square, self.diagonal]

    def advance(self):
        self.pieces = list(self.steps.pop(0)(self.pieces, self.grid, 2 * self.unit))

    @staticmethod
    def pair(pieces, grid, two):
        (block,) = pieces
        return (jnp.concatenate([block, swap(block, grid.pair)], axis=0),)

    @staticmethod
    def middle(pieces, grid, two):
        (near,) = pieces
        return (near, swap(near, grid.middle))

    @staticmethod
    def outward(pieces, grid, two):
        near, far = pieces
        z = lax.axis_index("fsdp") // 2
        far = jnp.where((z == 1) | (z == 2), far, swap(far, grid.outward))
        return (jnp.concatenate([near, far], axis=0),)

    @staticmethod
    def square(pieces, grid, two):
        (line,) = pieces
        return (line, swap(line, grid.first), swap(line, grid.second))

    @staticmethod
    def diagonal(pieces, grid, two):
        line, one, other = pieces
        late = swap(one[two:], grid.second)
        return (swap(other[:two], grid.first), late, one, other, line)

    def result(self):
        pieces = self.pieces
        return place_blocks(pieces + [swap(piece, self.grid.core) for piece in pieces], self.unit)


def place_blocks(pieces, unit):
    width = pieces[0].shape[1]
    dp, fsdp = lax.axis_index("dp"), lax.axis_index("fsdp")
    x, core, z, y = dp // 2, dp % 2, fsdp // 2, fsdp % 2
    s = jnp.asarray(SLOTS[:, 2], jnp.int32)
    place = jnp.where(s < 2, z ^ s, jnp.where(z < 2, s, 3 - s))
    rows = jnp.concatenate([slot_rows(SLOTS, place, x, y, owner) for owner in (core, 1 - core)])
    tiles = unit // 8

    def body(rows_ref, *refs):
        sources, target = refs[:10], refs[10]
        for half in range(2):
            for (low, high), source in zip(ROWS, sources[half * 5 : half * 5 + 5]):
                for slot in range(low, high):
                    row = rows_ref[half * 16 + slot] * tiles
                    first = (slot - low) * tiles
                    target[pl.ds(row, tiles)] = source[first : first + tiles]

    placed = pl.pallas_call(
        body,
        in_specs=[pl.BlockSpec(memory_space=pltpu.SMEM)]
        + [pl.BlockSpec(memory_space=pltpu.VMEM)] * 10,
        out_specs=pl.BlockSpec(memory_space=pltpu.VMEM),
        out_shape=jax.ShapeDtypeStruct((32 * tiles, 8, width), jnp.bfloat16),
        cost_estimate=LIGHT,
        compiler_params=params(22),
    )(rows, *(piece.reshape(-1, 8, width) for piece in pieces))
    return placed.reshape(32 * unit, width)


def per_device(
    sizes,
    tokens,
    lengths,
    query_weight,
    key_weight,
    value_weight,
    attn_out_weight,
    up_weight,
    down_weight,
    norm_gains,
    cotangent,
):
    shards = (
        query_weight,
        key_weight,
        value_weight,
        attn_out_weight,
        up_weight,
        down_weight,
        norm_gains,
    )
    if sizes == (4, 8):
        return grid_step(tokens, lengths, shards, cotangent)
    hidden = tokens[0].astype(jnp.float32)
    length = lengths[0]
    weights_all = [
        unpack(plain_gather(pack_attention(shards, j)), plain_gather(pack_ffn(shards, j)))
        for j in range(LAYERS)
    ]
    kept_all = []
    for layer in range(LAYERS):
        hidden, kept = layer_forward(hidden, length, weights_all[layer], layer % 2 == 1)
        kept_all.append(kept)
    grad = cotangent[0].astype(jnp.float32)
    outputs = [None] * LAYERS
    for layer in reversed(range(LAYERS)):
        kept, weights = kept_all[layer], weights_all[layer]
        grad_second, down_low, gain_second = down_backward(grad, kept, weights)
        grad_normed, up_low = up_backward(grad_second, down_low, kept, weights)
        ffn = plain_scatter(plain_ffn_terms((kept[7], up_low, down_low, kept[9])))
        grad_first, attn_low, grad_mixed, gain_first = mixed_backward(grad_normed, kept, weights)
        grad_qkv = scores_backward(grad_mixed, kept, layer % 2 == 1, length)
        grad = inputs_backward(grad_first, grad_qkv, weights)
        gains = jnp.stack([gain_first, gain_second])
        attention = plain_scatter(
            plain_attention_terms((kept[0], grad_qkv, kept[5], attn_low), gains)
        )
        outputs[layer] = (attention_outputs(attention), ffn_outputs(ffn))
    return finish(hidden, grad, outputs)


def finish(hidden, grad, outputs):
    layers = [(*attention[:4], *ffn, attention[4]) for attention, ffn in outputs]
    stacked = tuple((jnp.stack([entry[member] for entry in layers]) for member in range(7)))
    return (hidden.astype(jnp.bfloat16)[None], grad[None], *stacked)


def gather_first_layer(blocks, second, order, grid, attend):
    attention, ffn = (Gathering(block, grid) for block in blocks)

    def hold(*gatherings):
        pieces = [g.pieces[:2] if len(g.pieces) == 3 else g.pieces for g in gatherings]
        pieces = lax.optimization_barrier(pieces)
        for g, held in zip(gatherings, pieces):
            g.pieces = [*held, *g.pieces[len(held) :]]

    attention.advance()
    hold(attention)
    ffn.pieces = gate(ffn.pieces, attention.pieces)
    attention.advance()
    ffn.advance()
    hold(attention, ffn)
    attention.advance()
    ffn.advance()
    order, ffn.pieces = lax.optimization_barrier((order, ffn.pieces))
    hold(attention, ffn)
    attention.advance()
    ffn.advance()
    hold(attention, ffn)
    attention.advance()
    ffn.pieces = gate(ffn.pieces, attention.pieces[1])
    ffn.advance()
    hold(attention)
    weights = attention.result()
    attended = attend(weights)
    held, attended = lax.optimization_barrier((ffn.pieces[:2], attended))
    ffn.pieces = [*held, *ffn.pieces[2:]]
    ffn.advance()
    pieces, second = lax.optimization_barrier((ffn.pieces, second))
    ffn.pieces = list(pieces)
    return weights, ffn.result(), second, order, attended


def grid_step(tokens, lengths, shards, cotangent):
    grid, unit = Grid(), shards[0].shape[1]
    order = row_order(unit)
    hidden = tokens[0].astype(jnp.float32)

    second = plain_gather(
        jnp.concatenate([pack_ffn(shards, 1), pack_attention(shards, 1)], axis=1)
    )

    def attend(weights):
        return attention_forward(hidden, lengths, weights, 0, False)

    attention, ffn, second, order, attended = gather_first_layer(
        (pack_attention(shards, 0), pack_ffn(shards, 0)), second, order, grid, attend
    )
    attention_at = ((attention, 0, False), (second, 2 * FF, True))
    ffn_at = ((ffn, 0), (second, 0))

    kept, left, right = [], [], []
    for layer in range(LAYERS):
        if layer:
            attended = attention_forward(hidden, lengths, *attention_at[layer])
        inputs_low, qkv, mixed, first_sum, gains = attended
        normed_low, activated, slope, second_sum, hidden = ffn_forward(
            first_sum, gains, *ffn_at[layer]
        )
        kept.append((qkv, first_sum, gains, slope, second_sum))
        left.append(traded(share_left((inputs_low, mixed, normed_low), order), grid))
        right.append(both(activated, grid))

    def norm_part(layer, grad):
        return second_norm_backward(grad, kept[layer][4], kept[layer][2])

    def up_part(layer, grad_second, down_low):
        up_low, grad = up_backward_kernel(grad_second, down_low, kept[layer][3], *ffn_at[layer])
        return grad, up_low

    def attention_part(layer, grad):
        qkv, first_sum, gains = kept[layer][:3]
        return attention_backward_kernel(
            grad, first_sum, gains, qkv, lengths, *attention_at[layer]
        )

    def gain_rows(first, second):
        return jnp.concatenate([first, second, jnp.zeros((6, D), jnp.float32)], axis=0)

    def up_product(layer, up_low):
        return left[layer], 2, both(up_low, grid)

    def up_product_in_tiles(layer, up_low):
        received = [swap(up_low[:, j : j + D], grid.core) for j in range(0, FF, D)]
        return left[layer], 2, (up_low, received)

    segments = Segments()
    grad_second, down_low, gain_second = norm_part(1, cotangent[0])
    down_t = traded(share_left((down_low,), order), grid)
    pieces = matrix_terms([(down_t, 0, right[1])], unit)
    grad_second, down_low, pieces = lax.optimization_barrier((grad_second, down_low, pieces))
    down_1 = Reduction(pieces, grid, unit)

    def work(grad_second, down_low):
        grad, up_low = up_part(1, grad_second, down_low)
        pieces = matrix_terms([up_product_in_tiles(1, up_low)], unit)
        return attention_part(1, grad), pieces

    (grads, grad, gain_first), pieces = segments.run([down_1], work, (grad_second, down_low))
    up_1 = Reduction(pieces, grid, unit)
    gains_1 = gain_rows(gain_first, gain_second)

    def work(grad, grads, gains):
        grads = both(grads, grid)
        grad_second, down_low, gain_second = norm_part(0, grad)
        shared = traded(share_left((down_low, gains), order), grid)
        grad, up_low = up_part(0, grad_second, down_low)
        pieces = attention_terms(left[1], grads, shared, grads[0].shape[0], unit)
        return grad, up_low, gain_second, shared, pieces

    grad, up_low, gain_second, shared, pieces = segments.run(
        [up_1, down_1], work, (grad, grads, gains_1)
    )
    attention_1 = Reduction(pieces, grid, unit)

    def work(grad, up_low, shared):
        pieces = matrix_terms([(shared, 0, right[0]), up_product(0, up_low)], unit)
        return attention_part(0, grad), pieces

    (grads, grad, gain_first), pieces = segments.run(
        [attention_1, up_1], work, (grad, up_low, shared)
    )
    ffn_0 = Reduction(pieces, grid, unit)

    def work(grads, gain_first):
        gains = traded(share_left((gain_rows(gain_first, gain_second),), order), grid)
        return attention_terms(left[0], both(grads, grid), gains, 0, unit)

    segments.join(down_1, up_1)
    pieces = segments.run([ffn_0, attention_1, down_1], work, (grads, gain_first))
    attention_0 = Reduction(pieces, grid, unit)
    segments.run([ffn_0, attention_0, attention_1], pending=[attention_0])
    segments.run([ffn_0], pending=[ffn_0])
    segments.run([attention_0], pending=[ffn_0])
    segments.run([attention_0])

    summed_0, summed_1 = ffn_0.result(), down_1.result()
    outputs = [
        (attention_outputs(attention.result()), (summed[:, FF:], summed[:, :FF].T))
        for attention, summed in ((attention_0, summed_0), (attention_1, summed_1))
    ]
    return finish(hidden, grad, outputs)


def solution(mesh):
    placed = (
        P(("dp", "fsdp"), None, None),
        P(("dp", "fsdp")),
        P(None, ("dp", "fsdp"), None),
        P(None, ("dp", "fsdp"), None),
        P(None, ("dp", "fsdp"), None),
        P(None, ("dp", "fsdp"), None),
        P(None, ("dp", "fsdp"), None),
        P(None, None, ("dp", "fsdp")),
        P(None, None, ("dp", "fsdp")),
        P(("dp", "fsdp"), None, None),
    )
    return jax.shard_map(
        functools.partial(per_device, (mesh.shape["dp"], mesh.shape["fsdp"])),
        mesh=mesh,
        in_specs=placed,
        out_specs=(
            P(("dp", "fsdp"), None, None),
            P(("dp", "fsdp"), None, None),
            P(None, ("dp", "fsdp"), None),
            P(None, ("dp", "fsdp"), None),
            P(None, ("dp", "fsdp"), None),
            P(None, ("dp", "fsdp"), None),
            P(None, ("dp", "fsdp"), None),
            P(None, None, ("dp", "fsdp")),
            P(None, None, ("dp", "fsdp")),
        ),
        check_vma=False,
    )
```

```python
import functools

import jax
import jax.numpy as jnp
from jax import lax
from jax.experimental import pallas as pl
from jax.experimental.pallas import tpu as pltpu
import numpy as np
from jax.sharding import PartitionSpec as P

D = 768
HEADS = 12
HEAD_DIM = 64
FF = 3072
LAYERS = 2
PAD = 128
LIGHT = pl.CostEstimate(flops=1 << 20, bytes_accessed=1 << 16, transcendentals=0)


def norm(value, gain):
    centred = value - jnp.mean(value, axis=-1, keepdims=True)
    spread = jnp.mean(centred * centred, axis=-1, keepdims=True)
    return centred * lax.rsqrt(spread + 1e-05) * gain


def gelu_tanh(value):
    return jax.nn.gelu(value, approximate=True)


def product(left, right):
    return jnp.dot(left, right, preferred_element_type=jnp.float32)


def product_left_t(left, right):
    return lax.dot_general(
        left, right, (((0,), (0,)), ((), ())), preferred_element_type=jnp.float32
    )


def product_right_t(left, right):
    return lax.dot_general(
        left, right, (((1,), (1,)), ((), ())), preferred_element_type=jnp.float32
    )


def pack_attention(shards, layer):
    query_w, key_w, value_w, out_w, _, _, gains = (member[layer] for member in shards)
    gain_columns = jnp.pad(gains.T, ((0, 0), (0, PAD - 2)))
    return jnp.concatenate([query_w, key_w, value_w, out_w, gain_columns], axis=1)


def pack_ffn(shards, layer):
    return jnp.concatenate([shards[4][layer], shards[5][layer].T], axis=1)


def plain_gather(block):
    return lax.all_gather(block, ("dp", "fsdp"), axis=0, tiled=True)


def unpack(attention, ffn):
    return (
        attention[:, : 3 * D],
        attention[:, 3 * D : 4 * D],
        ffn[:, :FF],
        ffn[:, FF:],
        attention[:, 4 * D : 4 * D + 2].T.astype(jnp.float32),
    )


def visible_keys(length, token_count, swap):
    half = token_count // 2
    positions = lax.broadcasted_iota(jnp.int32, (2, half), 0) * half + lax.broadcasted_iota(
        jnp.int32, (2, half), 1
    )
    if swap:
        positions = positions[::-1]
    return positions < length


def split_heads(value):
    return value.reshape(2, value.shape[0] // 2, HEADS, HEAD_DIM)


def paired_heads(query, keys, values, swap):
    query_heads = split_heads(query)
    key_heads = split_heads(keys)
    value_heads = split_heads(values)
    if swap:
        key_heads = key_heads[::-1]
        value_heads = value_heads[::-1]
    return (query_heads, key_heads, value_heads)


def masked_scores(query_heads, key_heads, visible):
    scores = (
        jnp.einsum("bqhd,bkhd->bhqk", query_heads, key_heads, preferred_element_type=jnp.float32)
        * 0.125
    )
    return jnp.where(visible[:, None, None, :], scores, -1e30)


def attend_forward(query, keys, values, visible, swap):
    token_count = query.shape[0]
    query_heads, key_heads, value_heads = paired_heads(query, keys, values, swap)
    scores = masked_scores(query_heads, key_heads, visible)
    highest = jnp.max(scores, axis=-1, keepdims=True)
    raised = jnp.exp(scores - highest)
    total = jnp.sum(raised, axis=-1, keepdims=True)
    shares = (raised / total).astype(jnp.bfloat16)
    mixed = jnp.einsum("bhqk,bkhd->bqhd", shares, value_heads, preferred_element_type=jnp.float32)
    return (mixed.reshape(token_count, -1), highest + jnp.log(total))


def attend_backward(query, keys, values, visible, swap, log_total, grad_mixed):
    token_count = query.shape[0]
    query_heads, key_heads, value_heads = paired_heads(query, keys, values, swap)
    scores = masked_scores(query_heads, key_heads, visible)
    shares = jnp.exp(scores - log_total)
    shares_low = shares.astype(jnp.bfloat16)
    grad_heads = split_heads(grad_mixed)
    grad_values = jnp.einsum(
        "bhqk,bqhd->bkhd", shares_low, grad_heads, preferred_element_type=jnp.float32
    )
    grad_shares = jnp.einsum(
        "bqhd,bkhd->bhqk", grad_heads, value_heads, preferred_element_type=jnp.float32
    )
    inner = jnp.sum(shares * grad_shares, axis=-1, keepdims=True)
    grad_scores = (shares * (grad_shares - inner)).astype(jnp.bfloat16)
    grad_query = (
        jnp.einsum("bhqk,bkhd->bqhd", grad_scores, key_heads, preferred_element_type=jnp.float32)
        * 0.125
    )
    grad_keys = (
        jnp.einsum("bhqk,bqhd->bkhd", grad_scores, query_heads, preferred_element_type=jnp.float32)
        * 0.125
    )
    if swap:
        grad_keys = grad_keys[::-1]
        grad_values = grad_values[::-1]
    return tuple(
        (
            member.reshape(token_count, -1).astype(jnp.bfloat16)
            for member in (grad_query, grad_keys, grad_values)
        )
    )


def layer_forward(hidden, length, weights, swap):
    qkv_w, out_w, up_w, down_t, gains = weights
    inputs_low = hidden.astype(jnp.bfloat16)
    qkv = product(inputs_low, qkv_w).astype(jnp.bfloat16)
    query, keys, values = qkv[:, :D], qkv[:, D : 2 * D], qkv[:, 2 * D :]
    visible = visible_keys(length, hidden.shape[0], swap)
    mixed, log_total = attend_forward(query, keys, values, visible, swap)
    mixed_low = mixed.astype(jnp.bfloat16)
    first_sum = hidden + product(mixed_low, out_w)
    normed = norm(first_sum, gains[0])
    normed_low = normed.astype(jnp.bfloat16)
    expanded = product(normed_low, up_w)
    activated = gelu_tanh(expanded).astype(jnp.bfloat16)
    second_sum = normed + product_right_t(activated, down_t)
    output = norm(second_sum, gains[1])
    kept = (
        inputs_low,
        query,
        keys,
        values,
        log_total,
        mixed_low,
        first_sum,
        normed_low,
        expanded,
        activated,
        second_sum,
    )
    return (output, kept)


def down_backward(grad_output, kept, weights):
    grad_second, grad_gain = jax.vjp(norm, kept[10], weights[4][1])[1](grad_output)
    return (grad_second, grad_second.astype(jnp.bfloat16), grad_gain)


def up_backward(grad_second, down_low, kept, weights):
    grad_active = product(down_low, weights[3])
    up_low = jax.vjp(gelu_tanh, kept[8])[1](grad_active)[0].astype(jnp.bfloat16)
    return (grad_second + product_right_t(up_low, weights[2]), up_low)


def mixed_backward(grad_normed, kept, weights):
    grad_first, grad_gain = jax.vjp(norm, kept[6], weights[4][0])[1](grad_normed)
    attn_low = grad_first.astype(jnp.bfloat16)
    grad_mixed = product_right_t(attn_low, weights[1]).astype(jnp.bfloat16)
    return (grad_first, attn_low, grad_mixed, grad_gain)


def scores_backward(grad_mixed, kept, swapped, length):
    query, keys, values, log_total = kept[1:5]
    visible = visible_keys(length, query.shape[0], swapped)
    return jnp.concatenate(
        attend_backward(query, keys, values, visible, swapped, log_total, grad_mixed), axis=1
    )


def inputs_backward(grad_first, grad_qkv, weights):
    return grad_first + product_right_t(grad_qkv, weights[0])


def plain_scatter(terms):
    return lax.psum_scatter(
        terms.astype(jnp.bfloat16), ("dp", "fsdp"), scatter_dimension=0, tiled=True
    ).astype(jnp.float32)


def plain_ffn_terms(operands):
    normed_low, up_low, down_low, activated = operands
    return jnp.concatenate(
        [
            product_left_t(normed_low, up_low).astype(jnp.bfloat16),
            product_left_t(down_low, activated).astype(jnp.bfloat16),
        ],
        axis=1,
    )


def plain_attention_terms(operands, gains):
    inputs_low, grad_qkv, mixed_low, attn_low = operands
    return jnp.concatenate(
        [
            product_left_t(inputs_low, grad_qkv).astype(jnp.bfloat16),
            product_left_t(mixed_low, attn_low).astype(jnp.bfloat16),
            jnp.pad(gains.T, ((0, 0), (0, PAD - 2))).astype(jnp.bfloat16),
        ],
        axis=1,
    )


def attention_outputs(summed):
    return (
        *(summed[:, j * D : (j + 1) * D] for j in range(4)),
        summed[:, 4 * D : 4 * D + 2].T,
    )


def ffn_outputs(summed):
    return (summed[:, :FF], summed[:, FF:].T)


class Grid:
    def __init__(self):
        places = [
            (x, core, z, y) for x in range(2) for core in range(2) for z in range(4) for y in range(2)
        ]
        number = {place: index for index, place in enumerate(places)}

        def route(move, senders=range(4)):
            return [
                (number[place], number[move(*place)]) for place in places if place[2] in senders
            ]

        self.core = route(lambda x, core, z, y: (x, 1 - core, z, y))
        self.first = route(
            lambda x, core, z, y: (x, core, z, 1 - y) if core else (1 - x, core, z, y)
        )
        self.second = route(
            lambda x, core, z, y: (1 - x, core, z, y) if core else (x, core, z, 1 - y)
        )
        self.pair = route(lambda x, core, z, y: (x, core, z ^ 1, y))
        self.middle = route(lambda x, core, z, y: (x, core, 3 - z, y), (1, 2))
        self.outward = route(lambda x, core, z, y: (x, core, z ^ 1, y), (1, 2))
        self.line = [route(lambda x, core, z, y, s=s: (x, core, z ^ s, y)) for s in (1, 2, 3)]


def swap(value, route):
    return lax.ppermute(value, ("dp", "fsdp"), route)


SLOTS = np.array([(far, near, s) for far, near in ((1, 1), (1, 0), (0, 1), (0, 0)) for s in range(4)])
ROWS = tuple((j, j + 2) for j in range(0, 16, 2))
TERM_SLOTS = SLOTS[[0, 1, 4, 5, 2, 3, 10, 11, 6, 7, 8, 9, 12, 13, 14, 15]]
TERM_ROWS = ((0, 4), (4, 8), (8, 10), (10, 12), (12, 16))


def slot_rows(slots, place, x, y, owner):
    first, second = (jnp.asarray(slots[:, j], jnp.int32) for j in range(2))
    along_x = jnp.where(owner == 0, first, second)
    along_y = jnp.where(owner == 0, second, first)
    return (((x ^ along_x) * 2 + owner) * 4 + place) * 2 + (y ^ along_y)


def row_order(unit):
    dp, fsdp = lax.axis_index("dp"), lax.axis_index("fsdp")
    x, core, z, y = dp // 2, dp % 2, fsdp // 2, fsdp % 2
    slots = np.repeat(TERM_SLOTS, unit, axis=0)
    place = z ^ jnp.asarray(slots[:, 2], jnp.int32)
    offset = jnp.asarray(np.tile(np.arange(unit), 16), jnp.int32)
    rows = jnp.concatenate(
        [slot_rows(slots, place, x, y, owner) * unit + offset for owner in (core, 1 - core)]
    )
    natural = lax.broadcasted_iota(jnp.int32, (32 * unit, 32 * unit), 0)
    return (natural == rows[None]).astype(jnp.bfloat16)


def share_left(values, order):
    lengths = [max(value.shape[0], PAD) for value in values]
    half = D // 2

    def body(order_ref, *refs):
        mine, other = refs[len(values) :]
        start = 0
        for length, value_ref in zip(lengths, refs):
            ordered = dot(value_ref[...].astype(jnp.bfloat16), order_ref[...])
            short = length - ordered.shape[0]
            if short:
                ordered = jnp.concatenate([ordered, jnp.zeros((short, D), jnp.float32)], axis=0)
            turned = ordered.T.astype(jnp.bfloat16)
            mine[:, start : start + length] = turned[:half]
            other[:, start : start + length] = turned[half:]
            start += length

    return pl.pallas_call(
        body,
        in_specs=[VMEM_SPEC] * (1 + len(values)),
        out_specs=[VMEM_SPEC] * 2,
        out_shape=shapes(*[((half, sum(lengths)), jnp.bfloat16)] * 2),
        cost_estimate=LIGHT,
        compiler_params=params(8),
    )(order, *values)


def both(value, grid):
    return (value, swap(value, grid.core))


def traded(pair, grid):
    return (pair[0], swap(pair[1], grid.core))


def dot(left, right):
    return jnp.dot(left, right, preferred_element_type=jnp.float32)


def dot_nt(left, right):
    return lax.dot_general(
        left, right, (((1,), (1,)), ((), ())), preferred_element_type=jnp.float32
    )


def dot_tn(left, right):
    return lax.dot_general(
        left, right, (((0,), (0,)), ((), ())), preferred_element_type=jnp.float32
    )


def lane_masks():
    lane = lax.broadcasted_iota(jnp.int32, (1, 2 * HEAD_DIM), 1)
    first = (lane < HEAD_DIM).astype(jnp.float32)
    return first.astype(jnp.bfloat16), (1.0 - first).astype(jnp.bfloat16), lane < HEAD_DIM


def two_heads(value, masks):
    return jnp.concatenate([value * masks[0], value * masks[1]], axis=0)


def pair_softmax(query_pair, keys, key_block, length):
    scores = dot_nt(keys, query_pair) * 0.125
    position = lax.broadcasted_iota(jnp.int32, scores.shape, 0) + key_block * keys.shape[0]
    scores = jnp.where(position < length, scores, -1e30)
    raised = jnp.exp(scores - jnp.max(scores, axis=0, keepdims=True))
    return raised / jnp.sum(raised, axis=0, keepdims=True)


def normalised(value):
    centred = value - jnp.mean(value, axis=-1, keepdims=True)
    rate = lax.rsqrt(jnp.mean(centred * centred, axis=-1, keepdims=True) + 1e-05)
    return centred * rate, rate


def norm_backward(value, gain, grad):
    ratio, rate = normalised(value)
    scaled = grad * gain
    slope = jnp.mean(scaled * ratio, axis=-1, keepdims=True)
    result = rate * (scaled - jnp.mean(scaled, axis=-1, keepdims=True) - ratio * slope)
    return result, jnp.sum(grad * ratio, axis=0, keepdims=True)


def head_parts(half, swapped):
    for block in range(2):
        key_block = 1 - block if swapped else block
        rows = slice(block * half, (block + 1) * half)
        key_rows = slice(key_block * half, (key_block + 1) * half)
        for pair in range(HEADS // 2):
            yield key_block, rows, key_rows, pair * 2 * HEAD_DIM


VMEM_SPEC = pl.BlockSpec(memory_space=pltpu.VMEM)
SMEM_SPEC = pl.BlockSpec(memory_space=pltpu.SMEM)
ANY_SPEC = pl.BlockSpec(memory_space=pl.ANY)


def params(mebibytes):
    return pltpu.CompilerParams(vmem_limit_bytes=mebibytes << 20)


def shapes(*pairs):
    return [jax.ShapeDtypeStruct(shape, dtype) for shape, dtype in pairs]


def attention_columns(weights, start, target, sems):
    copies = []
    for part in range(5):
        width = D if part < 4 else PAD
        copies.append(
            pltpu.make_async_copy(
                weights.at[:, pl.ds(start + part * D, width)],
                target.at[:, pl.ds(part * D, width)],
                sems.at[part],
            )
        )
    for copy in copies:
        copy.start()
    return copies


def attention_forward(hidden, lengths, weights, start, swapped):
    tokens = hidden.shape[0]
    half = tokens // 2
    low = jnp.bfloat16

    def body(length_ref, hidden_ref, w_any, low_out, qkv, mixed, first_sum, gains, w, sems):
        copies = attention_columns(w_any, start, w, sems)
        value = hidden_ref[...].astype(low)
        low_out[...] = value
        masks = lane_masks()
        for part in range(3):
            copies[part].wait()
            columns = slice(part * D, (part + 1) * D)
            qkv[:, columns] = dot(value, w[:, columns]).astype(low)
        for key_block, rows, key_rows, lane in head_parts(half, swapped):
            query = two_heads(qkv[rows, lane : lane + 128], masks)
            keys = qkv[key_rows, D + lane : D + lane + 128]
            values = qkv[key_rows, 2 * D + lane : 2 * D + lane + 128]
            shares = pair_softmax(query, keys, key_block, length_ref[0]).astype(low)
            out = dot_tn(shares, values)
            mixed[rows, lane : lane + 128] = jnp.where(masks[2], out[:half], out[half:]).astype(low)
        copies[3].wait()
        first_sum[...] = hidden_ref[...] + dot(mixed[...], w[:, 3 * D : 4 * D])
        copies[4].wait()
        gains[...] = w[:, 4 * D :].astype(jnp.float32).T[:8]

    return pl.pallas_call(
        body,
        in_specs=[SMEM_SPEC, VMEM_SPEC, ANY_SPEC],
        out_specs=[VMEM_SPEC] * 5,
        out_shape=shapes(
            ((tokens, D), low),
            ((tokens, 3 * D), low),
            ((tokens, D), low),
            ((tokens, D), jnp.float32),
            ((8, D), jnp.float32),
        ),
        scratch_shapes=[pltpu.VMEM((D, 4 * D + PAD), low), pltpu.SemaphoreType.DMA((5,))],
        cost_estimate=LIGHT,
        compiler_params=params(14),
    )(lengths, hidden, weights)


FF_TILE = D


def ffn_forward(first_sum, gains, weights, start):
    tokens = first_sum.shape[0]
    low = jnp.bfloat16
    steps = FF // FF_TILE
    first = start // FF_TILE

    def body(sum_ref, gain_ref, up, down, normed_low, activated, slope, second_sum, out, total):
        step = pl.program_id(0)

        @pl.when(step == 0)
        def _():
            normed = normalised(sum_ref[...])[0] * gain_ref[0:1]
            normed_low[...] = normed.astype(low)
            total[...] = normed

        u = dot(normed_low[...], up[...])
        inner = 0.7978845608028654 * (u + 0.044715 * (u * u * u))
        wave = jnp.tanh(inner)
        active = (0.5 * u * (1.0 + wave)).astype(low)
        slope[...] = (
            0.5 * (1.0 + wave)
            + 0.5 * u * (1.0 - wave * wave) * (0.7978845608028654 * (1.0 + 0.134145 * (u * u)))
        ).astype(low)
        activated[...] = active
        total[...] += dot_nt(active, down[...])

        @pl.when(step == steps - 1)
        def _():
            second_sum[...] = total[...]
            out[...] = normalised(total[...])[0] * gain_ref[1:2]

    def fixed(shape):
        return pl.BlockSpec(shape, lambda j: (0, 0))

    wide = pl.BlockSpec((tokens, FF_TILE), lambda j: (0, j))
    return pl.pallas_call(
        body,
        grid=(steps,),
        in_specs=[
            fixed((tokens, D)),
            fixed((8, D)),
            pl.BlockSpec((D, FF_TILE), lambda j: (0, first + j)),
            pl.BlockSpec((D, FF_TILE), lambda j: (0, first + steps + j)),
        ],
        out_specs=[fixed((tokens, D)), wide, wide, fixed((tokens, D)), fixed((tokens, D))],
        out_shape=shapes(
            ((tokens, D), low),
            ((tokens, FF), low),
            ((tokens, FF), low),
            ((tokens, D), jnp.float32),
            ((tokens, D), jnp.float32),
        ),
        scratch_shapes=[pltpu.VMEM((tokens, D), jnp.float32)],
        cost_estimate=LIGHT,
        compiler_params=params(16),
    )(first_sum, gains, weights, weights)


def second_norm_backward(grad, second_sum, gains):
    tokens = grad.shape[0]

    def body(grad_ref, sum_ref, gain_ref, out, low_out, gain_out):
        result, gain_grad = norm_backward(sum_ref[...], gain_ref[1:2], grad_ref[...].astype(jnp.float32))
        out[...] = result
        low_out[...] = result.astype(jnp.bfloat16)
        gain_out[...] = gain_grad

    return pl.pallas_call(
        body,
        in_specs=[VMEM_SPEC] * 3,
        out_specs=[VMEM_SPEC] * 3,
        out_shape=shapes(
            ((tokens, D), jnp.float32), ((tokens, D), jnp.bfloat16), ((1, D), jnp.float32)
        ),
        cost_estimate=LIGHT,
        compiler_params=params(6),
    )(grad, second_sum, gains)


def up_backward_kernel(grad_second, down_low, slope, weights, start):
    tokens = grad_second.shape[0]
    low = jnp.bfloat16
    steps = FF // FF_TILE
    first = start // FF_TILE

    def body(grad_ref, low_ref, slope_ref, up, down, up_low, out):
        step = pl.program_id(0)

        @pl.when(step == 0)
        def _():
            out[...] = grad_ref[...]

        piece = (dot(low_ref[...], down[...]) * slope_ref[...].astype(jnp.float32)).astype(low)
        up_low[...] = piece
        out[...] += dot_nt(piece, up[...])

    def fixed(shape):
        return pl.BlockSpec(shape, lambda j: (0, 0))

    wide = pl.BlockSpec((tokens, FF_TILE), lambda j: (0, j))
    return pl.pallas_call(
        body,
        grid=(steps,),
        in_specs=[
            fixed((tokens, D)),
            fixed((tokens, D)),
            wide,
            pl.BlockSpec((D, FF_TILE), lambda j: (0, first + j)),
            pl.BlockSpec((D, FF_TILE), lambda j: (0, first + steps + j)),
        ],
        out_specs=[wide, fixed((tokens, D))],
        out_shape=shapes(((tokens, FF), low), ((tokens, D), jnp.float32)),
        cost_estimate=LIGHT,
        compiler_params=params(12),
    )(grad_second, down_low, slope, weights, weights)


def attention_backward_kernel(grad, first_sum, gains, qkv, lengths, weights, start, swapped):
    tokens = grad.shape[0]
    half = tokens // 2
    low = jnp.bfloat16

    def body(length_ref, grad_ref, sum_ref, gain_ref, qkv_ref, w_any, *rest):
        grads, grad_in, gain_out, grad_mixed, w, sems = rest
        copies = attention_columns(w_any, start, w, sems)
        masks = lane_masks()
        result, gain_grad = norm_backward(sum_ref[...], gain_ref[0:1], grad_ref[...])
        grad_in[...] = result
        grads[:, 3 * D :] = result.astype(low)
        gain_out[...] = gain_grad
        copies[3].wait()
        grad_mixed[...] = dot_nt(grads[:, 3 * D :], w[:, 3 * D : 4 * D]).astype(low)
        for key_block, rows, key_rows, lane in head_parts(half, swapped):
            query = two_heads(qkv_ref[rows, lane : lane + 128], masks)
            keys = qkv_ref[key_rows, D + lane : D + lane + 128]
            values = qkv_ref[key_rows, 2 * D + lane : 2 * D + lane + 128]
            arriving = two_heads(grad_mixed[rows, lane : lane + 128], masks)
            shares = pair_softmax(query, keys, key_block, length_ref[0])
            grad_values = dot(shares.astype(low), arriving)
            grad_shares = dot_nt(values, arriving)
            inner = jnp.sum(shares * grad_shares, axis=0, keepdims=True)
            grad_scores = (shares * (grad_shares - inner)).astype(low)
            grad_query = dot_tn(grad_scores, keys) * 0.125
            grad_keys = dot(grad_scores, query) * 0.125
            grads[rows, lane : lane + 128] = jnp.where(
                masks[2], grad_query[:half], grad_query[half:]
            ).astype(low)
            grads[key_rows, D + lane : D + lane + 128] = grad_keys.astype(low)
            grads[key_rows, 2 * D + lane : 2 * D + lane + 128] = grad_values.astype(low)
        for part in (0, 1, 2):
            copies[part].wait()
            columns = slice(part * D, (part + 1) * D)
            grad_in[...] += dot_nt(grads[:, columns], w[:, columns])
        copies[4].wait()

    return pl.pallas_call(
        body,
        in_specs=[SMEM_SPEC] + [VMEM_SPEC] * 4 + [ANY_SPEC],
        out_specs=[VMEM_SPEC] * 3,
        out_shape=shapes(
            ((tokens, 4 * D), low),
            ((tokens, D), jnp.float32),
            ((1, D), jnp.float32),
        ),
        scratch_shapes=[
            pltpu.VMEM((tokens, D), low),
            pltpu.VMEM((D, 4 * D + PAD), low),
            pltpu.SemaphoreType.DMA((5,)),
        ],
        cost_estimate=LIGHT,
        compiler_params=params(16),
    )(lengths, grad, first_sum, gains, qkv, weights)


def matrix_terms(products, unit):
    tile = D
    tokens, width = products[0][2][0].shape
    steps = width // tile

    def body(*refs):
        outs = refs[starts[-1] :]
        for j in range(len(products)):
            la, lb, ra, *received = refs[starts[j] : starts[j + 1]]
            for step in range(steps if len(received) > 1 else 1):
                rb = received[step]
                place = pl.program_id(0) - j * steps
                here = place == step if len(received) > 1 else place // steps == 0

                @pl.when(here)
                def _(la=la, lb=lb, ra=ra, rb=rb):
                    value = (dot(la[...], ra[...]) + dot(lb[...], rb[...])).astype(jnp.bfloat16)
                    for (low, high), out in zip(TERM_ROWS, outs):
                        out[...] = value[low * unit : high * unit]

    in_specs, operands, starts = [], [], [0]
    for j, (left, part, right) in enumerate(products):
        block = pl.BlockSpec((16 * unit, tokens), lambda i, part=part: (0, part))
        column = pl.BlockSpec(
            (tokens, tile), lambda i, j=j: (0, jnp.clip(i - j * steps, 0, steps - 1))
        )
        own, received = right
        if isinstance(received, list):
            whole = pl.BlockSpec((tokens, tile), lambda i: (0, 0))
            in_specs += [block, block, column] + [whole] * steps
            operands += [*left, own, *received]
        else:
            in_specs += [block, block, column, column]
            operands += [*left, own, received]
        starts.append(len(operands))
    wide = width * len(products)
    return pl.pallas_call(
        body,
        grid=(wide // tile,),
        in_specs=in_specs,
        out_specs=[pl.BlockSpec(((b - a) * unit, tile), lambda i: (0, i)) for a, b in TERM_ROWS],
        out_shape=shapes(*((((b - a) * unit, wide), jnp.bfloat16) for a, b in TERM_ROWS)),
        cost_estimate=LIGHT,
        compiler_params=params(10),
    )(*operands)


def attention_terms(left, grads, gains, start, unit):
    tokens = grads[0].shape[0]

    def body(la, lb, ra, rb, ga, gb, *outs):
        def put(value, column):
            value = value.astype(jnp.bfloat16)
            for (low, high), out in zip(TERM_ROWS, outs):
                out[:, column : column + value.shape[1]] = value[low * unit : high * unit]

        for j in range(4):
            part = slice(j * D, (j + 1) * D)
            from_left = slice(0, tokens) if j < 3 else slice(tokens, 2 * tokens)
            put(
                dot(la[:, from_left], ra[:, part]) + dot(lb[:, from_left], rb[:, part]),
                j * D,
            )
        gain = slice(start, start + PAD)
        put(ga[:, gain].astype(jnp.float32) + gb[:, gain].astype(jnp.float32), 4 * D)

    return pl.pallas_call(
        body,
        in_specs=[VMEM_SPEC] * 6,
        out_specs=[VMEM_SPEC] * 5,
        out_shape=shapes(*((((b - a) * unit, 4 * D + PAD), jnp.bfloat16) for a, b in TERM_ROWS)),
        cost_estimate=LIGHT,
        compiler_params=params(12),
    )(*left, *grads, *gains)


def square_sums(came_first, came_second, later_first, later_second):
    rows, width = later_first.shape

    def body(one, other, first, second, first_out, second_out):
        first_out[...] = add(first[...], other[:rows]).astype(jnp.bfloat16)
        second_out[...] = add(second[...], one[:rows]).astype(jnp.bfloat16)

    return pl.pallas_call(
        body,
        in_specs=[VMEM_SPEC] * 4,
        out_specs=[VMEM_SPEC] * 2,
        out_shape=shapes(*[((rows, width), jnp.bfloat16)] * 2),
        cost_estimate=LIGHT,
        compiler_params=params(8),
    )(came_first, came_second, later_first, later_second)


def line_sums(groups, unit):
    two = 2 * unit
    widths = [group[0].shape[1] for group in groups]

    def body(*refs):
        outs = refs[5 * len(groups) :]
        start = 0
        for j, width in enumerate(widths):
            own, one, other, last_first, last_second = refs[5 * j : 5 * j + 5]
            columns = slice(start, start + width)
            near = add(own[:two], one[two:], last_second[...])
            far = add(own[two:], other[two:], last_first[...])
            outs[0][:, columns] = near[:unit]
            outs[1][:, columns] = near[unit:].astype(jnp.bfloat16)
            outs[2][:, columns] = far[:unit].astype(jnp.bfloat16)
            outs[3][:, columns] = far[unit:].astype(jnp.bfloat16)
            start += width

    low = ((unit, sum(widths)), jnp.bfloat16)
    return pl.pallas_call(
        body,
        in_specs=[VMEM_SPEC] * (5 * len(groups)),
        out_specs=[VMEM_SPEC] * 4,
        out_shape=shapes(((unit, sum(widths)), jnp.float32), low, low, low),
        cost_estimate=LIGHT,
        compiler_params=params(14),
    )(*(value for group in groups for value in group))


def stack_attention(layers):
    rows, width = layers[0][0].shape
    starts = [0]
    for layer in layers:
        starts.append(starts[-1] + len(layer))

    def body(*refs):
        outs = refs[starts[-1] :]
        for layer in range(len(layers)):
            total = add(*(ref[...] for ref in refs[starts[layer] : starts[layer + 1]]))
            for j, out in enumerate(outs):
                out[layer] = total[:, j * D : min((j + 1) * D, width)]

    return pl.pallas_call(
        body,
        in_specs=[VMEM_SPEC] * starts[-1],
        out_specs=[VMEM_SPEC] * 5,
        out_shape=shapes(
            *[((len(layers), rows, D), jnp.float32)] * 4,
            ((len(layers), rows, PAD), jnp.float32),
        ),
        cost_estimate=LIGHT,
        compiler_params=params(8),
    )(*(value for layer in layers for value in layer))


def add(*values):
    return sum(value.astype(jnp.float32) for value in values)


class Reduction:
    def __init__(self, pieces, grid, unit):
        self.grid, self.unit, self.round, self.joined = grid, unit, 0, False
        self.out, self.kept = list(pieces[:2]), list(pieces[2:])

    def state(self, pending):
        return ([] if pending else self.out, self.kept)

    def restore(self, state):
        out, self.kept = state
        self.out = out or self.out

    def send(self):
        grid = self.grid
        routes = grid.line if self.round == 2 else (grid.first, grid.second)
        self.out = [swap(value, route) for value, route in zip(self.out, routes)]
        self.round += 1

    def prepare(self):
        if self.round == 1:
            later_first, later_second, own = self.kept
            self.kept = [own, *self.out]
            self.out = list(square_sums(*self.out, later_first, later_second))
        elif not self.joined:
            self.join()

    def join(self, *others):
        groups = [(*reduction.kept, *reduction.out) for reduction in (self, *others)]
        own, *self.out = line_sums(groups, self.unit)
        self.kept, self.joined = [own], True

    def result(self):
        return add(self.kept[0], *self.out)


def gate(values, *earlier):
    return lax.optimization_barrier((values, earlier))[0]


class Segments:
    def __init__(self):
        self.active = []

    def join(self, reduction, *others):
        reduction.join(*others)
        self.active = [r for r in self.active if r not in others]

    def run(self, sends, compute=None, values=(), pending=()):
        for reduction in sends:
            if reduction not in self.active:
                self.active.append(reduction)
            if reduction.round:
                reduction.prepare()
            reduction.send()
        if compute:
            values = compute(*values)
        states = [reduction.state(reduction in pending) for reduction in self.active]
        states, values = lax.optimization_barrier((states, values))
        for reduction, state in zip(self.active, states):
            reduction.restore(state)
        self.active = [r for r in self.active if r.round < 3 or r in pending]
        return values


class Gathering:
    def __init__(self, block, grid):
        self.pieces, self.grid, self.unit = [block], grid, block.shape[0]
        self.steps = [self.pair, self.middle, self.outward, self.square, self.diagonal]

    def advance(self):
        self.pieces = list(self.steps.pop(0)(self.pieces, self.grid, 2 * self.unit))

    @staticmethod
    def pair(pieces, grid, two):
        (block,) = pieces
        return (jnp.concatenate([block, swap(block, grid.pair)], axis=0),)

    @staticmethod
    def middle(pieces, grid, two):
        (near,) = pieces
        return (near, swap(near, grid.middle))

    @staticmethod
    def outward(pieces, grid, two):
        near, far = pieces
        z = lax.axis_index("fsdp") // 2
        return (near, jnp.where((z == 1) | (z == 2), far, swap(far, grid.outward)))

    @staticmethod
    def square(pieces, grid, two):
        near, far = pieces
        return (
            swap(far, grid.first),
            swap(near, grid.second),
            swap(near, grid.first),
            swap(far, grid.second),
            near,
            far,
        )

    @staticmethod
    def diagonal(pieces, grid, two):
        first_far, second_near, first_near, second_far, near, far = pieces
        return (
            swap(second_near, grid.first),
            swap(first_far, grid.second),
            first_near,
            first_far,
            second_near,
            second_far,
            near,
            far,
        )

    def result(self):
        pieces = self.pieces
        return place_blocks(pieces + [swap(piece, self.grid.core) for piece in pieces], self.unit)


def place_blocks(pieces, unit):
    width = pieces[0].shape[1]
    dp, fsdp = lax.axis_index("dp"), lax.axis_index("fsdp")
    x, core, z, y = dp // 2, dp % 2, fsdp // 2, fsdp % 2
    s = jnp.asarray(SLOTS[:, 2], jnp.int32)
    place = jnp.where(s < 2, z ^ s, jnp.where(z < 2, s, 3 - s))
    rows = jnp.concatenate([slot_rows(SLOTS, place, x, y, owner) for owner in (core, 1 - core)])
    tiles = unit // 8

    def body(rows_ref, *refs):
        sources, target = refs[:16], refs[16]
        for half in range(2):
            for (low, high), source in zip(ROWS, sources[half * 8 : half * 8 + 8]):
                for slot in range(low, high):
                    row = rows_ref[half * 16 + slot] * tiles
                    first = (slot - low) * tiles
                    target[pl.ds(row, tiles)] = source[first : first + tiles]

    placed = pl.pallas_call(
        body,
        in_specs=[pl.BlockSpec(memory_space=pltpu.SMEM)]
        + [pl.BlockSpec(memory_space=pltpu.VMEM)] * 16,
        out_specs=pl.BlockSpec(memory_space=pltpu.VMEM),
        out_shape=jax.ShapeDtypeStruct((32 * tiles, 8, width), jnp.bfloat16),
        cost_estimate=LIGHT,
        compiler_params=params(22),
    )(rows, *(piece.reshape(-1, 8, width) for piece in pieces))
    return placed.reshape(32 * unit, width)


def per_device(
    sizes,
    tokens,
    lengths,
    query_weight,
    key_weight,
    value_weight,
    attn_out_weight,
    up_weight,
    down_weight,
    norm_gains,
    cotangent,
):
    shards = (
        query_weight,
        key_weight,
        value_weight,
        attn_out_weight,
        up_weight,
        down_weight,
        norm_gains,
    )
    if sizes == (4, 8):
        return grid_step(tokens, lengths, shards, cotangent)
    hidden = tokens[0].astype(jnp.float32)
    length = lengths[0]
    weights_all = [
        unpack(plain_gather(pack_attention(shards, j)), plain_gather(pack_ffn(shards, j)))
        for j in range(LAYERS)
    ]
    kept_all = []
    for layer in range(LAYERS):
        hidden, kept = layer_forward(hidden, length, weights_all[layer], layer % 2 == 1)
        kept_all.append(kept)
    grad = cotangent[0].astype(jnp.float32)
    outputs = [None] * LAYERS
    for layer in reversed(range(LAYERS)):
        kept, weights = kept_all[layer], weights_all[layer]
        grad_second, down_low, gain_second = down_backward(grad, kept, weights)
        grad_normed, up_low = up_backward(grad_second, down_low, kept, weights)
        ffn = plain_scatter(plain_ffn_terms((kept[7], up_low, down_low, kept[9])))
        grad_first, attn_low, grad_mixed, gain_first = mixed_backward(grad_normed, kept, weights)
        grad_qkv = scores_backward(grad_mixed, kept, layer % 2 == 1, length)
        grad = inputs_backward(grad_first, grad_qkv, weights)
        gains = jnp.stack([gain_first, gain_second])
        attention = plain_scatter(
            plain_attention_terms((kept[0], grad_qkv, kept[5], attn_low), gains)
        )
        outputs[layer] = (attention_outputs(attention), ffn_outputs(ffn))
    return finish(hidden, grad, outputs)


def finish(hidden, grad, outputs):
    layers = [(*attention[:4], *ffn, attention[4]) for attention, ffn in outputs]
    stacked = tuple((jnp.stack([entry[member] for entry in layers]) for member in range(7)))
    return (hidden.astype(jnp.bfloat16)[None], grad[None], *stacked)


def gather_first_layer(blocks, second, order, grid, attend):
    attention, ffn = (Gathering(block, grid) for block in blocks)

    def hold(*gatherings):
        pieces = [g.pieces[:2] if len(g.pieces) == 6 else g.pieces for g in gatherings]
        pieces = lax.optimization_barrier(pieces)
        for g, held in zip(gatherings, pieces):
            g.pieces = [*held, *g.pieces[len(held) :]]

    attention.advance()
    hold(attention)
    ffn.pieces = gate(ffn.pieces, attention.pieces)
    attention.advance()
    ffn.advance()
    hold(attention, ffn)
    attention.advance()
    ffn.advance()
    order, ffn.pieces = lax.optimization_barrier((order, ffn.pieces))
    hold(attention, ffn)
    attention.advance()
    ffn.advance()
    hold(attention, ffn)
    attention.advance()
    ffn.pieces = gate(ffn.pieces, attention.pieces[3])
    ffn.advance()
    hold(attention)
    weights = attention.result()
    attended = attend(weights)
    held, attended = lax.optimization_barrier((ffn.pieces[:2], attended))
    ffn.pieces = [*held, *ffn.pieces[2:]]
    ffn.advance()
    held, second = lax.optimization_barrier((ffn.pieces[6:], second))
    ffn.pieces = [*ffn.pieces[:6], *held]
    return weights, ffn.result(), second, order, attended


def grid_step(tokens, lengths, shards, cotangent):
    grid, unit = Grid(), shards[0].shape[1]
    order = row_order(unit)
    hidden = tokens[0].astype(jnp.float32)

    second = plain_gather(
        jnp.concatenate([pack_ffn(shards, 1), pack_attention(shards, 1)], axis=1)
    )

    def attend(weights):
        return attention_forward(hidden, lengths, weights, 0, False)

    attention, ffn, second, order, attended = gather_first_layer(
        (pack_attention(shards, 0), pack_ffn(shards, 0)), second, order, grid, attend
    )
    attention_at = ((attention, 0, False), (second, 2 * FF, True))
    ffn_at = ((ffn, 0), (second, 0))

    kept, left, right = [], [], []
    for layer in range(LAYERS):
        if layer:
            attended = attention_forward(hidden, lengths, *attention_at[layer])
        inputs_low, qkv, mixed, first_sum, gains = attended
        normed_low, activated, slope, second_sum, hidden = ffn_forward(
            first_sum, gains, *ffn_at[layer]
        )
        kept.append((qkv, first_sum, gains, slope, second_sum))
        left.append(traded(share_left((inputs_low, mixed, normed_low), order), grid))
        right.append(both(activated, grid))

    def norm_part(layer, grad):
        return second_norm_backward(grad, kept[layer][4], kept[layer][2])

    def up_part(layer, grad_second, down_low):
        up_low, grad = up_backward_kernel(grad_second, down_low, kept[layer][3], *ffn_at[layer])
        return grad, up_low

    def attention_part(layer, grad):
        qkv, first_sum, gains = kept[layer][:3]
        return attention_backward_kernel(
            grad, first_sum, gains, qkv, lengths, *attention_at[layer]
        )

    def gain_rows(first, second):
        return jnp.concatenate([first, second, jnp.zeros((6, D), jnp.float32)], axis=0)

    def up_product(layer, up_low):
        return left[layer], 2, both(up_low, grid)

    def up_product_in_tiles(layer, up_low):
        received = [swap(up_low[:, j : j + D], grid.core) for j in range(0, FF, D)]
        return left[layer], 2, (up_low, received)

    segments = Segments()
    grad_second, down_low, gain_second = norm_part(1, cotangent[0])
    down_t = traded(share_left((down_low,), order), grid)
    pieces = matrix_terms([(down_t, 0, right[1])], unit)
    grad_second, down_low, pieces = lax.optimization_barrier((grad_second, down_low, pieces))
    down_1 = Reduction(pieces, grid, unit)

    def work(grad_second, down_low):
        grad, up_low = up_part(1, grad_second, down_low)
        pieces = matrix_terms([up_product_in_tiles(1, up_low)], unit)
        return attention_part(1, grad), pieces

    (grads, grad, gain_first), pieces = segments.run([down_1], work, (grad_second, down_low))
    up_1 = Reduction(pieces, grid, unit)
    gains_1 = gain_rows(gain_first, gain_second)

    def work(grad, grads, gains):
        grads = both(grads, grid)
        grad_second, down_low, gain_second = norm_part(0, grad)
        shared = traded(share_left((down_low, gains), order), grid)
        grad, up_low = up_part(0, grad_second, down_low)
        pieces = attention_terms(left[1], grads, shared, grads[0].shape[0], unit)
        return grad, up_low, gain_second, shared, pieces

    grad, up_low, gain_second, shared, pieces = segments.run(
        [up_1, down_1], work, (grad, grads, gains_1)
    )
    attention_1 = Reduction(pieces, grid, unit)

    def work(grad, up_low, shared):
        pieces = matrix_terms([(shared, 0, right[0]), up_product(0, up_low)], unit)
        return attention_part(0, grad), pieces

    (grads, grad, gain_first), pieces = segments.run(
        [attention_1, up_1], work, (grad, up_low, shared)
    )
    ffn_0 = Reduction(pieces, grid, unit)

    def work(grads, gain_first):
        gains = traded(share_left((gain_rows(gain_first, gain_second),), order), grid)
        return attention_terms(left[0], both(grads, grid), gains, 0, unit)

    segments.join(down_1, up_1)
    pieces = segments.run([ffn_0, attention_1, down_1], work, (grads, gain_first))
    attention_0 = Reduction(pieces, grid, unit)
    segments.run([ffn_0, attention_0, attention_1], pending=[attention_0])
    segments.run([attention_0, ffn_0])
    segments.run([attention_0])

    summed = [reduction.result() for reduction in (ffn_0, down_1)]
    done = attention_1.result()
    *attention, gains = stack_attention([(*attention_0.kept, *attention_0.out), (done,)])
    return (
        hidden.astype(jnp.bfloat16)[None],
        grad[None],
        *attention,
        jnp.stack([value[:, FF:] for value in summed]),
        jnp.stack([value[:, :FF].T for value in summed]),
        jnp.swapaxes(gains[:, :, :2], 1, 2),
    )


def solution(mesh):
    placed = (
        P(("dp", "fsdp"), None, None),
        P(("dp", "fsdp")),
        P(None, ("dp", "fsdp"), None),
        P(None, ("dp", "fsdp"), None),
        P(None, ("dp", "fsdp"), None),
        P(None, ("dp", "fsdp"), None),
        P(None, ("dp", "fsdp"), None),
        P(None, None, ("dp", "fsdp")),
        P(None, None, ("dp", "fsdp")),
        P(("dp", "fsdp"), None, None),
    )
    return jax.shard_map(
        functools.partial(per_device, (mesh.shape["dp"], mesh.shape["fsdp"])),
        mesh=mesh,
        in_specs=placed,
        out_specs=(
            P(("dp", "fsdp"), None, None),
            P(("dp", "fsdp"), None, None),
            P(None, ("dp", "fsdp"), None),
            P(None, ("dp", "fsdp"), None),
            P(None, ("dp", "fsdp"), None),
            P(None, ("dp", "fsdp"), None),
            P(None, ("dp", "fsdp"), None),
            P(None, None, ("dp", "fsdp")),
            P(None, None, ("dp", "fsdp")),
        ),
        check_vma=False,
    )
```

```python
import functools

import jax
import jax.numpy as jnp
from jax import lax
from jax.experimental import pallas as pl
from jax.experimental.pallas import tpu as pltpu
import numpy as np
from jax.sharding import PartitionSpec as P

D = 768
HEADS = 12
HEAD_DIM = 64
FF = 3072
LAYERS = 2
PAD = 128
LIGHT = pl.CostEstimate(flops=1 << 30, bytes_accessed=1 << 22, transcendentals=0)


def norm(value, gain):
    centred = value - jnp.mean(value, axis=-1, keepdims=True)
    spread = jnp.mean(centred * centred, axis=-1, keepdims=True)
    return centred * lax.rsqrt(spread + 1e-05) * gain


def gelu_tanh(value):
    return jax.nn.gelu(value, approximate=True)


def product(left, right):
    return jnp.dot(left, right, preferred_element_type=jnp.float32)


def product_left_t(left, right):
    return lax.dot_general(
        left, right, (((0,), (0,)), ((), ())), preferred_element_type=jnp.float32
    )


def product_right_t(left, right):
    return lax.dot_general(
        left, right, (((1,), (1,)), ((), ())), preferred_element_type=jnp.float32
    )


def pack_attention(shards, layer):
    query_w, key_w, value_w, out_w, _, _, gains = (member[layer] for member in shards)
    gain_columns = jnp.pad(gains.T, ((0, 0), (0, PAD - 2)))
    return jnp.concatenate([query_w, key_w, value_w, out_w, gain_columns], axis=1)


def pack_ffn(shards, layer):
    return jnp.concatenate([shards[4][layer], shards[5][layer].T], axis=1)


def plain_gather(block):
    return lax.all_gather(block, ("dp", "fsdp"), axis=0, tiled=True)


def unpack(attention, ffn):
    return (
        attention[:, : 3 * D],
        attention[:, 3 * D : 4 * D],
        ffn[:, :FF],
        ffn[:, FF:],
        attention[:, 4 * D : 4 * D + 2].T.astype(jnp.float32),
    )


def visible_keys(length, token_count, swap):
    half = token_count // 2
    positions = lax.broadcasted_iota(jnp.int32, (2, half), 0) * half + lax.broadcasted_iota(
        jnp.int32, (2, half), 1
    )
    if swap:
        positions = positions[::-1]
    return positions < length


def split_heads(value):
    return value.reshape(2, value.shape[0] // 2, HEADS, HEAD_DIM)


def paired_heads(query, keys, values, swap):
    query_heads = split_heads(query)
    key_heads = split_heads(keys)
    value_heads = split_heads(values)
    if swap:
        key_heads = key_heads[::-1]
        value_heads = value_heads[::-1]
    return (query_heads, key_heads, value_heads)


def masked_scores(query_heads, key_heads, visible):
    scores = (
        jnp.einsum("bqhd,bkhd->bhqk", query_heads, key_heads, preferred_element_type=jnp.float32)
        * 0.125
    )
    return jnp.where(visible[:, None, None, :], scores, -1e30)


def attend_forward(query, keys, values, visible, swap):
    token_count = query.shape[0]
    query_heads, key_heads, value_heads = paired_heads(query, keys, values, swap)
    scores = masked_scores(query_heads, key_heads, visible)
    highest = jnp.max(scores, axis=-1, keepdims=True)
    raised = jnp.exp(scores - highest)
    total = jnp.sum(raised, axis=-1, keepdims=True)
    shares = (raised / total).astype(jnp.bfloat16)
    mixed = jnp.einsum("bhqk,bkhd->bqhd", shares, value_heads, preferred_element_type=jnp.float32)
    return (mixed.reshape(token_count, -1), highest + jnp.log(total))


def attend_backward(query, keys, values, visible, swap, log_total, grad_mixed):
    token_count = query.shape[0]
    query_heads, key_heads, value_heads = paired_heads(query, keys, values, swap)
    scores = masked_scores(query_heads, key_heads, visible)
    shares = jnp.exp(scores - log_total)
    shares_low = shares.astype(jnp.bfloat16)
    grad_heads = split_heads(grad_mixed)
    grad_values = jnp.einsum(
        "bhqk,bqhd->bkhd", shares_low, grad_heads, preferred_element_type=jnp.float32
    )
    grad_shares = jnp.einsum(
        "bqhd,bkhd->bhqk", grad_heads, value_heads, preferred_element_type=jnp.float32
    )
    inner = jnp.sum(shares * grad_shares, axis=-1, keepdims=True)
    grad_scores = (shares * (grad_shares - inner)).astype(jnp.bfloat16)
    grad_query = (
        jnp.einsum("bhqk,bkhd->bqhd", grad_scores, key_heads, preferred_element_type=jnp.float32)
        * 0.125
    )
    grad_keys = (
        jnp.einsum("bhqk,bqhd->bkhd", grad_scores, query_heads, preferred_element_type=jnp.float32)
        * 0.125
    )
    if swap:
        grad_keys = grad_keys[::-1]
        grad_values = grad_values[::-1]
    return tuple(
        (
            member.reshape(token_count, -1).astype(jnp.bfloat16)
            for member in (grad_query, grad_keys, grad_values)
        )
    )


def layer_forward(hidden, length, weights, swap):
    qkv_w, out_w, up_w, down_t, gains = weights
    inputs_low = hidden.astype(jnp.bfloat16)
    qkv = product(inputs_low, qkv_w).astype(jnp.bfloat16)
    query, keys, values = qkv[:, :D], qkv[:, D : 2 * D], qkv[:, 2 * D :]
    visible = visible_keys(length, hidden.shape[0], swap)
    mixed, log_total = attend_forward(query, keys, values, visible, swap)
    mixed_low = mixed.astype(jnp.bfloat16)
    first_sum = hidden + product(mixed_low, out_w)
    normed = norm(first_sum, gains[0])
    normed_low = normed.astype(jnp.bfloat16)
    expanded = product(normed_low, up_w)
    activated = gelu_tanh(expanded).astype(jnp.bfloat16)
    second_sum = normed + product_right_t(activated, down_t)
    output = norm(second_sum, gains[1])
    kept = (
        inputs_low,
        query,
        keys,
        values,
        log_total,
        mixed_low,
        first_sum,
        normed_low,
        expanded,
        activated,
        second_sum,
    )
    return (output, kept)


def down_backward(grad_output, kept, weights):
    grad_second, grad_gain = jax.vjp(norm, kept[10], weights[4][1])[1](grad_output)
    return (grad_second, grad_second.astype(jnp.bfloat16), grad_gain)


def up_backward(grad_second, down_low, kept, weights):
    grad_active = product(down_low, weights[3])
    up_low = jax.vjp(gelu_tanh, kept[8])[1](grad_active)[0].astype(jnp.bfloat16)
    return (grad_second + product_right_t(up_low, weights[2]), up_low)


def mixed_backward(grad_normed, kept, weights):
    grad_first, grad_gain = jax.vjp(norm, kept[6], weights[4][0])[1](grad_normed)
    attn_low = grad_first.astype(jnp.bfloat16)
    grad_mixed = product_right_t(attn_low, weights[1]).astype(jnp.bfloat16)
    return (grad_first, attn_low, grad_mixed, grad_gain)


def scores_backward(grad_mixed, kept, swapped, length):
    query, keys, values, log_total = kept[1:5]
    visible = visible_keys(length, query.shape[0], swapped)
    return jnp.concatenate(
        attend_backward(query, keys, values, visible, swapped, log_total, grad_mixed), axis=1
    )


def inputs_backward(grad_first, grad_qkv, weights):
    return grad_first + product_right_t(grad_qkv, weights[0])


def plain_scatter(terms):
    return lax.psum_scatter(
        terms.astype(jnp.bfloat16), ("dp", "fsdp"), scatter_dimension=0, tiled=True
    ).astype(jnp.float32)


def plain_ffn_terms(operands):
    normed_low, up_low, down_low, activated = operands
    return jnp.concatenate(
        [
            product_left_t(normed_low, up_low).astype(jnp.bfloat16),
            product_left_t(down_low, activated).astype(jnp.bfloat16),
        ],
        axis=1,
    )


def plain_attention_terms(operands, gains):
    inputs_low, grad_qkv, mixed_low, attn_low = operands
    return jnp.concatenate(
        [
            product_left_t(inputs_low, grad_qkv).astype(jnp.bfloat16),
            product_left_t(mixed_low, attn_low).astype(jnp.bfloat16),
            jnp.pad(gains.T, ((0, 0), (0, PAD - 2))).astype(jnp.bfloat16),
        ],
        axis=1,
    )


def attention_outputs(summed):
    return (
        *(summed[:, j * D : (j + 1) * D] for j in range(4)),
        summed[:, 4 * D : 4 * D + 2].T,
    )


def ffn_outputs(summed):
    return (summed[:, :FF], summed[:, FF:].T)


class Grid:
    def __init__(self):
        places = [
            (x, core, z, y) for x in range(2) for core in range(2) for z in range(4) for y in range(2)
        ]
        number = {place: index for index, place in enumerate(places)}

        def route(move, senders=range(4)):
            return [
                (number[place], number[move(*place)]) for place in places if place[2] in senders
            ]

        self.core = route(lambda x, core, z, y: (x, 1 - core, z, y))
        self.first = route(
            lambda x, core, z, y: (x, core, z, 1 - y) if core else (1 - x, core, z, y)
        )
        self.second = route(
            lambda x, core, z, y: (1 - x, core, z, y) if core else (x, core, z, 1 - y)
        )
        self.pair = route(lambda x, core, z, y: (x, core, z ^ 1, y))
        self.middle = route(lambda x, core, z, y: (x, core, 3 - z, y), (1, 2))
        self.outward = route(lambda x, core, z, y: (x, core, z ^ 1, y), (1, 2))
        self.line = [route(lambda x, core, z, y, s=s: (x, core, z ^ s, y)) for s in (1, 2, 3)]


def swap(value, route):
    return lax.ppermute(value, ("dp", "fsdp"), route)


SLOTS = np.array([(far, near, s) for far, near in ((1, 1), (1, 0), (0, 1), (0, 0)) for s in range(4)])
ROWS = tuple((j, j + 2) for j in range(0, 16, 2))
TERM_SLOTS = SLOTS[[0, 1, 4, 5, 2, 3, 10, 11, 6, 7, 8, 9, 12, 13, 14, 15]]
TERM_ROWS = ((0, 4), (4, 8), (8, 10), (10, 12), (12, 16))


def slot_rows(slots, place, x, y, owner):
    first, second = (jnp.asarray(slots[:, j], jnp.int32) for j in range(2))
    along_x = jnp.where(owner == 0, first, second)
    along_y = jnp.where(owner == 0, second, first)
    return (((x ^ along_x) * 2 + owner) * 4 + place) * 2 + (y ^ along_y)


def row_order(unit):
    dp, fsdp = lax.axis_index("dp"), lax.axis_index("fsdp")
    x, core, z, y = dp // 2, dp % 2, fsdp // 2, fsdp % 2
    slots = np.repeat(TERM_SLOTS, unit, axis=0)
    place = z ^ jnp.asarray(slots[:, 2], jnp.int32)
    offset = jnp.asarray(np.tile(np.arange(unit), 16), jnp.int32)
    rows = jnp.concatenate(
        [slot_rows(slots, place, x, y, owner) * unit + offset for owner in (core, 1 - core)]
    )
    natural = lax.broadcasted_iota(jnp.int32, (32 * unit, 32 * unit), 0)
    return (natural == rows[None]).astype(jnp.bfloat16)


def share_left(values, order):
    lengths = [max(value.shape[0], PAD) for value in values]
    half = D // 2

    def body(order_ref, *refs):
        mine, other = refs[len(values) :]
        start = 0
        for length, value_ref in zip(lengths, refs):
            ordered = dot(value_ref[...].astype(jnp.bfloat16), order_ref[...])
            short = length - ordered.shape[0]
            if short:
                ordered = jnp.concatenate([ordered, jnp.zeros((short, D), jnp.float32)], axis=0)
            turned = ordered.T.astype(jnp.bfloat16)
            mine[:, start : start + length] = turned[:half]
            other[:, start : start + length] = turned[half:]
            start += length

    return pl.pallas_call(
        body,
        in_specs=[VMEM_SPEC] * (1 + len(values)),
        out_specs=[VMEM_SPEC] * 2,
        out_shape=shapes(*[((half, sum(lengths)), jnp.bfloat16)] * 2),
        cost_estimate=LIGHT,
        compiler_params=params(8),
    )(order, *values)


def both(value, grid):
    return (value, swap(value, grid.core))


def traded(pair, grid):
    return (pair[0], swap(pair[1], grid.core))


def dot(left, right):
    return jnp.dot(left, right, preferred_element_type=jnp.float32)


def dot_nt(left, right):
    return lax.dot_general(
        left, right, (((1,), (1,)), ((), ())), preferred_element_type=jnp.float32
    )


def dot_tn(left, right):
    return lax.dot_general(
        left, right, (((0,), (0,)), ((), ())), preferred_element_type=jnp.float32
    )


def lane_masks():
    lane = lax.broadcasted_iota(jnp.int32, (1, 2 * HEAD_DIM), 1)
    first = (lane < HEAD_DIM).astype(jnp.float32)
    return first.astype(jnp.bfloat16), (1.0 - first).astype(jnp.bfloat16), lane < HEAD_DIM


def two_heads(value, masks):
    return jnp.concatenate([value * masks[0], value * masks[1]], axis=0)


def pair_softmax(query_pair, keys, key_block, length):
    scores = dot_nt(keys, query_pair) * 0.125
    position = lax.broadcasted_iota(jnp.int32, scores.shape, 0) + key_block * keys.shape[0]
    scores = jnp.where(position < length, scores, -1e30)
    raised = jnp.exp(scores - jnp.max(scores, axis=0, keepdims=True))
    return raised / jnp.sum(raised, axis=0, keepdims=True)


def normalised(value):
    centred = value - jnp.mean(value, axis=-1, keepdims=True)
    rate = lax.rsqrt(jnp.mean(centred * centred, axis=-1, keepdims=True) + 1e-05)
    return centred * rate, rate


def norm_backward(value, gain, grad):
    ratio, rate = normalised(value)
    scaled = grad * gain
    slope = jnp.mean(scaled * ratio, axis=-1, keepdims=True)
    result = rate * (scaled - jnp.mean(scaled, axis=-1, keepdims=True) - ratio * slope)
    return result, jnp.sum(grad * ratio, axis=0, keepdims=True)


def head_parts(half, swapped):
    for block in range(2):
        key_block = 1 - block if swapped else block
        rows = slice(block * half, (block + 1) * half)
        key_rows = slice(key_block * half, (key_block + 1) * half)
        for pair in range(HEADS // 2):
            yield key_block, rows, key_rows, pair * 2 * HEAD_DIM


VMEM_SPEC = pl.BlockSpec(memory_space=pltpu.VMEM)
SMEM_SPEC = pl.BlockSpec(memory_space=pltpu.SMEM)
ANY_SPEC = pl.BlockSpec(memory_space=pl.ANY)


def params(mebibytes):
    return pltpu.CompilerParams(vmem_limit_bytes=mebibytes << 20)


def shapes(*pairs):
    return [jax.ShapeDtypeStruct(shape, dtype) for shape, dtype in pairs]


def attention_columns(weights, start, target, sems):
    copies = []
    for part in range(5):
        width = D if part < 4 else PAD
        copies.append(
            pltpu.make_async_copy(
                weights.at[:, pl.ds(start + part * D, width)],
                target.at[:, pl.ds(part * D, width)],
                sems.at[part],
            )
        )
    for copy in copies:
        copy.start()
    return copies


def attention_forward(hidden, lengths, weights, start, swapped):
    tokens = hidden.shape[0]
    half = tokens // 2
    low = jnp.bfloat16

    def body(length_ref, hidden_ref, w_any, low_out, qkv, mixed, first_sum, gains, w, sems):
        copies = attention_columns(w_any, start, w, sems)
        value = hidden_ref[...].astype(low)
        low_out[...] = value
        masks = lane_masks()
        for part in range(3):
            copies[part].wait()
            columns = slice(part * D, (part + 1) * D)
            qkv[:, columns] = dot(value, w[:, columns]).astype(low)
        for key_block, rows, key_rows, lane in head_parts(half, swapped):
            query = two_heads(qkv[rows, lane : lane + 128], masks)
            keys = qkv[key_rows, D + lane : D + lane + 128]
            values = qkv[key_rows, 2 * D + lane : 2 * D + lane + 128]
            shares = pair_softmax(query, keys, key_block, length_ref[0]).astype(low)
            out = dot_tn(shares, values)
            mixed[rows, lane : lane + 128] = jnp.where(masks[2], out[:half], out[half:]).astype(low)
        copies[3].wait()
        first_sum[...] = hidden_ref[...] + dot(mixed[...], w[:, 3 * D : 4 * D])
        copies[4].wait()
        gains[...] = w[:, 4 * D :].astype(jnp.float32).T[:8]

    return pl.pallas_call(
        body,
        in_specs=[SMEM_SPEC, VMEM_SPEC, ANY_SPEC],
        out_specs=[VMEM_SPEC] * 5,
        out_shape=shapes(
            ((tokens, D), low),
            ((tokens, 3 * D), low),
            ((tokens, D), low),
            ((tokens, D), jnp.float32),
            ((8, D), jnp.float32),
        ),
        scratch_shapes=[pltpu.VMEM((D, 4 * D + PAD), low), pltpu.SemaphoreType.DMA((5,))],
        cost_estimate=LIGHT,
        compiler_params=params(14),
    )(lengths, hidden, weights)


FF_TILE = D


def ffn_forward(first_sum, gains, weights, start):
    tokens = first_sum.shape[0]
    low = jnp.bfloat16
    steps = FF // FF_TILE
    first = start // FF_TILE

    def body(sum_ref, gain_ref, up, down, normed_low, activated, slope, second_sum, out, total):
        step = pl.program_id(0)

        @pl.when(step == 0)
        def _():
            normed = normalised(sum_ref[...])[0] * gain_ref[0:1]
            normed_low[...] = normed.astype(low)
            total[...] = normed

        u = dot(normed_low[...], up[...])
        inner = 0.7978845608028654 * (u + 0.044715 * (u * u * u))
        wave = jnp.tanh(inner)
        active = (0.5 * u * (1.0 + wave)).astype(low)
        slope[...] = (
            0.5 * (1.0 + wave)
            + 0.5 * u * (1.0 - wave * wave) * (0.7978845608028654 * (1.0 + 0.134145 * (u * u)))
        ).astype(low)
        activated[...] = active
        total[...] += dot_nt(active, down[...])

        @pl.when(step == steps - 1)
        def _():
            second_sum[...] = total[...]
            out[...] = normalised(total[...])[0] * gain_ref[1:2]

    def fixed(shape):
        return pl.BlockSpec(shape, lambda j: (0, 0))

    wide = pl.BlockSpec((tokens, FF_TILE), lambda j: (0, j))
    return pl.pallas_call(
        body,
        grid=(steps,),
        in_specs=[
            fixed((tokens, D)),
            fixed((8, D)),
            pl.BlockSpec((D, FF_TILE), lambda j: (0, first + j)),
            pl.BlockSpec((D, FF_TILE), lambda j: (0, first + steps + j)),
        ],
        out_specs=[fixed((tokens, D)), wide, wide, fixed((tokens, D)), fixed((tokens, D))],
        out_shape=shapes(
            ((tokens, D), low),
            ((tokens, FF), low),
            ((tokens, FF), low),
            ((tokens, D), jnp.float32),
            ((tokens, D), jnp.float32),
        ),
        scratch_shapes=[pltpu.VMEM((tokens, D), jnp.float32)],
        cost_estimate=LIGHT,
        compiler_params=params(16),
    )(first_sum, gains, weights, weights)


def second_norm_backward(grad, second_sum, gains):
    tokens = grad.shape[0]

    def body(grad_ref, sum_ref, gain_ref, out, low_out, gain_out):
        result, gain_grad = norm_backward(sum_ref[...], gain_ref[1:2], grad_ref[...].astype(jnp.float32))
        out[...] = result
        low_out[...] = result.astype(jnp.bfloat16)
        gain_out[...] = gain_grad

    return pl.pallas_call(
        body,
        in_specs=[VMEM_SPEC] * 3,
        out_specs=[VMEM_SPEC] * 3,
        out_shape=shapes(
            ((tokens, D), jnp.float32), ((tokens, D), jnp.bfloat16), ((1, D), jnp.float32)
        ),
        cost_estimate=LIGHT,
        compiler_params=params(6),
    )(grad, second_sum, gains)


def up_backward_kernel(grad_second, down_low, slope, weights, start):
    tokens = grad_second.shape[0]
    low = jnp.bfloat16
    steps = FF // FF_TILE
    first = start // FF_TILE

    def body(grad_ref, low_ref, slope_ref, up, down, up_low, out):
        step = pl.program_id(0)

        @pl.when(step == 0)
        def _():
            out[...] = grad_ref[...]

        piece = (dot(low_ref[...], down[...]) * slope_ref[...].astype(jnp.float32)).astype(low)
        up_low[...] = piece
        out[...] += dot_nt(piece, up[...])

    def fixed(shape):
        return pl.BlockSpec(shape, lambda j: (0, 0))

    wide = pl.BlockSpec((tokens, FF_TILE), lambda j: (0, j))
    return pl.pallas_call(
        body,
        grid=(steps,),
        in_specs=[
            fixed((tokens, D)),
            fixed((tokens, D)),
            wide,
            pl.BlockSpec((D, FF_TILE), lambda j: (0, first + j)),
            pl.BlockSpec((D, FF_TILE), lambda j: (0, first + steps + j)),
        ],
        out_specs=[wide, fixed((tokens, D))],
        out_shape=shapes(((tokens, FF), low), ((tokens, D), jnp.float32)),
        cost_estimate=LIGHT,
        compiler_params=params(12),
    )(grad_second, down_low, slope, weights, weights)


def attention_backward_kernel(grad, first_sum, gains, qkv, lengths, weights, start, swapped):
    tokens = grad.shape[0]
    half = tokens // 2
    low = jnp.bfloat16

    def body(length_ref, grad_ref, sum_ref, gain_ref, qkv_ref, w_any, *rest):
        grads, grad_in, gain_out, grad_mixed, w, sems = rest
        copies = attention_columns(w_any, start, w, sems)
        masks = lane_masks()
        result, gain_grad = norm_backward(sum_ref[...], gain_ref[0:1], grad_ref[...])
        grad_in[...] = result
        grads[:, 3 * D :] = result.astype(low)
        gain_out[...] = gain_grad
        copies[3].wait()
        grad_mixed[...] = dot_nt(grads[:, 3 * D :], w[:, 3 * D : 4 * D]).astype(low)
        for key_block, rows, key_rows, lane in head_parts(half, swapped):
            query = two_heads(qkv_ref[rows, lane : lane + 128], masks)
            keys = qkv_ref[key_rows, D + lane : D + lane + 128]
            values = qkv_ref[key_rows, 2 * D + lane : 2 * D + lane + 128]
            arriving = two_heads(grad_mixed[rows, lane : lane + 128], masks)
            shares = pair_softmax(query, keys, key_block, length_ref[0])
            grad_values = dot(shares.astype(low), arriving)
            grad_shares = dot_nt(values, arriving)
            inner = jnp.sum(shares * grad_shares, axis=0, keepdims=True)
            grad_scores = (shares * (grad_shares - inner)).astype(low)
            grad_query = dot_tn(grad_scores, keys) * 0.125
            grad_keys = dot(grad_scores, query) * 0.125
            grads[rows, lane : lane + 128] = jnp.where(
                masks[2], grad_query[:half], grad_query[half:]
            ).astype(low)
            grads[key_rows, D + lane : D + lane + 128] = grad_keys.astype(low)
            grads[key_rows, 2 * D + lane : 2 * D + lane + 128] = grad_values.astype(low)
        for part in (0, 1, 2):
            copies[part].wait()
            columns = slice(part * D, (part + 1) * D)
            grad_in[...] += dot_nt(grads[:, columns], w[:, columns])
        copies[4].wait()

    return pl.pallas_call(
        body,
        in_specs=[SMEM_SPEC] + [VMEM_SPEC] * 4 + [ANY_SPEC],
        out_specs=[VMEM_SPEC] * 3,
        out_shape=shapes(
            ((tokens, 4 * D), low),
            ((tokens, D), jnp.float32),
            ((1, D), jnp.float32),
        ),
        scratch_shapes=[
            pltpu.VMEM((tokens, D), low),
            pltpu.VMEM((D, 4 * D + PAD), low),
            pltpu.SemaphoreType.DMA((5,)),
        ],
        cost_estimate=LIGHT,
        compiler_params=params(16),
    )(lengths, grad, first_sum, gains, qkv, weights)


def matrix_terms(products, unit):
    tile = D
    tokens, width = products[0][2][0].shape
    steps = width // tile

    def body(*refs):
        outs = refs[starts[-1] :]
        for j in range(len(products)):
            la, lb, ra, *received = refs[starts[j] : starts[j + 1]]
            for step in range(steps if len(received) > 1 else 1):
                rb = received[step]
                place = pl.program_id(0) - j * steps
                here = place == step if len(received) > 1 else place // steps == 0

                @pl.when(here)
                def _(la=la, lb=lb, ra=ra, rb=rb):
                    value = (dot(la[...], ra[...]) + dot(lb[...], rb[...])).astype(jnp.bfloat16)
                    for (low, high), out in zip(TERM_ROWS, outs):
                        out[...] = value[low * unit : high * unit]

    in_specs, operands, starts = [], [], [0]
    for j, (left, part, right) in enumerate(products):
        block = pl.BlockSpec((16 * unit, tokens), lambda i, part=part: (0, part))
        column = pl.BlockSpec(
            (tokens, tile), lambda i, j=j: (0, jnp.clip(i - j * steps, 0, steps - 1))
        )
        own, received = right
        if isinstance(received, list):
            whole = pl.BlockSpec((tokens, tile), lambda i: (0, 0))
            in_specs += [block, block, column] + [whole] * steps
            operands += [*left, own, *received]
        else:
            in_specs += [block, block, column, column]
            operands += [*left, own, received]
        starts.append(len(operands))
    wide = width * len(products)
    return pl.pallas_call(
        body,
        grid=(wide // tile,),
        in_specs=in_specs,
        out_specs=[pl.BlockSpec(((b - a) * unit, tile), lambda i: (0, i)) for a, b in TERM_ROWS],
        out_shape=shapes(*((((b - a) * unit, wide), jnp.bfloat16) for a, b in TERM_ROWS)),
        cost_estimate=LIGHT,
        compiler_params=params(10),
    )(*operands)


def attention_terms(left, grads, gains, start, unit):
    tokens = grads[0].shape[0]

    def body(la, lb, ra, rb, ga, gb, *outs):
        def put(value, column):
            value = value.astype(jnp.bfloat16)
            for (low, high), out in zip(TERM_ROWS, outs):
                out[:, column : column + value.shape[1]] = value[low * unit : high * unit]

        for j in range(4):
            part = slice(j * D, (j + 1) * D)
            from_left = slice(0, tokens) if j < 3 else slice(tokens, 2 * tokens)
            put(
                dot(la[:, from_left], ra[:, part]) + dot(lb[:, from_left], rb[:, part]),
                j * D,
            )
        gain = slice(start, start + PAD)
        put(ga[:, gain].astype(jnp.float32) + gb[:, gain].astype(jnp.float32), 4 * D)

    return pl.pallas_call(
        body,
        in_specs=[VMEM_SPEC] * 6,
        out_specs=[VMEM_SPEC] * 5,
        out_shape=shapes(*((((b - a) * unit, 4 * D + PAD), jnp.bfloat16) for a, b in TERM_ROWS)),
        cost_estimate=LIGHT,
        compiler_params=params(12),
    )(*left, *grads, *gains)


def square_sums(came_first, came_second, later_first, later_second):
    rows, width = later_first.shape

    def body(one, other, first, second, first_out, second_out):
        first_out[...] = add(first[...], other[:rows]).astype(jnp.bfloat16)
        second_out[...] = add(second[...], one[:rows]).astype(jnp.bfloat16)

    return pl.pallas_call(
        body,
        in_specs=[VMEM_SPEC] * 4,
        out_specs=[VMEM_SPEC] * 2,
        out_shape=shapes(*[((rows, width), jnp.bfloat16)] * 2),
        cost_estimate=LIGHT,
        compiler_params=params(8),
    )(came_first, came_second, later_first, later_second)


def line_sums(groups, unit):
    two = 2 * unit
    widths = [group[0].shape[1] for group in groups]

    def body(*refs):
        outs = refs[5 * len(groups) :]
        start = 0
        for j, width in enumerate(widths):
            own, one, other, last_first, last_second = refs[5 * j : 5 * j + 5]
            columns = slice(start, start + width)
            near = add(own[:two], one[two:], last_second[...])
            far = add(own[two:], other[two:], last_first[...])
            outs[0][:, columns] = near[:unit]
            outs[1][:, columns] = near[unit:].astype(jnp.bfloat16)
            outs[2][:, columns] = far[:unit].astype(jnp.bfloat16)
            outs[3][:, columns] = far[unit:].astype(jnp.bfloat16)
            start += width

    low = ((unit, sum(widths)), jnp.bfloat16)
    return pl.pallas_call(
        body,
        in_specs=[VMEM_SPEC] * (5 * len(groups)),
        out_specs=[VMEM_SPEC] * 4,
        out_shape=shapes(((unit, sum(widths)), jnp.float32), low, low, low),
        cost_estimate=LIGHT,
        compiler_params=params(14),
    )(*(value for group in groups for value in group))


def stack_attention(layers):
    rows, width = layers[0][0].shape
    starts = [0]
    for layer in layers:
        starts.append(starts[-1] + len(layer))

    def body(*refs):
        outs = refs[starts[-1] :]
        for layer in range(len(layers)):
            total = add(*(ref[...] for ref in refs[starts[layer] : starts[layer + 1]]))
            for j, out in enumerate(outs):
                out[layer] = total[:, j * D : min((j + 1) * D, width)]

    return pl.pallas_call(
        body,
        in_specs=[VMEM_SPEC] * starts[-1],
        out_specs=[VMEM_SPEC] * 5,
        out_shape=shapes(
            *[((len(layers), rows, D), jnp.float32)] * 4,
            ((len(layers), rows, PAD), jnp.float32),
        ),
        cost_estimate=LIGHT,
        compiler_params=params(8),
    )(*(value for layer in layers for value in layer))


def add(*values):
    return sum(value.astype(jnp.float32) for value in values)


class Reduction:
    def __init__(self, pieces, grid, unit):
        self.grid, self.unit, self.round, self.joined = grid, unit, 0, False
        self.out, self.kept = list(pieces[:2]), list(pieces[2:])

    def state(self, pending):
        return ([] if pending else self.out, self.kept)

    def restore(self, state):
        out, self.kept = state
        self.out = out or self.out

    def send(self):
        grid = self.grid
        routes = grid.line if self.round == 2 else (grid.first, grid.second)
        self.out = [swap(value, route) for value, route in zip(self.out, routes)]
        self.round += 1

    def prepare(self):
        if self.round == 1:
            later_first, later_second, own = self.kept
            self.kept = [own, *self.out]
            self.out = list(square_sums(*self.out, later_first, later_second))
        elif not self.joined:
            self.join()

    def join(self, *others):
        groups = [(*reduction.kept, *reduction.out) for reduction in (self, *others)]
        own, *self.out = line_sums(groups, self.unit)
        self.kept, self.joined = [own], True

    def result(self):
        return add(self.kept[0], *self.out)


def gate(values, *earlier):
    return lax.optimization_barrier((values, earlier))[0]


class Segments:
    def __init__(self):
        self.active = []

    def join(self, reduction, *others):
        reduction.join(*others)
        self.active = [r for r in self.active if r not in others]

    def run(self, sends, compute=None, values=(), pending=()):
        for reduction in sends:
            if reduction not in self.active:
                self.active.append(reduction)
            if reduction.round:
                reduction.prepare()
            reduction.send()
        if compute:
            values = compute(*values)
        states = [reduction.state(reduction in pending) for reduction in self.active]
        states, values = lax.optimization_barrier((states, values))
        for reduction, state in zip(self.active, states):
            reduction.restore(state)
        self.active = [r for r in self.active if r.round < 3 or r in pending]
        return values


class Gathering:
    def __init__(self, block, grid):
        self.pieces, self.grid, self.unit = [block], grid, block.shape[0]
        self.steps = [self.pair, self.middle, self.outward, self.square, self.diagonal]

    def advance(self):
        self.pieces = list(self.steps.pop(0)(self.pieces, self.grid, 2 * self.unit))

    @staticmethod
    def pair(pieces, grid, two):
        (block,) = pieces
        return (jnp.concatenate([block, swap(block, grid.pair)], axis=0),)

    @staticmethod
    def middle(pieces, grid, two):
        (near,) = pieces
        return (near, swap(near, grid.middle))

    @staticmethod
    def outward(pieces, grid, two):
        near, far = pieces
        z = lax.axis_index("fsdp") // 2
        return (near, jnp.where((z == 1) | (z == 2), far, swap(far, grid.outward)))

    @staticmethod
    def square(pieces, grid, two):
        near, far = pieces
        return (
            swap(far, grid.first),
            swap(near, grid.second),
            swap(near, grid.first),
            swap(far, grid.second),
            near,
            far,
        )

    @staticmethod
    def diagonal(pieces, grid, two):
        first_far, second_near, first_near, second_far, near, far = pieces
        return (
            swap(second_near, grid.first),
            swap(first_far, grid.second),
            first_near,
            first_far,
            second_near,
            second_far,
            near,
            far,
        )

    def result(self):
        pieces = self.pieces
        return place_blocks(pieces + [swap(piece, self.grid.core) for piece in pieces], self.unit)


def place_blocks(pieces, unit):
    width = pieces[0].shape[1]
    dp, fsdp = lax.axis_index("dp"), lax.axis_index("fsdp")
    x, core, z, y = dp // 2, dp % 2, fsdp // 2, fsdp % 2
    s = jnp.asarray(SLOTS[:, 2], jnp.int32)
    place = jnp.where(s < 2, z ^ s, jnp.where(z < 2, s, 3 - s))
    rows = jnp.concatenate([slot_rows(SLOTS, place, x, y, owner) for owner in (core, 1 - core)])
    tiles = unit // 8

    def body(rows_ref, *refs):
        sources, target = refs[:16], refs[16]
        for half in range(2):
            for (low, high), source in zip(ROWS, sources[half * 8 : half * 8 + 8]):
                for slot in range(low, high):
                    row = rows_ref[half * 16 + slot] * tiles
                    first = (slot - low) * tiles
                    target[pl.ds(row, tiles)] = source[first : first + tiles]

    placed = pl.pallas_call(
        body,
        in_specs=[pl.BlockSpec(memory_space=pltpu.SMEM)]
        + [pl.BlockSpec(memory_space=pltpu.VMEM)] * 16,
        out_specs=pl.BlockSpec(memory_space=pltpu.VMEM),
        out_shape=jax.ShapeDtypeStruct((32 * tiles, 8, width), jnp.bfloat16),
        cost_estimate=LIGHT,
        compiler_params=params(22),
    )(rows, *(piece.reshape(-1, 8, width) for piece in pieces))
    return placed.reshape(32 * unit, width)


def per_device(
    sizes,
    tokens,
    lengths,
    query_weight,
    key_weight,
    value_weight,
    attn_out_weight,
    up_weight,
    down_weight,
    norm_gains,
    cotangent,
):
    shards = (
        query_weight,
        key_weight,
        value_weight,
        attn_out_weight,
        up_weight,
        down_weight,
        norm_gains,
    )
    if sizes == (4, 8):
        return grid_step(tokens, lengths, shards, cotangent)
    hidden = tokens[0].astype(jnp.float32)
    length = lengths[0]
    weights_all = [
        unpack(plain_gather(pack_attention(shards, j)), plain_gather(pack_ffn(shards, j)))
        for j in range(LAYERS)
    ]
    kept_all = []
    for layer in range(LAYERS):
        hidden, kept = layer_forward(hidden, length, weights_all[layer], layer % 2 == 1)
        kept_all.append(kept)
    grad = cotangent[0].astype(jnp.float32)
    outputs = [None] * LAYERS
    for layer in reversed(range(LAYERS)):
        kept, weights = kept_all[layer], weights_all[layer]
        grad_second, down_low, gain_second = down_backward(grad, kept, weights)
        grad_normed, up_low = up_backward(grad_second, down_low, kept, weights)
        ffn = plain_scatter(plain_ffn_terms((kept[7], up_low, down_low, kept[9])))
        grad_first, attn_low, grad_mixed, gain_first = mixed_backward(grad_normed, kept, weights)
        grad_qkv = scores_backward(grad_mixed, kept, layer % 2 == 1, length)
        grad = inputs_backward(grad_first, grad_qkv, weights)
        gains = jnp.stack([gain_first, gain_second])
        attention = plain_scatter(
            plain_attention_terms((kept[0], grad_qkv, kept[5], attn_low), gains)
        )
        outputs[layer] = (attention_outputs(attention), ffn_outputs(ffn))
    return finish(hidden, grad, outputs)


def finish(hidden, grad, outputs):
    layers = [(*attention[:4], *ffn, attention[4]) for attention, ffn in outputs]
    stacked = tuple((jnp.stack([entry[member] for entry in layers]) for member in range(7)))
    return (hidden.astype(jnp.bfloat16)[None], grad[None], *stacked)


def gather_first_layer(blocks, second, order, grid, attend):
    attention, ffn = (Gathering(block, grid) for block in blocks)

    def hold(*gatherings):
        pieces = [g.pieces[:2] if len(g.pieces) == 6 else g.pieces for g in gatherings]
        pieces = lax.optimization_barrier(pieces)
        for g, held in zip(gatherings, pieces):
            g.pieces = [*held, *g.pieces[len(held) :]]

    attention.advance()
    hold(attention)
    ffn.pieces = gate(ffn.pieces, attention.pieces)
    attention.advance()
    ffn.advance()
    hold(attention, ffn)
    attention.advance()
    ffn.advance()
    order, ffn.pieces = lax.optimization_barrier((order, ffn.pieces))
    hold(attention, ffn)
    attention.advance()
    ffn.advance()
    hold(attention, ffn)
    attention.advance()
    ffn.pieces = gate(ffn.pieces, attention.pieces[3])
    ffn.advance()
    hold(attention)
    weights = attention.result()
    attended = attend(weights)
    held, attended = lax.optimization_barrier((ffn.pieces[:2], attended))
    ffn.pieces = [*held, *ffn.pieces[2:]]
    ffn.advance()
    held, second = lax.optimization_barrier((ffn.pieces[7:], second))
    ffn.pieces = [*ffn.pieces[:7], *held]
    return weights, ffn.result(), second, order, attended


def grid_step(tokens, lengths, shards, cotangent):
    grid, unit = Grid(), shards[0].shape[1]
    order = row_order(unit)
    hidden = tokens[0].astype(jnp.float32)

    second = plain_gather(
        jnp.concatenate([pack_ffn(shards, 1), pack_attention(shards, 1)], axis=1)
    )

    def attend(weights):
        return attention_forward(hidden, lengths, weights, 0, False)

    attention, ffn, second, order, attended = gather_first_layer(
        (pack_attention(shards, 0), pack_ffn(shards, 0)), second, order, grid, attend
    )
    attention_at = ((attention, 0, False), (second, 2 * FF, True))
    ffn_at = ((ffn, 0), (second, 0))

    kept, left, right = [], [], []
    for layer in range(LAYERS):
        if layer:
            attended = attention_forward(hidden, lengths, *attention_at[layer])
        inputs_low, qkv, mixed, first_sum, gains = attended
        normed_low, activated, slope, second_sum, hidden = ffn_forward(
            first_sum, gains, *ffn_at[layer]
        )
        kept.append((qkv, first_sum, gains, slope, second_sum))
        left.append(traded(share_left((inputs_low, mixed, normed_low), order), grid))
        right.append(both(activated, grid))

    def norm_part(layer, grad):
        return second_norm_backward(grad, kept[layer][4], kept[layer][2])

    def up_part(layer, grad_second, down_low):
        up_low, grad = up_backward_kernel(grad_second, down_low, kept[layer][3], *ffn_at[layer])
        return grad, up_low

    def attention_part(layer, grad):
        qkv, first_sum, gains = kept[layer][:3]
        return attention_backward_kernel(
            grad, first_sum, gains, qkv, lengths, *attention_at[layer]
        )

    def gain_rows(first, second):
        return jnp.concatenate([first, second, jnp.zeros((6, D), jnp.float32)], axis=0)

    def up_product(layer, up_low):
        return left[layer], 2, both(up_low, grid)

    def up_product_in_tiles(layer, up_low):
        received = [swap(up_low[:, j : j + D], grid.core) for j in range(0, FF, D)]
        return left[layer], 2, (up_low, received)

    segments = Segments()
    grad_second, down_low, gain_second = norm_part(1, cotangent[0])
    down_t = traded(share_left((down_low,), order), grid)
    pieces = matrix_terms([(down_t, 0, right[1])], unit)
    grad_second, down_low, pieces = lax.optimization_barrier((grad_second, down_low, pieces))
    down_1 = Reduction(pieces, grid, unit)

    def work(grad_second, down_low):
        grad, up_low = up_part(1, grad_second, down_low)
        pieces = matrix_terms([up_product_in_tiles(1, up_low)], unit)
        return attention_part(1, grad), pieces

    (grads, grad, gain_first), pieces = segments.run([down_1], work, (grad_second, down_low))
    up_1 = Reduction(pieces, grid, unit)
    gains_1 = gain_rows(gain_first, gain_second)

    def work(grad, grads, gains):
        grads = both(grads, grid)
        grad_second, down_low, gain_second = norm_part(0, grad)
        shared = traded(share_left((down_low, gains), order), grid)
        grad, up_low = up_part(0, grad_second, down_low)
        pieces = attention_terms(left[1], grads, shared, grads[0].shape[0], unit)
        return grad, up_low, gain_second, shared, pieces

    grad, up_low, gain_second, shared, pieces = segments.run(
        [up_1, down_1], work, (grad, grads, gains_1)
    )
    attention_1 = Reduction(pieces, grid, unit)

    def work(grad, up_low, shared):
        pieces = matrix_terms([(shared, 0, right[0]), up_product(0, up_low)], unit)
        return attention_part(0, grad), pieces

    (grads, grad, gain_first), pieces = segments.run(
        [attention_1, up_1], work, (grad, up_low, shared)
    )
    ffn_0 = Reduction(pieces, grid, unit)

    def work(grads, gain_first):
        gains = traded(share_left((gain_rows(gain_first, gain_second),), order), grid)
        return attention_terms(left[0], both(grads, grid), gains, 0, unit)

    segments.join(down_1, up_1)
    pieces = segments.run([ffn_0, attention_1, down_1], work, (grads, gain_first))
    attention_0 = Reduction(pieces, grid, unit)
    segments.run([ffn_0, attention_0, attention_1], pending=[attention_0])
    segments.run([attention_0, ffn_0])
    segments.run([attention_0])

    summed = [reduction.result() for reduction in (ffn_0, down_1)]
    done = attention_1.result()
    *attention, gains = stack_attention([(*attention_0.kept, *attention_0.out), (done,)])
    return (
        hidden.astype(jnp.bfloat16)[None],
        grad[None],
        *attention,
        jnp.stack([value[:, FF:] for value in summed]),
        jnp.stack([value[:, :FF].T for value in summed]),
        jnp.swapaxes(gains[:, :, :2], 1, 2),
    )


def solution(mesh):
    placed = (
        P(("dp", "fsdp"), None, None),
        P(("dp", "fsdp")),
        P(None, ("dp", "fsdp"), None),
        P(None, ("dp", "fsdp"), None),
        P(None, ("dp", "fsdp"), None),
        P(None, ("dp", "fsdp"), None),
        P(None, ("dp", "fsdp"), None),
        P(None, None, ("dp", "fsdp")),
        P(None, None, ("dp", "fsdp")),
        P(("dp", "fsdp"), None, None),
    )
    return jax.shard_map(
        functools.partial(per_device, (mesh.shape["dp"], mesh.shape["fsdp"])),
        mesh=mesh,
        in_specs=placed,
        out_specs=(
            P(("dp", "fsdp"), None, None),
            P(("dp", "fsdp"), None, None),
            P(None, ("dp", "fsdp"), None),
            P(None, ("dp", "fsdp"), None),
            P(None, ("dp", "fsdp"), None),
            P(None, ("dp", "fsdp"), None),
            P(None, ("dp", "fsdp"), None),
            P(None, None, ("dp", "fsdp")),
            P(None, None, ("dp", "fsdp")),
        ),
        check_vma=False,
    )
```

```python
import functools

import jax
import jax.numpy as jnp
from jax import lax
from jax.experimental import pallas as pl
from jax.experimental.pallas import tpu as pltpu
import numpy as np
from jax.sharding import PartitionSpec as P

D = 768
HEADS = 12
HEAD_DIM = 64
FF = 3072
LAYERS = 2
PAD = 128
LIGHT = pl.CostEstimate(flops=1 << 30, bytes_accessed=1 << 22, transcendentals=0)


def norm(value, gain):
    centred = value - jnp.mean(value, axis=-1, keepdims=True)
    spread = jnp.mean(centred * centred, axis=-1, keepdims=True)
    return centred * lax.rsqrt(spread + 1e-05) * gain


def gelu_tanh(value):
    return jax.nn.gelu(value, approximate=True)


def product(left, right):
    return jnp.dot(left, right, preferred_element_type=jnp.float32)


def product_left_t(left, right):
    return lax.dot_general(
        left, right, (((0,), (0,)), ((), ())), preferred_element_type=jnp.float32
    )


def product_right_t(left, right):
    return lax.dot_general(
        left, right, (((1,), (1,)), ((), ())), preferred_element_type=jnp.float32
    )


def pack_attention(shards, layer):
    query_w, key_w, value_w, out_w, _, _, gains = (member[layer] for member in shards)
    gain_columns = jnp.pad(gains.T, ((0, 0), (0, PAD - 2)))
    return jnp.concatenate([query_w, key_w, value_w, out_w, gain_columns], axis=1)


def pack_ffn(shards, layer):
    return jnp.concatenate([shards[4][layer], shards[5][layer].T], axis=1)


def plain_gather(block):
    return lax.all_gather(block, ("dp", "fsdp"), axis=0, tiled=True)


def unpack(attention, ffn):
    return (
        attention[:, : 3 * D],
        attention[:, 3 * D : 4 * D],
        ffn[:, :FF],
        ffn[:, FF:],
        attention[:, 4 * D : 4 * D + 2].T.astype(jnp.float32),
    )


def visible_keys(length, token_count, swap):
    half = token_count // 2
    positions = lax.broadcasted_iota(jnp.int32, (2, half), 0) * half + lax.broadcasted_iota(
        jnp.int32, (2, half), 1
    )
    if swap:
        positions = positions[::-1]
    return positions < length


def split_heads(value):
    return value.reshape(2, value.shape[0] // 2, HEADS, HEAD_DIM)


def paired_heads(query, keys, values, swap):
    query_heads = split_heads(query)
    key_heads = split_heads(keys)
    value_heads = split_heads(values)
    if swap:
        key_heads = key_heads[::-1]
        value_heads = value_heads[::-1]
    return (query_heads, key_heads, value_heads)


def masked_scores(query_heads, key_heads, visible):
    scores = (
        jnp.einsum("bqhd,bkhd->bhqk", query_heads, key_heads, preferred_element_type=jnp.float32)
        * 0.125
    )
    return jnp.where(visible[:, None, None, :], scores, -1e30)


def attend_forward(query, keys, values, visible, swap):
    token_count = query.shape[0]
    query_heads, key_heads, value_heads = paired_heads(query, keys, values, swap)
    scores = masked_scores(query_heads, key_heads, visible)
    highest = jnp.max(scores, axis=-1, keepdims=True)
    raised = jnp.exp(scores - highest)
    total = jnp.sum(raised, axis=-1, keepdims=True)
    shares = (raised / total).astype(jnp.bfloat16)
    mixed = jnp.einsum("bhqk,bkhd->bqhd", shares, value_heads, preferred_element_type=jnp.float32)
    return (mixed.reshape(token_count, -1), highest + jnp.log(total))


def attend_backward(query, keys, values, visible, swap, log_total, grad_mixed):
    token_count = query.shape[0]
    query_heads, key_heads, value_heads = paired_heads(query, keys, values, swap)
    scores = masked_scores(query_heads, key_heads, visible)
    shares = jnp.exp(scores - log_total)
    shares_low = shares.astype(jnp.bfloat16)
    grad_heads = split_heads(grad_mixed)
    grad_values = jnp.einsum(
        "bhqk,bqhd->bkhd", shares_low, grad_heads, preferred_element_type=jnp.float32
    )
    grad_shares = jnp.einsum(
        "bqhd,bkhd->bhqk", grad_heads, value_heads, preferred_element_type=jnp.float32
    )
    inner = jnp.sum(shares * grad_shares, axis=-1, keepdims=True)
    grad_scores = (shares * (grad_shares - inner)).astype(jnp.bfloat16)
    grad_query = (
        jnp.einsum("bhqk,bkhd->bqhd", grad_scores, key_heads, preferred_element_type=jnp.float32)
        * 0.125
    )
    grad_keys = (
        jnp.einsum("bhqk,bqhd->bkhd", grad_scores, query_heads, preferred_element_type=jnp.float32)
        * 0.125
    )
    if swap:
        grad_keys = grad_keys[::-1]
        grad_values = grad_values[::-1]
    return tuple(
        (
            member.reshape(token_count, -1).astype(jnp.bfloat16)
            for member in (grad_query, grad_keys, grad_values)
        )
    )


def layer_forward(hidden, length, weights, swap):
    qkv_w, out_w, up_w, down_t, gains = weights
    inputs_low = hidden.astype(jnp.bfloat16)
    qkv = product(inputs_low, qkv_w).astype(jnp.bfloat16)
    query, keys, values = qkv[:, :D], qkv[:, D : 2 * D], qkv[:, 2 * D :]
    visible = visible_keys(length, hidden.shape[0], swap)
    mixed, log_total = attend_forward(query, keys, values, visible, swap)
    mixed_low = mixed.astype(jnp.bfloat16)
    first_sum = hidden + product(mixed_low, out_w)
    normed = norm(first_sum, gains[0])
    normed_low = normed.astype(jnp.bfloat16)
    expanded = product(normed_low, up_w)
    activated = gelu_tanh(expanded).astype(jnp.bfloat16)
    second_sum = normed + product_right_t(activated, down_t)
    output = norm(second_sum, gains[1])
    kept = (
        inputs_low,
        query,
        keys,
        values,
        log_total,
        mixed_low,
        first_sum,
        normed_low,
        expanded,
        activated,
        second_sum,
    )
    return (output, kept)


def down_backward(grad_output, kept, weights):
    grad_second, grad_gain = jax.vjp(norm, kept[10], weights[4][1])[1](grad_output)
    return (grad_second, grad_second.astype(jnp.bfloat16), grad_gain)


def up_backward(grad_second, down_low, kept, weights):
    grad_active = product(down_low, weights[3])
    up_low = jax.vjp(gelu_tanh, kept[8])[1](grad_active)[0].astype(jnp.bfloat16)
    return (grad_second + product_right_t(up_low, weights[2]), up_low)


def mixed_backward(grad_normed, kept, weights):
    grad_first, grad_gain = jax.vjp(norm, kept[6], weights[4][0])[1](grad_normed)
    attn_low = grad_first.astype(jnp.bfloat16)
    grad_mixed = product_right_t(attn_low, weights[1]).astype(jnp.bfloat16)
    return (grad_first, attn_low, grad_mixed, grad_gain)


def scores_backward(grad_mixed, kept, swapped, length):
    query, keys, values, log_total = kept[1:5]
    visible = visible_keys(length, query.shape[0], swapped)
    return jnp.concatenate(
        attend_backward(query, keys, values, visible, swapped, log_total, grad_mixed), axis=1
    )


def inputs_backward(grad_first, grad_qkv, weights):
    return grad_first + product_right_t(grad_qkv, weights[0])


def plain_scatter(terms):
    return lax.psum_scatter(
        terms.astype(jnp.bfloat16), ("dp", "fsdp"), scatter_dimension=0, tiled=True
    ).astype(jnp.float32)


def plain_ffn_terms(operands):
    normed_low, up_low, down_low, activated = operands
    return jnp.concatenate(
        [
            product_left_t(normed_low, up_low).astype(jnp.bfloat16),
            product_left_t(down_low, activated).astype(jnp.bfloat16),
        ],
        axis=1,
    )


def plain_attention_terms(operands, gains):
    inputs_low, grad_qkv, mixed_low, attn_low = operands
    return jnp.concatenate(
        [
            product_left_t(inputs_low, grad_qkv).astype(jnp.bfloat16),
            product_left_t(mixed_low, attn_low).astype(jnp.bfloat16),
            jnp.pad(gains.T, ((0, 0), (0, PAD - 2))).astype(jnp.bfloat16),
        ],
        axis=1,
    )


def attention_outputs(summed):
    return (
        *(summed[:, j * D : (j + 1) * D] for j in range(4)),
        summed[:, 4 * D : 4 * D + 2].T,
    )


def ffn_outputs(summed):
    return (summed[:, :FF], summed[:, FF:].T)


class Grid:
    def __init__(self):
        places = [
            (x, core, z, y) for x in range(2) for core in range(2) for z in range(4) for y in range(2)
        ]
        number = {place: index for index, place in enumerate(places)}

        def route(move, senders=range(4)):
            return [
                (number[place], number[move(*place)]) for place in places if place[2] in senders
            ]

        self.core = route(lambda x, core, z, y: (x, 1 - core, z, y))
        self.first = route(
            lambda x, core, z, y: (x, core, z, 1 - y) if core else (1 - x, core, z, y)
        )
        self.second = route(
            lambda x, core, z, y: (1 - x, core, z, y) if core else (x, core, z, 1 - y)
        )
        self.pair = route(lambda x, core, z, y: (x, core, z ^ 1, y))
        self.middle = route(lambda x, core, z, y: (x, core, 3 - z, y), (1, 2))
        self.outward = route(lambda x, core, z, y: (x, core, z ^ 1, y), (1, 2))
        self.line = [route(lambda x, core, z, y, s=s: (x, core, z ^ s, y)) for s in (1, 2, 3)]


def swap(value, route):
    return lax.ppermute(value, ("dp", "fsdp"), route)


SLOTS = np.array([(far, near, s) for far, near in ((1, 1), (1, 0), (0, 1), (0, 0)) for s in range(4)])
ROWS = tuple((j, j + 2) for j in range(0, 16, 2))
TERM_SLOTS = SLOTS[[0, 1, 4, 5, 2, 3, 10, 11, 6, 7, 8, 9, 12, 13, 14, 15]]
TERM_ROWS = ((0, 4), (4, 8), (8, 10), (10, 12), (12, 16))


def slot_rows(slots, place, x, y, owner):
    first, second = (jnp.asarray(slots[:, j], jnp.int32) for j in range(2))
    along_x = jnp.where(owner == 0, first, second)
    along_y = jnp.where(owner == 0, second, first)
    return (((x ^ along_x) * 2 + owner) * 4 + place) * 2 + (y ^ along_y)


def row_order(unit):
    dp, fsdp = lax.axis_index("dp"), lax.axis_index("fsdp")
    x, core, z, y = dp // 2, dp % 2, fsdp // 2, fsdp % 2
    slots = np.repeat(TERM_SLOTS, unit, axis=0)
    place = z ^ jnp.asarray(slots[:, 2], jnp.int32)
    offset = jnp.asarray(np.tile(np.arange(unit), 16), jnp.int32)
    rows = jnp.concatenate(
        [slot_rows(slots, place, x, y, owner) * unit + offset for owner in (core, 1 - core)]
    )
    natural = lax.broadcasted_iota(jnp.int32, (32 * unit, 32 * unit), 0)
    return (natural == rows[None]).astype(jnp.bfloat16)


def share_left(values, order):
    lengths = [max(value.shape[0], PAD) for value in values]
    half = D // 2

    def body(order_ref, *refs):
        mine, other = refs[len(values) :]
        start = 0
        for length, value_ref in zip(lengths, refs):
            ordered = dot(value_ref[...].astype(jnp.bfloat16), order_ref[...])
            short = length - ordered.shape[0]
            if short:
                ordered = jnp.concatenate([ordered, jnp.zeros((short, D), jnp.float32)], axis=0)
            turned = ordered.T.astype(jnp.bfloat16)
            mine[:, start : start + length] = turned[:half]
            other[:, start : start + length] = turned[half:]
            start += length

    return pl.pallas_call(
        body,
        in_specs=[VMEM_SPEC] * (1 + len(values)),
        out_specs=[VMEM_SPEC] * 2,
        out_shape=shapes(*[((half, sum(lengths)), jnp.bfloat16)] * 2),
        cost_estimate=LIGHT,
        compiler_params=params(8),
    )(order, *values)


def both(value, grid):
    return (value, swap(value, grid.core))


def traded(pair, grid):
    return (pair[0], swap(pair[1], grid.core))


def dot(left, right):
    return jnp.dot(left, right, preferred_element_type=jnp.float32)


def dot_nt(left, right):
    return lax.dot_general(
        left, right, (((1,), (1,)), ((), ())), preferred_element_type=jnp.float32
    )


def dot_tn(left, right):
    return lax.dot_general(
        left, right, (((0,), (0,)), ((), ())), preferred_element_type=jnp.float32
    )


def lane_masks():
    lane = lax.broadcasted_iota(jnp.int32, (1, 2 * HEAD_DIM), 1)
    first = (lane < HEAD_DIM).astype(jnp.float32)
    return first.astype(jnp.bfloat16), (1.0 - first).astype(jnp.bfloat16), lane < HEAD_DIM


def two_heads(value, masks):
    return jnp.concatenate([value * masks[0], value * masks[1]], axis=0)


def pair_softmax(query_pair, keys, key_block, length):
    scores = dot_nt(keys, query_pair) * 0.125
    position = lax.broadcasted_iota(jnp.int32, scores.shape, 0) + key_block * keys.shape[0]
    scores = jnp.where(position < length, scores, -1e30)
    raised = jnp.exp(scores - jnp.max(scores, axis=0, keepdims=True))
    return raised / jnp.sum(raised, axis=0, keepdims=True)


def normalised(value):
    centred = value - jnp.mean(value, axis=-1, keepdims=True)
    rate = lax.rsqrt(jnp.mean(centred * centred, axis=-1, keepdims=True) + 1e-05)
    return centred * rate, rate


def norm_backward(value, gain, grad):
    ratio, rate = normalised(value)
    scaled = grad * gain
    slope = jnp.mean(scaled * ratio, axis=-1, keepdims=True)
    result = rate * (scaled - jnp.mean(scaled, axis=-1, keepdims=True) - ratio * slope)
    return result, jnp.sum(grad * ratio, axis=0, keepdims=True)


def head_parts(half, swapped):
    for block in range(2):
        key_block = 1 - block if swapped else block
        rows = slice(block * half, (block + 1) * half)
        key_rows = slice(key_block * half, (key_block + 1) * half)
        for pair in range(HEADS // 2):
            yield key_block, rows, key_rows, pair * 2 * HEAD_DIM


VMEM_SPEC = pl.BlockSpec(memory_space=pltpu.VMEM)
SMEM_SPEC = pl.BlockSpec(memory_space=pltpu.SMEM)
ANY_SPEC = pl.BlockSpec(memory_space=pl.ANY)


def params(mebibytes):
    return pltpu.CompilerParams(vmem_limit_bytes=mebibytes << 20)


def shapes(*pairs):
    return [jax.ShapeDtypeStruct(shape, dtype) for shape, dtype in pairs]


def attention_columns(weights, start, target, sems):
    copies = []
    for part in range(5):
        width = D if part < 4 else PAD
        copies.append(
            pltpu.make_async_copy(
                weights.at[:, pl.ds(start + part * D, width)],
                target.at[:, pl.ds(part * D, width)],
                sems.at[part],
            )
        )
    for copy in copies:
        copy.start()
    return copies


def attention_forward(hidden, lengths, weights, start, swapped):
    tokens = hidden.shape[0]
    half = tokens // 2
    low = jnp.bfloat16

    def body(length_ref, hidden_ref, w_any, low_out, qkv, mixed, first_sum, gains, w, sems):
        copies = attention_columns(w_any, start, w, sems)
        value = hidden_ref[...].astype(low)
        low_out[...] = value
        masks = lane_masks()
        for part in range(3):
            copies[part].wait()
            columns = slice(part * D, (part + 1) * D)
            qkv[:, columns] = dot(value, w[:, columns]).astype(low)
        for key_block, rows, key_rows, lane in head_parts(half, swapped):
            query = two_heads(qkv[rows, lane : lane + 128], masks)
            keys = qkv[key_rows, D + lane : D + lane + 128]
            values = qkv[key_rows, 2 * D + lane : 2 * D + lane + 128]
            shares = pair_softmax(query, keys, key_block, length_ref[0]).astype(low)
            out = dot_tn(shares, values)
            mixed[rows, lane : lane + 128] = jnp.where(masks[2], out[:half], out[half:]).astype(low)
        copies[3].wait()
        first_sum[...] = hidden_ref[...] + dot(mixed[...], w[:, 3 * D : 4 * D])
        copies[4].wait()
        gains[...] = w[:, 4 * D :].astype(jnp.float32).T[:8]

    return pl.pallas_call(
        body,
        in_specs=[SMEM_SPEC, VMEM_SPEC, ANY_SPEC],
        out_specs=[VMEM_SPEC] * 5,
        out_shape=shapes(
            ((tokens, D), low),
            ((tokens, 3 * D), low),
            ((tokens, D), low),
            ((tokens, D), jnp.float32),
            ((8, D), jnp.float32),
        ),
        scratch_shapes=[pltpu.VMEM((D, 4 * D + PAD), low), pltpu.SemaphoreType.DMA((5,))],
        cost_estimate=LIGHT,
        compiler_params=params(14),
    )(lengths, hidden, weights)


FF_TILE = D


def ffn_forward(first_sum, gains, weights, start):
    tokens = first_sum.shape[0]
    low = jnp.bfloat16
    steps = FF // FF_TILE
    first = start // FF_TILE

    def body(sum_ref, gain_ref, up, down, normed_low, activated, slope, second_sum, out, total):
        step = pl.program_id(0)

        @pl.when(step == 0)
        def _():
            normed = normalised(sum_ref[...])[0] * gain_ref[0:1]
            normed_low[...] = normed.astype(low)
            total[...] = normed

        u = dot(normed_low[...], up[...])
        inner = 0.7978845608028654 * (u + 0.044715 * (u * u * u))
        wave = jnp.tanh(inner)
        active = (0.5 * u * (1.0 + wave)).astype(low)
        slope[...] = (
            0.5 * (1.0 + wave)
            + 0.5 * u * (1.0 - wave * wave) * (0.7978845608028654 * (1.0 + 0.134145 * (u * u)))
        ).astype(low)
        activated[...] = active
        total[...] += dot_nt(active, down[...])

        @pl.when(step == steps - 1)
        def _():
            second_sum[...] = total[...]
            out[...] = normalised(total[...])[0] * gain_ref[1:2]

    def fixed(shape):
        return pl.BlockSpec(shape, lambda j: (0, 0))

    wide = pl.BlockSpec((tokens, FF_TILE), lambda j: (0, j))
    return pl.pallas_call(
        body,
        grid=(steps,),
        in_specs=[
            fixed((tokens, D)),
            fixed((8, D)),
            pl.BlockSpec((D, FF_TILE), lambda j: (0, first + j)),
            pl.BlockSpec((D, FF_TILE), lambda j: (0, first + steps + j)),
        ],
        out_specs=[fixed((tokens, D)), wide, wide, fixed((tokens, D)), fixed((tokens, D))],
        out_shape=shapes(
            ((tokens, D), low),
            ((tokens, FF), low),
            ((tokens, FF), low),
            ((tokens, D), jnp.float32),
            ((tokens, D), jnp.float32),
        ),
        scratch_shapes=[pltpu.VMEM((tokens, D), jnp.float32)],
        cost_estimate=LIGHT,
        compiler_params=params(16),
    )(first_sum, gains, weights, weights)


def second_norm_backward(grad, second_sum, gains):
    tokens = grad.shape[0]

    def body(grad_ref, sum_ref, gain_ref, out, low_out, gain_out):
        result, gain_grad = norm_backward(sum_ref[...], gain_ref[1:2], grad_ref[...].astype(jnp.float32))
        out[...] = result
        low_out[...] = result.astype(jnp.bfloat16)
        gain_out[...] = gain_grad

    return pl.pallas_call(
        body,
        in_specs=[VMEM_SPEC] * 3,
        out_specs=[VMEM_SPEC] * 3,
        out_shape=shapes(
            ((tokens, D), jnp.float32), ((tokens, D), jnp.bfloat16), ((1, D), jnp.float32)
        ),
        cost_estimate=LIGHT,
        compiler_params=params(6),
    )(grad, second_sum, gains)


def up_backward_kernel(grad_second, down_low, slope, weights, start):
    tokens = grad_second.shape[0]
    low = jnp.bfloat16
    steps = FF // FF_TILE
    first = start // FF_TILE

    def body(grad_ref, low_ref, slope_ref, up, down, up_low, out):
        step = pl.program_id(0)

        @pl.when(step == 0)
        def _():
            out[...] = grad_ref[...]

        piece = (dot(low_ref[...], down[...]) * slope_ref[...].astype(jnp.float32)).astype(low)
        up_low[...] = piece
        out[...] += dot_nt(piece, up[...])

    def fixed(shape):
        return pl.BlockSpec(shape, lambda j: (0, 0))

    wide = pl.BlockSpec((tokens, FF_TILE), lambda j: (0, j))
    return pl.pallas_call(
        body,
        grid=(steps,),
        in_specs=[
            fixed((tokens, D)),
            fixed((tokens, D)),
            wide,
            pl.BlockSpec((D, FF_TILE), lambda j: (0, first + j)),
            pl.BlockSpec((D, FF_TILE), lambda j: (0, first + steps + j)),
        ],
        out_specs=[wide, fixed((tokens, D))],
        out_shape=shapes(((tokens, FF), low), ((tokens, D), jnp.float32)),
        cost_estimate=LIGHT,
        compiler_params=params(12),
    )(grad_second, down_low, slope, weights, weights)


def attention_backward_kernel(grad, first_sum, gains, qkv, lengths, weights, start, swapped):
    tokens = grad.shape[0]
    half = tokens // 2
    low = jnp.bfloat16

    def body(length_ref, grad_ref, sum_ref, gain_ref, qkv_ref, w_any, *rest):
        grads, grad_in, gain_out, grad_mixed, w, sems = rest
        copies = attention_columns(w_any, start, w, sems)
        masks = lane_masks()
        result, gain_grad = norm_backward(sum_ref[...], gain_ref[0:1], grad_ref[...])
        grad_in[...] = result
        grads[:, 3 * D :] = result.astype(low)
        gain_out[...] = gain_grad
        copies[3].wait()
        grad_mixed[...] = dot_nt(grads[:, 3 * D :], w[:, 3 * D : 4 * D]).astype(low)
        for key_block, rows, key_rows, lane in head_parts(half, swapped):
            query = two_heads(qkv_ref[rows, lane : lane + 128], masks)
            keys = qkv_ref[key_rows, D + lane : D + lane + 128]
            values = qkv_ref[key_rows, 2 * D + lane : 2 * D + lane + 128]
            arriving = two_heads(grad_mixed[rows, lane : lane + 128], masks)
            shares = pair_softmax(query, keys, key_block, length_ref[0])
            grad_values = dot(shares.astype(low), arriving)
            grad_shares = dot_nt(values, arriving)
            inner = jnp.sum(shares * grad_shares, axis=0, keepdims=True)
            grad_scores = (shares * (grad_shares - inner)).astype(low)
            grad_query = dot_tn(grad_scores, keys) * 0.125
            grad_keys = dot(grad_scores, query) * 0.125
            grads[rows, lane : lane + 128] = jnp.where(
                masks[2], grad_query[:half], grad_query[half:]
            ).astype(low)
            grads[key_rows, D + lane : D + lane + 128] = grad_keys.astype(low)
            grads[key_rows, 2 * D + lane : 2 * D + lane + 128] = grad_values.astype(low)
        for part in (0, 1, 2):
            copies[part].wait()
            columns = slice(part * D, (part + 1) * D)
            grad_in[...] += dot_nt(grads[:, columns], w[:, columns])
        copies[4].wait()

    return pl.pallas_call(
        body,
        in_specs=[SMEM_SPEC] + [VMEM_SPEC] * 4 + [ANY_SPEC],
        out_specs=[VMEM_SPEC] * 3,
        out_shape=shapes(
            ((tokens, 4 * D), low),
            ((tokens, D), jnp.float32),
            ((1, D), jnp.float32),
        ),
        scratch_shapes=[
            pltpu.VMEM((tokens, D), low),
            pltpu.VMEM((D, 4 * D + PAD), low),
            pltpu.SemaphoreType.DMA((5,)),
        ],
        cost_estimate=LIGHT,
        compiler_params=params(16),
    )(lengths, grad, first_sum, gains, qkv, weights)


def matrix_terms(products, unit):
    tile = D
    tokens, width = products[0][2][0].shape
    steps = width // tile

    def body(*refs):
        outs = refs[starts[-1] :]
        for j in range(len(products)):
            la, lb, ra, *received = refs[starts[j] : starts[j + 1]]
            for step in range(steps if len(received) > 1 else 1):
                rb = received[step]
                place = pl.program_id(0) - j * steps
                here = place == step if len(received) > 1 else place // steps == 0

                @pl.when(here)
                def _(la=la, lb=lb, ra=ra, rb=rb):
                    value = (dot(la[...], ra[...]) + dot(lb[...], rb[...])).astype(jnp.bfloat16)
                    for (low, high), out in zip(TERM_ROWS, outs):
                        out[...] = value[low * unit : high * unit]

    in_specs, operands, starts = [], [], [0]
    for j, (left, part, right) in enumerate(products):
        block = pl.BlockSpec((16 * unit, tokens), lambda i, part=part: (0, part))
        column = pl.BlockSpec(
            (tokens, tile), lambda i, j=j: (0, jnp.clip(i - j * steps, 0, steps - 1))
        )
        own, received = right
        if isinstance(received, list):
            whole = pl.BlockSpec((tokens, tile), lambda i: (0, 0))
            in_specs += [block, block, column] + [whole] * steps
            operands += [*left, own, *received]
        else:
            in_specs += [block, block, column, column]
            operands += [*left, own, received]
        starts.append(len(operands))
    wide = width * len(products)
    return pl.pallas_call(
        body,
        grid=(wide // tile,),
        in_specs=in_specs,
        out_specs=[pl.BlockSpec(((b - a) * unit, tile), lambda i: (0, i)) for a, b in TERM_ROWS],
        out_shape=shapes(*((((b - a) * unit, wide), jnp.bfloat16) for a, b in TERM_ROWS)),
        cost_estimate=LIGHT,
        compiler_params=params(10),
    )(*operands)


def attention_terms(left, grads, gains, start, unit):
    tokens = grads[0].shape[0]

    def body(la, lb, ra, rb, ga, gb, *outs):
        def put(value, column):
            value = value.astype(jnp.bfloat16)
            for (low, high), out in zip(TERM_ROWS, outs):
                out[:, column : column + value.shape[1]] = value[low * unit : high * unit]

        for j in range(4):
            part = slice(j * D, (j + 1) * D)
            from_left = slice(0, tokens) if j < 3 else slice(tokens, 2 * tokens)
            put(
                dot(la[:, from_left], ra[:, part]) + dot(lb[:, from_left], rb[:, part]),
                j * D,
            )
        gain = slice(start, start + PAD)
        put(ga[:, gain].astype(jnp.float32) + gb[:, gain].astype(jnp.float32), 4 * D)

    return pl.pallas_call(
        body,
        in_specs=[VMEM_SPEC] * 6,
        out_specs=[VMEM_SPEC] * 5,
        out_shape=shapes(*((((b - a) * unit, 4 * D + PAD), jnp.bfloat16) for a, b in TERM_ROWS)),
        cost_estimate=LIGHT,
        compiler_params=params(12),
    )(*left, *grads, *gains)


def square_sums(came_first, came_second, later_first, later_second):
    rows, width = later_first.shape

    def body(one, other, first, second, first_out, second_out):
        first_out[...] = add(first[...], other[:rows]).astype(jnp.bfloat16)
        second_out[...] = add(second[...], one[:rows]).astype(jnp.bfloat16)

    return pl.pallas_call(
        body,
        in_specs=[VMEM_SPEC] * 4,
        out_specs=[VMEM_SPEC] * 2,
        out_shape=shapes(*[((rows, width), jnp.bfloat16)] * 2),
        cost_estimate=LIGHT,
        compiler_params=params(8),
    )(came_first, came_second, later_first, later_second)


def line_sums(groups, unit):
    two = 2 * unit
    widths = [group[0].shape[1] for group in groups]

    def body(*refs):
        outs = refs[5 * len(groups) :]
        start = 0
        for j, width in enumerate(widths):
            own, one, other, last_first, last_second = refs[5 * j : 5 * j + 5]
            columns = slice(start, start + width)
            near = add(own[:two], one[two:], last_second[...])
            far = add(own[two:], other[two:], last_first[...])
            outs[0][:, columns] = near[:unit]
            outs[1][:, columns] = near[unit:].astype(jnp.bfloat16)
            outs[2][:, columns] = far[:unit].astype(jnp.bfloat16)
            outs[3][:, columns] = far[unit:].astype(jnp.bfloat16)
            start += width

    low = ((unit, sum(widths)), jnp.bfloat16)
    return pl.pallas_call(
        body,
        in_specs=[VMEM_SPEC] * (5 * len(groups)),
        out_specs=[VMEM_SPEC] * 4,
        out_shape=shapes(((unit, sum(widths)), jnp.float32), low, low, low),
        cost_estimate=LIGHT,
        compiler_params=params(14),
    )(*(value for group in groups for value in group))


def stack_attention(layers):
    rows, width = layers[0][0].shape
    starts = [0]
    for layer in layers:
        starts.append(starts[-1] + len(layer))

    def body(*refs):
        outs = refs[starts[-1] :]
        for layer in range(len(layers)):
            total = add(*(ref[...] for ref in refs[starts[layer] : starts[layer + 1]]))
            for j, out in enumerate(outs):
                out[layer] = total[:, j * D : min((j + 1) * D, width)]

    return pl.pallas_call(
        body,
        in_specs=[VMEM_SPEC] * starts[-1],
        out_specs=[VMEM_SPEC] * 5,
        out_shape=shapes(
            *[((len(layers), rows, D), jnp.float32)] * 4,
            ((len(layers), rows, PAD), jnp.float32),
        ),
        cost_estimate=LIGHT,
        compiler_params=params(8),
    )(*(value for layer in layers for value in layer))


def add(*values):
    return sum(value.astype(jnp.float32) for value in values)


class Reduction:
    def __init__(self, pieces, grid, unit):
        self.grid, self.unit, self.round, self.joined = grid, unit, 0, False
        self.out, self.kept = list(pieces[:2]), list(pieces[2:])

    def state(self, pending):
        return ([] if pending else self.out, self.kept)

    def restore(self, state):
        out, self.kept = state
        self.out = out or self.out

    def send(self):
        grid = self.grid
        routes = grid.line if self.round == 2 else (grid.first, grid.second)
        self.out = [swap(value, route) for value, route in zip(self.out, routes)]
        self.round += 1

    def prepare(self):
        if self.round == 1:
            later_first, later_second, own = self.kept
            self.kept = [own, *self.out]
            self.out = list(square_sums(*self.out, later_first, later_second))
        elif not self.joined:
            self.join()

    def join(self, *others):
        groups = [(*reduction.kept, *reduction.out) for reduction in (self, *others)]
        own, *self.out = line_sums(groups, self.unit)
        self.kept, self.joined = [own], True

    def result(self):
        return add(self.kept[0], *self.out)


def gate(values, *earlier):
    return lax.optimization_barrier((values, earlier))[0]


class Segments:
    def __init__(self):
        self.active = []

    def join(self, reduction, *others):
        reduction.join(*others)
        self.active = [r for r in self.active if r not in others]

    def run(self, sends, compute=None, values=(), pending=()):
        for reduction in sends:
            if reduction not in self.active:
                self.active.append(reduction)
            if reduction.round:
                reduction.prepare()
            reduction.send()
        if compute:
            values = compute(*values)
        states = [reduction.state(reduction in pending) for reduction in self.active]
        states, values = lax.optimization_barrier((states, values))
        for reduction, state in zip(self.active, states):
            reduction.restore(state)
        self.active = [r for r in self.active if r.round < 3 or r in pending]
        return values


class Gathering:
    def __init__(self, block, grid):
        self.pieces, self.grid, self.unit = [block], grid, block.shape[0]
        self.steps = [self.pair, self.middle, self.outward, self.square, self.diagonal]

    def advance(self):
        self.pieces = list(self.steps.pop(0)(self.pieces, self.grid, 2 * self.unit))

    @staticmethod
    def pair(pieces, grid, two):
        (block,) = pieces
        return (jnp.concatenate([block, swap(block, grid.pair)], axis=0),)

    @staticmethod
    def middle(pieces, grid, two):
        (near,) = pieces
        return (near, swap(near, grid.middle))

    @staticmethod
    def outward(pieces, grid, two):
        near, far = pieces
        z = lax.axis_index("fsdp") // 2
        return (near, jnp.where((z == 1) | (z == 2), far, swap(far, grid.outward)))

    @staticmethod
    def square(pieces, grid, two):
        near, far = pieces
        return (
            swap(far, grid.first),
            swap(near, grid.second),
            swap(near, grid.first),
            swap(far, grid.second),
            near,
            far,
        )

    @staticmethod
    def diagonal(pieces, grid, two):
        first_far, second_near, first_near, second_far, near, far = pieces
        return (
            swap(second_near, grid.first),
            swap(first_far, grid.second),
            first_near,
            first_far,
            second_near,
            second_far,
            near,
            far,
        )

    def result(self):
        pieces = self.pieces
        return place_blocks(pieces + [swap(piece, self.grid.core) for piece in pieces], self.unit)


def place_blocks(pieces, unit):
    width = pieces[0].shape[1]
    dp, fsdp = lax.axis_index("dp"), lax.axis_index("fsdp")
    x, core, z, y = dp // 2, dp % 2, fsdp // 2, fsdp % 2
    s = jnp.asarray(SLOTS[:, 2], jnp.int32)
    place = jnp.where(s < 2, z ^ s, jnp.where(z < 2, s, 3 - s))
    rows = jnp.concatenate([slot_rows(SLOTS, place, x, y, owner) for owner in (core, 1 - core)])
    tiles = unit // 8

    def body(rows_ref, *refs):
        sources, target = refs[:16], refs[16]
        for half in range(2):
            for (low, high), source in zip(ROWS, sources[half * 8 : half * 8 + 8]):
                for slot in range(low, high):
                    row = rows_ref[half * 16 + slot] * tiles
                    first = (slot - low) * tiles
                    target[pl.ds(row, tiles)] = source[first : first + tiles]

    placed = pl.pallas_call(
        body,
        in_specs=[pl.BlockSpec(memory_space=pltpu.SMEM)]
        + [pl.BlockSpec(memory_space=pltpu.VMEM)] * 16,
        out_specs=pl.BlockSpec(memory_space=pltpu.VMEM),
        out_shape=jax.ShapeDtypeStruct((32 * tiles, 8, width), jnp.bfloat16),
        cost_estimate=LIGHT,
        compiler_params=params(22),
    )(rows, *(piece.reshape(-1, 8, width) for piece in pieces))
    return placed.reshape(32 * unit, width)


def per_device(
    sizes,
    tokens,
    lengths,
    query_weight,
    key_weight,
    value_weight,
    attn_out_weight,
    up_weight,
    down_weight,
    norm_gains,
    cotangent,
):
    shards = (
        query_weight,
        key_weight,
        value_weight,
        attn_out_weight,
        up_weight,
        down_weight,
        norm_gains,
    )
    if sizes == (4, 8):
        return grid_step(tokens, lengths, shards, cotangent)
    hidden = tokens[0].astype(jnp.float32)
    length = lengths[0]
    weights_all = [
        unpack(plain_gather(pack_attention(shards, j)), plain_gather(pack_ffn(shards, j)))
        for j in range(LAYERS)
    ]
    kept_all = []
    for layer in range(LAYERS):
        hidden, kept = layer_forward(hidden, length, weights_all[layer], layer % 2 == 1)
        kept_all.append(kept)
    grad = cotangent[0].astype(jnp.float32)
    outputs = [None] * LAYERS
    for layer in reversed(range(LAYERS)):
        kept, weights = kept_all[layer], weights_all[layer]
        grad_second, down_low, gain_second = down_backward(grad, kept, weights)
        grad_normed, up_low = up_backward(grad_second, down_low, kept, weights)
        ffn = plain_scatter(plain_ffn_terms((kept[7], up_low, down_low, kept[9])))
        grad_first, attn_low, grad_mixed, gain_first = mixed_backward(grad_normed, kept, weights)
        grad_qkv = scores_backward(grad_mixed, kept, layer % 2 == 1, length)
        grad = inputs_backward(grad_first, grad_qkv, weights)
        gains = jnp.stack([gain_first, gain_second])
        attention = plain_scatter(
            plain_attention_terms((kept[0], grad_qkv, kept[5], attn_low), gains)
        )
        outputs[layer] = (attention_outputs(attention), ffn_outputs(ffn))
    return finish(hidden, grad, outputs)


def finish(hidden, grad, outputs):
    layers = [(*attention[:4], *ffn, attention[4]) for attention, ffn in outputs]
    stacked = tuple((jnp.stack([entry[member] for entry in layers]) for member in range(7)))
    return (hidden.astype(jnp.bfloat16)[None], grad[None], *stacked)


def gather_first_layer(blocks, second, order, grid, attend):
    attention, ffn = (Gathering(block, grid) for block in blocks)

    def hold(*gatherings):
        pieces = [g.pieces[:2] if len(g.pieces) == 6 else g.pieces for g in gatherings]
        pieces = lax.optimization_barrier(pieces)
        for g, held in zip(gatherings, pieces):
            g.pieces = [*held, *g.pieces[len(held) :]]

    attention.advance()
    hold(attention)
    ffn.pieces = gate(ffn.pieces, attention.pieces)
    attention.advance()
    ffn.advance()
    hold(attention, ffn)
    attention.advance()
    ffn.advance()
    order, ffn.pieces = lax.optimization_barrier((order, ffn.pieces))
    hold(attention, ffn)
    attention.advance()
    ffn.advance()
    hold(attention, ffn)
    attention.advance()
    ffn.pieces = gate(ffn.pieces, attention.pieces[2])
    ffn.advance()
    hold(attention)
    weights = attention.result()
    attended = attend(weights)
    held, attended = lax.optimization_barrier((ffn.pieces[:2], attended))
    ffn.pieces = [*held, *ffn.pieces[2:]]
    ffn.advance()
    held, second = lax.optimization_barrier((ffn.pieces[6:7], second))
    ffn.pieces = [*ffn.pieces[:6], *held, ffn.pieces[7]]
    return weights, ffn.result(), second, order, attended


def grid_step(tokens, lengths, shards, cotangent):
    grid, unit = Grid(), shards[0].shape[1]
    order = row_order(unit)
    hidden = tokens[0].astype(jnp.float32)

    second = plain_gather(
        jnp.concatenate([pack_ffn(shards, 1), pack_attention(shards, 1)], axis=1)
    )

    def attend(weights):
        return attention_forward(hidden, lengths, weights, 0, False)

    attention, ffn, second, order, attended = gather_first_layer(
        (pack_attention(shards, 0), pack_ffn(shards, 0)), second, order, grid, attend
    )
    attention_at = ((attention, 0, False), (second, 2 * FF, True))
    ffn_at = ((ffn, 0), (second, 0))

    kept, left, right = [], [], []
    for layer in range(LAYERS):
        if layer:
            attended = attention_forward(hidden, lengths, *attention_at[layer])
        inputs_low, qkv, mixed, first_sum, gains = attended
        normed_low, activated, slope, second_sum, hidden = ffn_forward(
            first_sum, gains, *ffn_at[layer]
        )
        kept.append((qkv, first_sum, gains, slope, second_sum))
        left.append(traded(share_left((inputs_low, mixed, normed_low), order), grid))
        right.append(both(activated, grid))

    def norm_part(layer, grad):
        return second_norm_backward(grad, kept[layer][4], kept[layer][2])

    def up_part(layer, grad_second, down_low):
        up_low, grad = up_backward_kernel(grad_second, down_low, kept[layer][3], *ffn_at[layer])
        return grad, up_low

    def attention_part(layer, grad):
        qkv, first_sum, gains = kept[layer][:3]
        return attention_backward_kernel(
            grad, first_sum, gains, qkv, lengths, *attention_at[layer]
        )

    def gain_rows(first, second):
        return jnp.concatenate([first, second, jnp.zeros((6, D), jnp.float32)], axis=0)

    def up_product(layer, up_low):
        return left[layer], 2, both(up_low, grid)

    def up_product_in_tiles(layer, up_low):
        received = [swap(up_low[:, j : j + D], grid.core) for j in range(0, FF, D)]
        return left[layer], 2, (up_low, received)

    segments = Segments()
    grad_second, down_low, gain_second = norm_part(1, cotangent[0])
    down_t = traded(share_left((down_low,), order), grid)
    pieces = matrix_terms([(down_t, 0, right[1])], unit)
    grad_second, down_low, pieces = lax.optimization_barrier((grad_second, down_low, pieces))
    down_1 = Reduction(pieces, grid, unit)

    def work(grad_second, down_low):
        grad, up_low = up_part(1, grad_second, down_low)
        pieces = matrix_terms([up_product_in_tiles(1, up_low)], unit)
        return attention_part(1, grad), pieces

    (grads, grad, gain_first), pieces = segments.run([down_1], work, (grad_second, down_low))
    up_1 = Reduction(pieces, grid, unit)
    gains_1 = gain_rows(gain_first, gain_second)

    def work(grad, grads, gains):
        grads = both(grads, grid)
        grad_second, down_low, gain_second = norm_part(0, grad)
        shared = traded(share_left((down_low, gains), order), grid)
        grad, up_low = up_part(0, grad_second, down_low)
        pieces = attention_terms(left[1], grads, shared, grads[0].shape[0], unit)
        return grad, up_low, gain_second, shared, pieces

    grad, up_low, gain_second, shared, pieces = segments.run(
        [up_1, down_1], work, (grad, grads, gains_1)
    )
    attention_1 = Reduction(pieces, grid, unit)

    def work(grad, up_low, shared):
        pieces = matrix_terms([(shared, 0, right[0]), up_product(0, up_low)], unit)
        return attention_part(0, grad), pieces

    (grads, grad, gain_first), pieces = segments.run(
        [attention_1, up_1], work, (grad, up_low, shared)
    )
    ffn_0 = Reduction(pieces, grid, unit)

    def work(grads, gain_first):
        gains = traded(share_left((gain_rows(gain_first, gain_second),), order), grid)
        return attention_terms(left[0], both(grads, grid), gains, 0, unit)

    segments.join(down_1, up_1)
    pieces = segments.run([ffn_0, attention_1, down_1], work, (grads, gain_first))
    attention_0 = Reduction(pieces, grid, unit)
    segments.run([ffn_0, attention_0, attention_1], pending=[attention_0])
    segments.run([attention_0, ffn_0])
    segments.run([attention_0])

    summed = [reduction.result() for reduction in (ffn_0, down_1)]
    done = attention_1.result()
    *attention, gains = stack_attention([(*attention_0.kept, *attention_0.out), (done,)])
    return (
        hidden.astype(jnp.bfloat16)[None],
        grad[None],
        *attention,
        jnp.stack([value[:, FF:] for value in summed]),
        jnp.stack([value[:, :FF].T for value in summed]),
        jnp.swapaxes(gains[:, :, :2], 1, 2),
    )


def solution(mesh):
    placed = (
        P(("dp", "fsdp"), None, None),
        P(("dp", "fsdp")),
        P(None, ("dp", "fsdp"), None),
        P(None, ("dp", "fsdp"), None),
        P(None, ("dp", "fsdp"), None),
        P(None, ("dp", "fsdp"), None),
        P(None, ("dp", "fsdp"), None),
        P(None, None, ("dp", "fsdp")),
        P(None, None, ("dp", "fsdp")),
        P(("dp", "fsdp"), None, None),
    )
    return jax.shard_map(
        functools.partial(per_device, (mesh.shape["dp"], mesh.shape["fsdp"])),
        mesh=mesh,
        in_specs=placed,
        out_specs=(
            P(("dp", "fsdp"), None, None),
            P(("dp", "fsdp"), None, None),
            P(None, ("dp", "fsdp"), None),
            P(None, ("dp", "fsdp"), None),
            P(None, ("dp", "fsdp"), None),
            P(None, ("dp", "fsdp"), None),
            P(None, ("dp", "fsdp"), None),
            P(None, None, ("dp", "fsdp")),
            P(None, None, ("dp", "fsdp")),
        ),
        check_vma=False,
    )
```
